32 devices in a mesh: dp: 8 (over y, x, core), seq: 4 (over z).
Axes of the slice: x: 2, y: 2, z: 4, core: 2. Of those that a mesh axis runs over, the one named last changes fastest.
Arguments:
- inputs: bfloat16 [8, 1024, 1024], P('dp', 'seq'), may hold values from -6 to 6
- lengths: int32 [8], P('dp'), may hold values from 640 to 1024, as said below
- token_mask: int32 [8, 1024], P('dp', 'seq'), may hold values from 0 to 1, as said below
- mask_vector: bfloat16 [1024], P(('dp', 'seq')), may hold values from -6 to 6
- gain_first: bfloat16 [1024], P(('dp', 'seq')), may hold values from 0.25 to 1.75
- first_up: bfloat16 [1024, 4096], P(('dp', 'seq')), may hold values from -0.1875 to 0.1875
- first_down: bfloat16 [4096, 1024], P(('dp', 'seq')), may hold values from -0.1875 to 0.1875
- gain_attend: bfloat16 [1024], P(('dp', 'seq')), may hold values from 0.25 to 1.75
- joint_proj: bfloat16 [1024, 3072], P(('dp', 'seq')), may hold values from -0.25 to 0.25
- attend_out: bfloat16 [1024, 1024], P(('dp', 'seq')), may hold values from -4 to 4
- gain_conv: bfloat16 [1024], P(('dp', 'seq')), may hold values from 0.25 to 1.75
- conv_pair: bfloat16 [1024, 2048], P(('dp', 'seq')), may hold values from -0.1875 to 0.1875
- conv_taps: bfloat16 [1024, 31], P(('dp', 'seq')), may hold values from -1 to 1
- batch_scale: bfloat16 [1024], P(('dp', 'seq')), may hold values from 0.25 to 1.75
- batch_shift: bfloat16 [1024], P(('dp', 'seq')), may hold values from -3 to 3
- conv_out: bfloat16 [1024, 1024], P(('dp', 'seq')), may hold values from -0.25 to 0.25
- gain_second: bfloat16 [1024], P(('dp', 'seq')), may hold values from 0.25 to 1.75
- second_up: bfloat16 [1024, 4096], P(('dp', 'seq')), may hold values from -0.1875 to 0.1875
- second_down: bfloat16 [4096, 1024], P(('dp', 'seq')), may hold values from -0.1875 to 0.1875
- gain_final: bfloat16 [1024], P(('dp', 'seq')), may hold values from 0.25 to 1.75
- cotangent: bfloat16 [8, 1024, 1024], P('dp', 'seq'), may hold values from -6 to 6
Outputs:
- output: bfloat16 [8, 1024, 1024], P('dp', 'seq')
- input_grad: float32 [8, 1024, 1024], P('dp', 'seq')
- mask_vector_grad: float32 [1024], P(('dp', 'seq'))
- gain_first_grad: float32 [1024], P(('dp', 'seq'))
- first_up_grad: float32 [1024, 4096], P(('dp', 'seq'))
- first_down_grad: float32 [4096, 1024], P(('dp', 'seq'))
- gain_attend_grad: float32 [1024], P(('dp', 'seq'))
- joint_proj_grad: float32 [1024, 3072], P(('dp', 'seq'))
- attend_out_grad: float32 [1024, 1024], P(('dp', 'seq'))
- gain_conv_grad: float32 [1024], P(('dp', 'seq'))
- conv_pair_grad: float32 [1024, 2048], P(('dp', 'seq'))
- conv_taps_grad: float32 [1024, 31], P(('dp', 'seq'))
- batch_scale_grad: float32 [1024], P(('dp', 'seq'))
- batch_shift_grad: float32 [1024], P(('dp', 'seq'))
- conv_out_grad: float32 [1024, 1024], P(('dp', 'seq'))
- gain_second_grad: float32 [1024], P(('dp', 'seq'))
- second_up_grad: float32 [1024, 4096], P(('dp', 'seq'))
- second_down_grad: float32 [4096, 1024], P(('dp', 'seq'))
- gain_final_grad: float32 [1024], P(('dp', 'seq'))
- moment_mean: float32 [1024], replicated
- moment_var: float32 [1024], replicated
The draws below stay inside these ranges and needn't reach their ends.
Inputs may be any that keep to these rules, and one draw needn't show every extreme that they name: `lengths`: valid frames of each item, which come first; one item has exactly 1024 and one exactly 640. `token_mask`: 1 marks a frame whose input is replaced by the mask vector.
All inputs are finite; a program needn't handle non-finite values.
Results may differ from the reference program's by a relative error of at most 0.025.
Values may be sent and summed in bfloat16 or wider, within the bound.
No kernel may reach another device: no remote copies, remote signals or barrier semaphores. Data moves between devices by JAX's collectives and lax.ppermute only.
A program may use at most 384 MiB of HBM per device.

```python
import math
import jax
import jax.numpy as jnp
from jax import lax

D = 1024
FF = 4096
HEADS = 16
HEAD_DIM = 64
KERNEL = 31
LENGTH = 1024
ITEMS = 8


def draw_lengths(key, part):
    shortest = LENGTH * 5 // 8
    first_key, second_key = jax.random.split(key)
    lengths_drawn = jax.random.randint(first_key, (ITEMS,), shortest, LENGTH + 1, dtype=jnp.int32)
    shuffled = jax.random.permutation(second_key, ITEMS)
    lengths_drawn = lengths_drawn.at[shuffled[0]].set(LENGTH)
    lengths_drawn = lengths_drawn.at[shuffled[1]].set(shortest)
    return lengths_drawn


def draw_token_mask(key, part):
    rate_key, cell_key = jax.random.split(key)
    levels = jax.random.randint(rate_key, (ITEMS, 1), 0, 1000, dtype=jnp.int32)
    mask_rates = levels * levels // 1000
    cell_draws = jax.random.randint(cell_key, (ITEMS, LENGTH), 0, 1000, dtype=jnp.int32)
    return (cell_draws < mask_rates).astype(jnp.int32)


def steps_of(stream_key, extent, shards, least, largest):
    level, own = 1.0, jax.random.fold_in(stream_key, 6)
    for position, shards_of in shards:
        steps = jnp.exp(jax.random.uniform(jax.random.fold_in(own, position), (shards_of,), jnp.float32, least / len(shards), largest / len(shards)))
        level = level * jnp.repeat(steps, extent[position] // shards_of).reshape([-1 if axis == position else 1 for axis in range(len(extent))])
    return level


def normal_values(rng, shape, scale, reach, pieces=(), kind=jnp.bfloat16):
    drawn = scale * jax.random.normal(rng, shape, jnp.float32)
    if pieces:
        drawn = drawn * steps_of(rng, shape, pieces, -0.22, 0.18)
    return jnp.clip(drawn, -reach, reach).astype(kind)


def setup_inputs(seed: int = 0) -> dict:
    arg_keys = jax.random.split(jax.random.key(seed), 22)
    inputs = normal_values(arg_keys[0], (ITEMS, LENGTH, D), 1.0, 6.0, ((0, 8), (1, 4)))
    lengths = draw_lengths(jax.random.fold_in(arg_keys[21], 71), 0)
    token_mask = draw_token_mask(jax.random.fold_in(arg_keys[21], 71), 0)
    mask_vector = normal_values(arg_keys[3], (D,), 1.0, 6.0, ((0, 32),))
    gain_first = jnp.clip(1.0 + 0.15 * jax.random.normal(arg_keys[4], (D,), jnp.float32), 0.25, 1.75).astype(jnp.bfloat16)
    first_up = normal_values(arg_keys[5], (D, FF), D ** -0.5, 0.1875, ((0, 32),))
    first_down = normal_values(arg_keys[6], (FF, D), (FF // 4) ** -0.5, 0.1875, ((0, 32),))
    gain_attend = jnp.clip(1.0 + 0.15 * jax.random.normal(arg_keys[7], (D,), jnp.float32), 0.25, 1.75).astype(jnp.bfloat16)
    joint_proj = normal_values(arg_keys[8], (D, 3 * D), (D // 2) ** -0.5, 0.25, ((0, 32),))
    attend_out = normal_values(arg_keys[9], (D, D), (max(1, 2 * D // LENGTH)) ** -0.5, 4.0, ((0, 32),))
    gain_conv = jnp.clip(1.0 + 0.15 * jax.random.normal(arg_keys[10], (D,), jnp.float32), 0.25, 1.75).astype(jnp.bfloat16)
    conv_pair = normal_values(arg_keys[11], (D, 2 * D), D ** -0.5, 0.1875, ((0, 32),))
    conv_taps = normal_values(arg_keys[12], (D, KERNEL), KERNEL ** -0.5, 1.0, ((0, 32),))
    batch_scale = jnp.clip(1.0 + 0.15 * jax.random.normal(arg_keys[13], (D,), jnp.float32), 0.25, 1.75).astype(jnp.bfloat16)
    batch_shift = normal_values(arg_keys[14], (D,), 0.5, 3.0, ((0, 32),))
    conv_out = normal_values(arg_keys[15], (D, D), (D // 2) ** -0.5, 0.25, ((0, 32),))
    gain_second = jnp.clip(1.0 + 0.15 * jax.random.normal(arg_keys[16], (D,), jnp.float32), 0.25, 1.75).astype(jnp.bfloat16)
    second_up = normal_values(arg_keys[17], (D, FF), D ** -0.5, 0.1875, ((0, 32),))
    second_down = normal_values(arg_keys[18], (FF, D), (FF // 4) ** -0.5, 0.1875, ((0, 32),))
    gain_final = jnp.clip(1.0 + 0.15 * jax.random.normal(arg_keys[19], (D,), jnp.float32), 0.25, 1.75).astype(jnp.bfloat16)
    cotangent = normal_values(arg_keys[20], (ITEMS, LENGTH, D), 1.0, 6.0, ((0, 8), (1, 4)))
    return dict(inputs=inputs, lengths=lengths, token_mask=token_mask, mask_vector=mask_vector, gain_first=gain_first, first_up=first_up, first_down=first_down, gain_attend=gain_attend, joint_proj=joint_proj, attend_out=attend_out, gain_conv=gain_conv, conv_pair=conv_pair, conv_taps=conv_taps, batch_scale=batch_scale, batch_shift=batch_shift, conv_out=conv_out, gain_second=gain_second, second_up=second_up, second_down=second_down, gain_final=gain_final, cotangent=cotangent)


@jax.custom_vjp
def low(v):
    return lax.optimization_barrier(v.astype(jnp.bfloat16)).astype(jnp.float32)

@jax.custom_vjp
def low_back(v):
    return v

def low_keep(v):
    return (low(v), None)

def low_pass(kept, grad):
    return (grad,)

def back_keep(v):
    return (v, None)

def back_low(kept, grad):
    return (low(grad),)
low.defvjp(low_keep, low_pass)
low_back.defvjp(back_keep, back_low)
epsilon = 1e-05
exact_mode = lax.Precision.HIGHEST

def product(left_side, right_side):
    return jnp.dot(left_side, right_side, precision=exact_mode, preferred_element_type=jnp.float32)

def layer_norm(values, norm_gain):
    centered = values - lax.optimization_barrier(jnp.mean(values, axis=-1, keepdims=True))
    variance = lax.optimization_barrier(jnp.mean(centered * centered, axis=-1, keepdims=True))
    return centered * lax.rsqrt(variance + epsilon) * norm_gain

def feed_forward(values, norm_gain, upward, downward):
    normed = low(layer_norm(values, norm_gain))
    hidden = low_back(product(normed, upward))
    active = low(jax.nn.silu(hidden))
    return values + 0.5 * low_back(product(active, downward))

def attend(values, length, norm_gain, joint_matrix, outward):
    frames = values.shape[0]
    normed = low(layer_norm(values, norm_gain))
    joined = low(low_back(product(normed, joint_matrix)))
    query_rows = joined[:, :D].reshape(frames, HEADS, HEAD_DIM)
    key_rows = joined[:, D:2 * D].reshape(frames, HEADS, HEAD_DIM)
    value_rows = joined[:, 2 * D:].reshape(frames, HEADS, HEAD_DIM)
    score_scale = 1.0 / math.sqrt(HEAD_DIM)
    scores = low_back(jnp.einsum('qhd,khd->hqk', query_rows, key_rows, precision=exact_mode) * score_scale)
    key_valid = jnp.arange(frames) < length
    scores = jnp.where(key_valid[None, None, :], scores, -1e+30)
    weights = jax.nn.softmax(scores, axis=-1)
    mixture = jnp.einsum('hqk,khd->qhd', low(weights), value_rows, precision=exact_mode).reshape(frames, D)
    mixture = low(low_back(mixture))
    return values + low_back(product(mixture, outward))

def convolve_front(values, valid_item, norm_gain, pairing, conv_taps):
    frames = values.shape[0]
    normed = low(layer_norm(values, norm_gain))
    paired = low_back(product(normed, pairing))
    gated_rows = low(paired[:, :D] * jax.nn.sigmoid(paired[:, D:]) * valid_item[:, None])
    half_width = KERNEL // 2
    widened = jnp.pad(gated_rows, ((half_width, half_width), (0, 0)))
    mixture = jnp.zeros_like(gated_rows)
    for offset in range(KERNEL):
        mixture = mixture + widened[offset:offset + frames] * conv_taps[:, offset]
    return low_back(mixture)

def forward(inputs, mask_vector, gain_first, first_up, first_down, gain_attend, joint_proj, attend_out, gain_conv, conv_pair, conv_taps, batch_scale, batch_shift, conv_out, gain_second, second_up, second_down, gain_final, lengths, token_mask):
    masked = token_mask[:, :, None] > 0
    start_rows = jnp.where(masked, mask_vector, inputs)
    positions = jnp.arange(LENGTH)
    valid_rows = (positions[None, :] < lengths[:, None]).astype(jnp.float32)

    def front_item(carried):
        values, length, valid_item = carried
        values = feed_forward(values, gain_first, first_up, first_down)
        values = attend(values, length, gain_attend, joint_proj, attend_out)
        return (values, convolve_front(values, valid_item, gain_conv, conv_pair, conv_taps))
    residual, conv_mixed = lax.map(jax.checkpoint(front_item), (start_rows, lengths, valid_rows))
    frame_count = jnp.sum(valid_rows)
    batch_mean = lax.optimization_barrier(jnp.sum(conv_mixed * valid_rows[:, :, None], axis=(0, 1))) / frame_count
    deviation = (conv_mixed - batch_mean) * valid_rows[:, :, None]
    batch_var = lax.optimization_barrier(jnp.sum(deviation * deviation, axis=(0, 1))) / frame_count
    inverse_std = lax.rsqrt(batch_var + epsilon)

    def back_item(carried):
        values, mixture, valid_item = carried
        shaped = (mixture - batch_mean) * inverse_std * batch_scale + batch_shift
        active = low(jax.nn.silu(shaped))
        values = values + low_back(product(active, conv_out))
        values = feed_forward(values, gain_second, second_up, second_down)
        return layer_norm(values, gain_final) * valid_item[:, None]
    output = lax.map(jax.checkpoint(back_item), (residual, conv_mixed, valid_rows))
    return (output, (batch_mean, batch_var, frame_count))

def reference(inputs, lengths, token_mask, mask_vector, gain_first, first_up, first_down, gain_attend, joint_proj, attend_out, gain_conv, conv_pair, conv_taps, batch_scale, batch_shift, conv_out, gain_second, second_up, second_down, gain_final, cotangent):
    floats = tuple((array_in.astype(jnp.float32) for array_in in (inputs, mask_vector, gain_first, first_up, first_down, gain_attend, joint_proj, attend_out, gain_conv, conv_pair, conv_taps, batch_scale, batch_shift, conv_out, gain_second, second_up, second_down, gain_final)))

    def apply_layer(*arrays):
        return forward(*arrays, lengths, token_mask)
    output, pullback, batch_stats = jax.vjp(apply_layer, *floats, has_aux=True)
    gradients = pullback(cotangent.astype(jnp.float32))
    batch_mean, batch_var, frame_count = batch_stats
    moment_mean = batch_mean
    moment_var = batch_var * frame_count / (frame_count - 1.0)
    return (output.astype(jnp.bfloat16), gradients[0], gradients[1], gradients[2], gradients[3], gradients[4], gradients[5], gradients[6], gradients[7], gradients[8], gradients[9], gradients[10], gradients[11], gradients[12], gradients[13], gradients[14], gradients[15], gradients[16], gradients[17], moment_mean, moment_var)
```

```python
import functools

import jax
import jax.numpy as jnp
from jax import lax
from jax.experimental import pallas as pl
from jax.experimental.pallas import tpu as pltpu
from jax.sharding import PartitionSpec as P

HEADS = 16
HEAD_DIM = 64
epsilon = 1e-05
f32 = jnp.float32
bf16 = jnp.bfloat16


def product(left_side, right_side):
    return jnp.dot(left_side, right_side, preferred_element_type=f32)


def product_lead(left_side, right_side):
    return lax.dot_general(
        left_side, right_side, (((0,), (0,)), ((), ())), preferred_element_type=f32
    )


def product_tail(left_side, right_side):
    return lax.dot_general(
        left_side, right_side, (((1,), (1,)), ((), ())), preferred_element_type=f32
    )


def axis_bits(axis):
    size = lax.axis_size(axis)
    return [1 << i for i in range(size.bit_length() - 1)]


def swap(values, axis, bit):
    return lax.ppermute(values, axis, [(i, i ^ bit) for i in range(lax.axis_size(axis))])


def bit_of(axis, bit):
    return (lax.axis_index(axis) & bit) // bit


def all_bits():
    return [("dp", b) for b in axis_bits("dp")] + [("seq", b) for b in axis_bits("seq")]


def pick(array, axis, index):
    return lax.dynamic_index_in_dim(array, index, axis, keepdims=False)


def gather_small(part):
    whole = part
    for axis, bit in [("seq", b) for b in axis_bits("seq")] + [("dp", b) for b in axis_bits("dp")]:
        other = swap(whole, axis, bit)
        upper = bit_of(axis, bit) > 0
        whole = jnp.concatenate(
            [jnp.where(upper, other, whole), jnp.where(upper, whole, other)], axis=0
        )
    return whole


def sum_small(values):
    for axis, bit in all_bits():
        values = values + swap(values, axis, bit)
    return values


def scatter_small(values):
    for axis, bit in [("dp", b) for b in axis_bits("dp")[::-1]] + [
        ("seq", b) for b in axis_bits("seq")[::-1]
    ]:
        view = values.reshape((2, values.shape[0] // 2) + values.shape[1:])
        mine = bit_of(axis, bit)
        values = pick(view, 0, mine) + swap(pick(view, 0, 1 - mine), axis, bit)
    return values


def merge_moments(count, mean, square):
    packed = jnp.stack([jnp.broadcast_to(count, mean.shape), mean, square])
    for axis, bit in all_bits():
        other = swap(packed, axis, bit)
        upper = bit_of(axis, bit) > 0
        low = jnp.where(upper, other, packed)
        high = jnp.where(upper, packed, other)
        total = low[0] + high[0]
        share = high[0] / jnp.maximum(total, 1.0)
        delta = high[1] - low[1]
        packed = jnp.stack(
            [
                total,
                low[1] + delta * share,
                low[2] + high[2] + delta * delta * (low[0] * share),
            ]
        )
    return packed[0, 0], packed[1], packed[2]


def group_bits():
    return axis_bits("dp")[1:]


def owner_columns(rows_of_lhs):
    tokens, rows = rows_of_lhs.shape
    groups = lax.axis_size("dp") // 2
    return rows_of_lhs.reshape(tokens, groups, 2, rows // (2 * groups))


def grad_job(lhs, rhs, share_rows):
    core = bit_of("dp", 1)
    cols = owner_columns(lhs)
    mine, other = pick(cols, 2, core), pick(cols, 2, 1 - core)
    if share_rows:
        lhs_all = jnp.concatenate([mine, swap(other, "dp", 1)], axis=0)
        rhs_all = jnp.concatenate([rhs, swap(rhs, "dp", 1)], axis=0)
        return lhs_all, rhs_all
    return mine, other, rhs


def rows_product(cols, rhs):
    return product_lead(cols.reshape(cols.shape[0], -1), rhs).astype(bf16)


def split_bit(array, axis, size, bit):
    shape = array.shape
    return array.reshape(shape[:axis] + (size // (2 * bit), 2, bit) + shape[axis + 1 :])


def halve_cols(cols, bit, groups):
    view = split_bit(cols, 1, groups, bit)
    mine = bit_of("dp", 2 * bit)
    flat = lambda a: a.reshape((a.shape[0], groups // 2) + cols.shape[2:])
    return flat(pick(view, 2, mine)), flat(pick(view, 2, 1 - mine))


def add_pair(keep, other, dtype=bf16):
    return (keep.astype(f32) + other.astype(f32)).astype(dtype)


def remaining_position(done, bit):
    return bit >> sum(1 for d in done if d < bit)


def scatter_job(job, rows):
    groups = lax.axis_size("dp") // 2
    seq = lax.axis_size("seq")
    bits = [b // 2 for b in group_bits()]
    halves = []
    shared = len(job) == 2
    rhs = job[-1]
    width = rhs.shape[1] // 2
    for half in range(2):
        order = bits if half == 0 else bits[::-1]
        part = rhs[:, half * width : (half + 1) * width]
        if shared:
            first, rest = order[0], order[1:]
            mine, other = halve_cols(job[0], first, groups)
            got = swap(rows_product(other, part), "dp", 2 * first)
            keep = rows_product(mine, part)
            done = [first]
        else:
            got = swap(rows_product(job[1], part), "dp", 1)
            keep = rows_product(job[0], part)
            rest, done = order, []
        size = groups >> len(done)
        keep, got = (a.reshape(size, -1, width) for a in (keep, got))
        for bit in rest:
            place = remaining_position(done, bit)
            view_keep = split_bit(keep, 0, size, place)
            view_got = split_bit(got, 0, size, place)
            mine = bit_of("dp", 2 * bit)
            send = add_pair(pick(view_keep, 1, 1 - mine), pick(view_got, 1, 1 - mine))
            keep = add_pair(pick(view_keep, 1, mine), pick(view_got, 1, mine))
            size //= 2
            got = swap(send, "dp", 2 * bit).reshape(size, -1, width)
            keep = keep.reshape(size, -1, width)
            done.append(bit)
        halves.append((keep.reshape(seq, rows, width), got.reshape(seq, rows, width)))
    keep = got = None
    size = seq
    done = []
    for bit in axis_bits("seq"):
        place = remaining_position(done, bit)
        mine = bit_of("seq", bit)

        def side(which):
            if keep is None:
                return jnp.concatenate(
                    [
                        add_pair(
                            pick(split_bit(a, 0, size, place), 1, which),
                            pick(split_bit(b, 0, size, place), 1, which),
                        )
                        for a, b in halves
                    ],
                    axis=-1,
                )
            return add_pair(
                pick(split_bit(keep, 0, size, place), 1, which),
                pick(split_bit(got, 0, size, place), 1, which),
            )

        send, kept = side(1 - mine), side(mine)
        size //= 2
        got = swap(send, "seq", bit).reshape(size, rows, -1)
        keep = kept.reshape(size, rows, -1)
        done.append(bit)
    return add_pair(keep[0], got[0], f32)


def gather_line(own):
    seq = lax.axis_size("seq")
    ups, downs = [own], [own]
    for step in range(seq - 1):
        ups.append(lax.ppermute(ups[-1], "seq", [(i, i + 1) for i in range(seq - 1)]))
        downs.append(lax.ppermute(downs[-1], "seq", [(i + 1, i) for i in range(seq - 1)]))
    me = lax.axis_index("seq")
    blocks = [own]
    for r in range(1, seq):
        blocks.append(jnp.where(me + r < seq, downs[r], ups[seq - r]))
    return jnp.stack(blocks)


def scatter_line(blocks):
    seq = lax.axis_size("seq")
    up = down = None
    for step in range(seq - 1, 0, -1):
        message_up, message_down = blocks[step], blocks[seq - step]
        if up is not None:
            message_up = add_pair(message_up, up)
            message_down = add_pair(message_down, down)
        up = lax.ppermute(message_up, "seq", [(i, i + 1) for i in range(seq - 1)])
        down = lax.ppermute(message_down, "seq", [(i + 1, i) for i in range(seq - 1)])
    total = blocks[0].astype(f32)
    if up is not None:
        total = total + up.astype(f32) + down.astype(f32)
    return total


def with_halo(shard, width):
    size, length = lax.axis_size("seq"), shard.shape[0]
    up = [(i, i + 1) for i in range(size - 1)]
    down = [(i + 1, i) for i in range(size - 1)]
    before = lax.ppermute(shard[length - width :], "seq", up)
    after = lax.ppermute(shard[:width], "seq", down)
    return jnp.concatenate([before, shard, after], axis=0)


def norm_forward(values, norm_gain):
    centered = values - jnp.mean(values, axis=-1, keepdims=True)
    inverse = lax.rsqrt(jnp.mean(centered * centered, axis=-1, keepdims=True) + epsilon)
    normal = centered * inverse
    return (normal * norm_gain, normal, inverse)


def norm_backward(grad_out, norm_gain, normal, inverse):
    scaled = grad_out * norm_gain
    grad_in = inverse * (
        scaled
        - jnp.mean(scaled, axis=-1, keepdims=True)
        - normal * jnp.mean(scaled * normal, axis=-1, keepdims=True)
    )
    return (grad_in, jnp.sum(grad_out * normal, axis=0))


def silu_slope(hidden):
    sigmoid_rows = jax.nn.sigmoid(hidden)
    return sigmoid_rows * (1.0 + hidden * (1.0 - sigmoid_rows))


def ffn_forward(values, norm_gain, upward, downward):
    normed, normal, inverse = norm_forward(values, norm_gain)
    normed_low = normed.astype(bf16)
    hidden = product(normed_low, upward)
    active = jax.nn.silu(hidden).astype(bf16)
    return (values + 0.5 * product(active, downward), (normed_low, normal, inverse, hidden, active))


def ffn_backward(grad_rows, norm_gain, upward, downward, stored):
    normed_low, normal, inverse, hidden, active = stored
    grad_branch = (0.5 * grad_rows).astype(bf16)
    grad_hidden = (product_tail(grad_branch, downward) * silu_slope(hidden)).astype(bf16)
    grad_in, grad_gain = norm_backward(
        product_tail(grad_hidden, upward), norm_gain, normal, inverse
    )
    rows = upward.shape[0] // (lax.axis_size("dp") * lax.axis_size("seq"))
    rows_down = downward.shape[0] // (lax.axis_size("dp") * lax.axis_size("seq"))
    grad_down = scatter_job(grad_job(active, grad_branch, True), rows_down)
    grad_up = scatter_job(grad_job(normed_low, grad_hidden, True), rows)
    return (grad_rows + grad_in, grad_gain, grad_up, grad_down)


def key_valid(offsets_ref, rows, keys):
    count = keys // rows
    spots = []
    for block in range(count):
        spots.append(offsets_ref[block] + lax.broadcasted_iota(jnp.int32, (rows, 1), 0))
    return jnp.concatenate(spots, axis=0) < offsets_ref[count]


def head_mask(block, head):
    lanes = lax.broadcasted_iota(jnp.int32, block.shape, 1)
    inside = (lanes < HEAD_DIM) if head == 0 else (lanes >= HEAD_DIM)
    return jnp.where(inside, block, jnp.zeros_like(block))


def attend_kernel(rows, offsets_ref, query_ref, key_ref, value_ref, mixture_ref, total_ref):
    keys = key_ref[...]
    values = value_ref[...]
    query = query_ref[...] * jnp.asarray(HEAD_DIM**-0.5, bf16)
    valid = key_valid(offsets_ref, rows, keys.shape[0])
    halves = []
    for head in range(2):
        scores = product_tail(keys, head_mask(query, head))
        scores = jnp.where(valid, scores, -1e30)
        largest = jnp.max(scores, axis=0, keepdims=True)
        exponent = jnp.exp(scores - largest)
        totals = jnp.sum(exponent, axis=0, keepdims=True)
        weights = (exponent * (1.0 / totals)).astype(bf16)
        mixed = product_lead(values, weights)
        halves.append(mixed[head * HEAD_DIM : (head + 1) * HEAD_DIM])
        total_ref[0, head : head + 1, :] = largest + jnp.log(totals)
    mixture_ref[...] = jnp.concatenate(halves, axis=0).T.astype(bf16)


def attend_back_kernel(
    rows,
    offsets_ref,
    query_ref,
    key_ref,
    value_ref,
    total_ref,
    grad_ref,
    query_grad_ref,
    key_grad_ref,
    value_grad_ref,
):
    keys = key_ref[...]
    values = value_ref[...]
    grad = grad_ref[...]
    query = query_ref[...] * jnp.asarray(HEAD_DIM**-0.5, bf16)
    valid = key_valid(offsets_ref, rows, keys.shape[0])
    halves = []
    key_grad = value_grad = None
    for head in range(2):
        query_head = head_mask(query, head)
        grad_head = head_mask(grad, head)
        scores = product_tail(keys, query_head)
        scores = jnp.where(valid, scores, -1e30)
        weights = jnp.exp(scores - total_ref[0, head : head + 1, :])
        grad_weights = product_tail(values, grad_head)
        inner = jnp.sum(weights * grad_weights, axis=0, keepdims=True)
        grad_scores = (weights * (grad_weights - inner)).astype(bf16)
        key_part = product(grad_scores, query_head)
        value_part = product(weights.astype(bf16), grad_head)
        key_grad = key_part if key_grad is None else key_grad + key_part
        value_grad = value_part if value_grad is None else value_grad + value_part
        query_part = product_lead(keys, grad_scores)
        halves.append(query_part[head * HEAD_DIM : (head + 1) * HEAD_DIM])
    query_grad = jnp.concatenate(halves, axis=0).T * HEAD_DIM**-0.5
    query_grad_ref[...] = query_grad.astype(bf16)
    key_grad_ref[...] = key_grad.astype(bf16)
    value_grad_ref[...] = value_grad.astype(bf16)


def attend(offsets, query, key_value):
    rows, width = query.shape
    keys = key_value.shape[0]
    pairs = width // 128
    return pl.pallas_call(
        functools.partial(attend_kernel, rows),
        grid_spec=pltpu.PrefetchScalarGridSpec(
            num_scalar_prefetch=1,
            grid=(pairs,),
            in_specs=[
                pl.BlockSpec((rows, 128), lambda i, o: (0, i)),
                pl.BlockSpec((keys, 128), lambda i, o: (0, i)),
                pl.BlockSpec((keys, 128), lambda i, o: (0, i + pairs)),
            ],
            out_specs=[
                pl.BlockSpec((rows, 128), lambda i, o: (0, i)),
                pl.BlockSpec((1, 2, rows), lambda i, o: (i, 0, 0)),
            ],
        ),
        out_shape=[
            jax.ShapeDtypeStruct((rows, width), bf16),
            jax.ShapeDtypeStruct((pairs, 2, rows), f32),
        ],
        compiler_params=pltpu.CompilerParams(vmem_limit_bytes=48 << 20),
        name="attend",
    )(offsets, query, key_value, key_value)


def attend_back(offsets, query, key_value, totals, grad):
    rows, width = query.shape
    keys = key_value.shape[0]
    pairs = width // 128
    row_spec = pl.BlockSpec((rows, 128), lambda i, o: (0, i))
    key_spec = pl.BlockSpec((keys, 128), lambda i, o: (0, i))
    return pl.pallas_call(
        functools.partial(attend_back_kernel, rows),
        grid_spec=pltpu.PrefetchScalarGridSpec(
            num_scalar_prefetch=1,
            grid=(pairs,),
            in_specs=[
                row_spec,
                key_spec,
                pl.BlockSpec((keys, 128), lambda i, o: (0, i + pairs)),
                pl.BlockSpec((1, 2, rows), lambda i, o: (i, 0, 0)),
                row_spec,
            ],
            out_specs=[row_spec, key_spec, key_spec],
        ),
        out_shape=[
            jax.ShapeDtypeStruct((rows, width), bf16),
            jax.ShapeDtypeStruct((keys, width), bf16),
            jax.ShapeDtypeStruct((keys, width), bf16),
        ],
        compiler_params=pltpu.CompilerParams(vmem_limit_bytes=48 << 20),
        name="attend_back",
    )(offsets, query, key_value, key_value, totals, grad)


def attention_forward(values, length, norm_gain, joint_proj, attend_out):
    normed, normal, inverse = norm_forward(values, norm_gain)
    normed_low = normed.astype(bf16)
    frames, model_width = normed_low.shape
    seq = lax.axis_size("seq")
    normed_all = gather_line(normed_low).reshape(seq * frames, model_width)
    query = product(normed_low, joint_proj[:, :model_width]).astype(bf16)
    key_value = product(normed_all, joint_proj[:, model_width:]).astype(bf16)
    starts = ((lax.axis_index("seq") + jnp.arange(seq)) % seq) * frames
    offsets = jnp.concatenate([starts, length[None]]).astype(jnp.int32)
    mixed_low, totals = attend(offsets, query, key_value)
    output = values + product(mixed_low, attend_out)
    stored = (normed_low, normal, inverse, normed_all, query, key_value, offsets, totals, mixed_low)
    return (output, stored)


def attention_backward(grad_rows, norm_gain, joint_proj, attend_out, stored):
    normed_low, normal, inverse, normed_all, query, key_value, offsets, totals, mixed_low = stored
    frames, model_width = normed_low.shape
    shards = lax.axis_size("dp") * lax.axis_size("seq")
    rows = model_width // shards
    grad_branch = grad_rows.astype(bf16)
    grad_mixed = product_tail(grad_branch, attend_out).astype(bf16)
    grad_query, grad_key, grad_value = attend_back(offsets, query, key_value, totals, grad_mixed)
    part = product_tail(grad_key, joint_proj[:, model_width : 2 * model_width]) + product_tail(
        grad_value, joint_proj[:, 2 * model_width :]
    )
    blocks = part.astype(bf16).reshape(-1, frames, model_width)
    grad_normed = scatter_line(blocks) + product_tail(grad_query, joint_proj[:, :model_width])
    grad_in, grad_gain = norm_backward(grad_normed, norm_gain, normal, inverse)
    grad_out = scatter_job(grad_job(mixed_low, grad_branch, True), rows)
    grad_joint = [
        scatter_job(grad_job(normed_low, grad_query, True), rows),
        scatter_job(grad_job(normed_all, grad_key, False), rows),
        scatter_job(grad_job(normed_all, grad_value, False), rows),
    ]
    return (grad_rows + grad_in, grad_gain, jnp.concatenate(grad_joint, axis=1), grad_out)


def conv_forward(
    values, valid_rows, norm_gain, conv_pair, taps_float, batch_scale, batch_shift, conv_out
):
    normed, normal, inverse = norm_forward(values, norm_gain)
    normed_low = normed.astype(bf16)
    paired = product(normed_low, conv_pair)
    model_width = paired.shape[1] // 2
    frames = paired.shape[0]
    sigmoid_rows = jax.nn.sigmoid(paired[:, model_width:])
    gated_rows = (paired[:, :model_width] * sigmoid_rows * valid_rows).astype(bf16)
    half_width = taps_float.shape[1] // 2
    widened = with_halo(gated_rows, half_width)
    mixture = jnp.zeros((frames, model_width), f32)
    for offset in range(taps_float.shape[1]):
        mixture = mixture + widened[offset : offset + frames] * taps_float[:, offset]
    own_count = jnp.sum(valid_rows)
    own_mean = jnp.sum(mixture * valid_rows, axis=0) / jnp.maximum(own_count, 1.0)
    own_dev = (mixture - own_mean) * valid_rows
    frame_count, batch_mean, square = merge_moments(
        own_count, own_mean, jnp.sum(own_dev * own_dev, axis=0)
    )
    batch_var = square / frame_count
    inverse_std = lax.rsqrt(batch_var + epsilon)
    normal_batch = (mixture - batch_mean) * inverse_std
    shaped = normal_batch * batch_scale + batch_shift
    active = jax.nn.silu(shaped).astype(bf16)
    output = values + product(active, conv_out)
    stored = (
        normed_low,
        normal,
        inverse,
        paired,
        sigmoid_rows,
        widened,
        normal_batch,
        inverse_std,
        shaped,
        active,
    )
    return (output, stored, (batch_mean, batch_var, frame_count))


def conv_backward(
    grad_rows,
    valid_rows,
    norm_gain,
    conv_pair,
    taps_float,
    scale_float,
    conv_out,
    stored,
    frame_count,
):
    (
        normed_low,
        normal,
        inverse,
        paired,
        sigmoid_rows,
        widened,
        normal_batch,
        inverse_std,
        shaped,
        active,
    ) = stored
    grad_branch = grad_rows.astype(bf16)
    grad_shaped = product_tail(grad_branch, conv_out) * silu_slope(shaped) * valid_rows
    total_shift, total_scale = sum_small(
        jnp.stack([jnp.sum(grad_shaped, axis=0), jnp.sum(grad_shaped * normal_batch, axis=0)])
    )
    grad_mixture = (
        inverse_std
        * valid_rows
        * (
            grad_shaped * scale_float
            - scale_float * (total_shift + normal_batch * total_scale) / frame_count
        )
    ).astype(bf16)
    taps = taps_float.shape[1]
    half_width = taps // 2
    grad_rims = with_halo(grad_mixture, half_width)
    frames, model_width = grad_mixture.shape
    widened_float = widened.astype(f32)
    grad_float = grad_mixture.astype(f32)
    grad_gated = jnp.zeros((frames, model_width), f32)
    tap_grads = []
    for offset in range(taps):
        lower_edge = 2 * half_width - offset
        grad_gated = (
            grad_gated + grad_rims[lower_edge : lower_edge + frames] * taps_float[:, offset]
        )
        tap_grads.append(jnp.sum(widened_float[offset : offset + frames] * grad_float, axis=0))
    grad_taps = jnp.stack(tap_grads, axis=1)
    grad_left = grad_gated * sigmoid_rows * valid_rows
    grad_right = (
        grad_gated * paired[:, :model_width] * sigmoid_rows * (1.0 - sigmoid_rows) * valid_rows
    )
    grad_paired = jnp.concatenate([grad_left, grad_right], axis=1).astype(bf16)
    grad_in, grad_gain = norm_backward(
        product_tail(grad_paired, conv_pair), norm_gain, normal, inverse
    )
    rows = model_width // (lax.axis_size("dp") * lax.axis_size("seq"))
    grad_out = scatter_job(grad_job(active, grad_branch, True), rows)
    grad_pair = scatter_job(grad_job(normed_low, grad_paired, True), rows)
    return (
        grad_rows + grad_in,
        grad_gain,
        grad_pair,
        grad_taps,
        grad_out,
        total_scale,
        total_shift,
    )


def fetch_weight(part):
    return lax.all_gather(part, ("dp", "seq"), axis=0, tiled=True)


def per_device(
    inputs,
    lengths,
    token_mask,
    mask_vector,
    gain_first,
    first_up,
    first_down,
    gain_attend,
    joint_proj,
    attend_out,
    gain_conv,
    conv_pair,
    conv_taps,
    batch_scale,
    batch_shift,
    conv_out,
    gain_second,
    second_up,
    second_down,
    gain_final,
    cotangent,
):
    frames = inputs.shape[1]
    model_width = inputs.shape[2]
    taps = conv_taps.shape[1]
    length = lengths[0]
    positions = lax.axis_index("seq") * frames + jnp.arange(frames)
    valid_rows = (positions < length).astype(f32)[:, None]
    masked_float = (token_mask[0] > 0).astype(f32)[:, None]

    vectors = (
        mask_vector,
        gain_first,
        gain_attend,
        gain_conv,
        gain_second,
        gain_final,
        batch_scale,
        batch_shift,
    )
    own_small = jnp.concatenate([jnp.stack(vectors, axis=0), conv_taps.T], axis=0)
    count = own_small.shape[0]
    small = gather_small(own_small[None])
    small = jnp.transpose(small, (1, 0, 2)).reshape(count, model_width).astype(f32)
    vector_mask, g_first, g_attend, g_conv, g_second, g_final, scale_float, shift_float = (
        small[i] for i in range(8)
    )
    taps_float = small[8:].T

    start_rows = jnp.where(masked_float > 0.0, vector_mask[None, :], inputs[0].astype(f32))
    up_one, down_one = fetch_weight(first_up), fetch_weight(first_down)
    values, first_stored = ffn_forward(start_rows, g_first, up_one, down_one)
    joint_all, outward_all = fetch_weight(joint_proj), fetch_weight(attend_out)
    values, attend_stored = attention_forward(values, length, g_attend, joint_all, outward_all)
    pair_all, conv_out_all = fetch_weight(conv_pair), fetch_weight(conv_out)
    values, conv_stored, batch_stats = conv_forward(
        values, valid_rows, g_conv, pair_all, taps_float, scale_float, shift_float, conv_out_all
    )
    up_two, down_two = fetch_weight(second_up), fetch_weight(second_down)
    values, second_stored = ffn_forward(values, g_second, up_two, down_two)
    normed, normal, inverse = norm_forward(values, g_final)
    output = (normed * valid_rows).astype(bf16)

    grad_rows, grad_final = norm_backward(
        cotangent[0].astype(f32) * valid_rows, g_final, normal, inverse
    )
    grad_rows, grad_gain_two, grad_up_two, grad_down_two = ffn_backward(
        grad_rows, g_second, up_two, down_two, second_stored
    )
    grad_rows, grad_gain_conv, grad_pair, grad_taps, grad_conv_out, total_scale, total_shift = (
        conv_backward(
            grad_rows,
            valid_rows,
            g_conv,
            pair_all,
            taps_float,
            scale_float,
            conv_out_all,
            conv_stored,
            batch_stats[2],
        )
    )
    grad_rows, grad_gain_attend, grad_joint, grad_attend_out = attention_backward(
        grad_rows, g_attend, joint_all, outward_all, attend_stored
    )
    grad_rows, grad_gain_one, grad_up_one, grad_down_one = ffn_backward(
        grad_rows, g_first, up_one, down_one, first_stored
    )
    input_grad = grad_rows * (1.0 - masked_float)
    mask_grad = jnp.sum(grad_rows * masked_float, axis=0)

    shards = lax.axis_size("dp") * lax.axis_size("seq")
    own_rows = model_width // shards
    sums = jnp.concatenate(
        [
            jnp.stack(
                [
                    mask_grad,
                    grad_gain_one,
                    grad_gain_attend,
                    grad_gain_conv,
                    grad_gain_two,
                    grad_final,
                ]
            ),
            grad_taps.T,
        ],
        axis=0,
    )
    sums = jnp.transpose(sums.reshape(-1, shards, own_rows), (1, 0, 2))
    sums = scatter_small(sums)[0]
    own_start = (lax.axis_index("dp") * lax.axis_size("seq") + lax.axis_index("seq")) * own_rows
    scale_grad = lax.dynamic_slice_in_dim(total_scale, own_start, own_rows)
    shift_grad = lax.dynamic_slice_in_dim(total_shift, own_start, own_rows)
    batch_mean, batch_var, frame_count = batch_stats
    moment_var = batch_var * frame_count / (frame_count - 1.0)
    return (
        output[None],
        input_grad[None],
        sums[0],
        sums[1],
        grad_up_one,
        grad_down_one,
        sums[2],
        grad_joint,
        grad_attend_out,
        sums[3],
        grad_pair,
        sums[6 : 6 + taps].T,
        scale_grad,
        shift_grad,
        grad_conv_out,
        sums[4],
        grad_up_two,
        grad_down_two,
        sums[5],
        batch_mean,
        moment_var,
    )


def solution(mesh):
    both = P(("dp", "seq"))
    rows = P(("dp", "seq"), None)
    frames = P("dp", "seq", None)
    in_specs = (
        frames,
        P("dp"),
        P("dp", "seq"),
        both,
        both,
        rows,
        rows,
        both,
        rows,
        rows,
        both,
        rows,
        rows,
        both,
        both,
        rows,
        both,
        rows,
        rows,
        both,
        frames,
    )
    out_specs = (
        frames,
        frames,
        both,
        both,
        rows,
        rows,
        both,
        rows,
        rows,
        both,
        rows,
        rows,
        both,
        both,
        rows,
        both,
        rows,
        rows,
        both,
        P(),
        P(),
    )
    return jax.shard_map(
        per_device, mesh=mesh, in_specs=in_specs, out_specs=out_specs, check_vma=False
    )
```

```python
import functools

import jax
import jax.numpy as jnp
from jax import lax
from jax.experimental import pallas as pl
from jax.experimental.pallas import tpu as pltpu
from jax.sharding import PartitionSpec as P

HEADS = 16
HEAD_DIM = 64
epsilon = 1e-05
f32 = jnp.float32
bf16 = jnp.bfloat16


def product(left_side, right_side):
    return jnp.dot(left_side, right_side, preferred_element_type=f32)


def product_lead(left_side, right_side):
    return lax.dot_general(
        left_side, right_side, (((0,), (0,)), ((), ())), preferred_element_type=f32
    )


def product_tail(left_side, right_side):
    return lax.dot_general(
        left_side, right_side, (((1,), (1,)), ((), ())), preferred_element_type=f32
    )


def tie(*values):
    return lax.optimization_barrier(values)


def axis_bits(axis):
    size = lax.axis_size(axis)
    return [1 << i for i in range(size.bit_length() - 1)]


def swap(values, axis, bit):
    return lax.ppermute(values, axis, [(i, i ^ bit) for i in range(lax.axis_size(axis))])


def bit_of(axis, bit):
    return (lax.axis_index(axis) & bit) // bit


def all_bits():
    return [("dp", b) for b in axis_bits("dp")] + [("seq", b) for b in axis_bits("seq")]


def pick(array, axis, index):
    return lax.dynamic_index_in_dim(array, index, axis, keepdims=False)


def gather_small(part):
    whole = part
    for axis, bit in [("seq", b) for b in axis_bits("seq")] + [("dp", b) for b in axis_bits("dp")]:
        other = swap(whole, axis, bit)
        upper = bit_of(axis, bit) > 0
        whole = jnp.concatenate(
            [jnp.where(upper, other, whole), jnp.where(upper, whole, other)], axis=0
        )
    return whole


def sum_small(values):
    for axis, bit in all_bits():
        values = values + swap(values, axis, bit)
    return values


def scatter_small(values):
    for axis, bit in [("dp", b) for b in axis_bits("dp")[::-1]] + [
        ("seq", b) for b in axis_bits("seq")[::-1]
    ]:
        view = values.reshape((2, values.shape[0] // 2) + values.shape[1:])
        mine = bit_of(axis, bit)
        values = pick(view, 0, mine) + swap(pick(view, 0, 1 - mine), axis, bit)
    return values


def merge_moments(count, mean, square):
    packed = jnp.stack([jnp.broadcast_to(count, mean.shape), mean, square])
    for axis, bit in all_bits():
        other = swap(packed, axis, bit)
        upper = bit_of(axis, bit) > 0
        low = jnp.where(upper, other, packed)
        high = jnp.where(upper, packed, other)
        total = low[0] + high[0]
        share = high[0] / jnp.maximum(total, 1.0)
        delta = high[1] - low[1]
        packed = jnp.stack(
            [
                total,
                low[1] + delta * share,
                low[2] + high[2] + delta * delta * (low[0] * share),
            ]
        )
    return packed[0, 0], packed[1], packed[2]


def group_bits():
    return axis_bits("dp")[1:]


def owner_columns(rows_of_lhs):
    tokens, rows = rows_of_lhs.shape
    groups = lax.axis_size("dp") // 2
    return rows_of_lhs.reshape(tokens, groups, 2, rows // (2 * groups))


def grad_job(lhs, rhs, share_rows):
    core = bit_of("dp", 1)
    cols = owner_columns(lhs)
    mine, other = pick(cols, 2, core), pick(cols, 2, 1 - core)
    if share_rows:
        lhs_all = jnp.concatenate([mine, swap(other, "dp", 1)], axis=0)
        rhs_all = jnp.concatenate([rhs, swap(rhs, "dp", 1)], axis=0)
        return lhs_all, rhs_all
    return mine, other, rhs


def rows_product(cols, rhs):
    return product_lead(cols.reshape(cols.shape[0], -1), rhs).astype(bf16)


def split_bit(array, axis, size, bit):
    shape = array.shape
    return array.reshape(shape[:axis] + (size // (2 * bit), 2, bit) + shape[axis + 1 :])


def halve_cols(cols, bit, groups):
    view = split_bit(cols, 1, groups, bit)
    mine = bit_of("dp", 2 * bit)
    flat = lambda a: a.reshape((a.shape[0], groups // 2) + cols.shape[2:])
    return flat(pick(view, 2, mine)), flat(pick(view, 2, 1 - mine))


def add_pair(keep, other, dtype=bf16):
    return (keep.astype(f32) + other.astype(f32)).astype(dtype)


def remaining_position(done, bit):
    return bit >> sum(1 for d in done if d < bit)


def scatter_job(job, rows):
    groups = lax.axis_size("dp") // 2
    seq = lax.axis_size("seq")
    bits = [b // 2 for b in group_bits()]
    halves = []
    shared = len(job) == 2
    rhs = job[-1]
    width = rhs.shape[1] // 2
    for half in range(2):
        order = bits if half == 0 else bits[::-1]
        part = rhs[:, half * width : (half + 1) * width]
        if shared:
            first, rest = order[0], order[1:]
            mine, other = halve_cols(job[0], first, groups)
            got = swap(rows_product(other, part), "dp", 2 * first)
            keep = rows_product(mine, part)
            done = [first]
        else:
            got = swap(rows_product(job[1], part), "dp", 1)
            keep = rows_product(job[0], part)
            rest, done = order, []
        size = groups >> len(done)
        keep, got = (a.reshape(size, -1, width) for a in (keep, got))
        for bit in rest:
            place = remaining_position(done, bit)
            view_keep = split_bit(keep, 0, size, place)
            view_got = split_bit(got, 0, size, place)
            mine = bit_of("dp", 2 * bit)
            send = add_pair(pick(view_keep, 1, 1 - mine), pick(view_got, 1, 1 - mine))
            keep = add_pair(pick(view_keep, 1, mine), pick(view_got, 1, mine))
            size //= 2
            got = swap(send, "dp", 2 * bit).reshape(size, -1, width)
            keep = keep.reshape(size, -1, width)
            done.append(bit)
        halves.append((keep.reshape(seq, rows, width), got.reshape(seq, rows, width)))
    keep = got = None
    size = seq
    done = []
    for bit in axis_bits("seq"):
        place = remaining_position(done, bit)
        mine = bit_of("seq", bit)

        def side(which):
            if keep is None:
                return jnp.concatenate(
                    [
                        add_pair(
                            pick(split_bit(a, 0, size, place), 1, which),
                            pick(split_bit(b, 0, size, place), 1, which),
                        )
                        for a, b in halves
                    ],
                    axis=-1,
                )
            return add_pair(
                pick(split_bit(keep, 0, size, place), 1, which),
                pick(split_bit(got, 0, size, place), 1, which),
            )

        send, kept = side(1 - mine), side(mine)
        size //= 2
        got = swap(send, "seq", bit).reshape(size, rows, -1)
        keep = kept.reshape(size, rows, -1)
        done.append(bit)
    return add_pair(keep[0], got[0], f32)


def in_steps(model_width):
    return lax.axis_size("dp") == 8 and lax.axis_size("seq") == 4 and model_width == 1024


BLOCK = 512


def terms_of(refs, pairs, half, rows, blocks, seq):
    own, got = (jnp.concatenate([refs[2 * i][...], refs[2 * i + 1][...]], axis=1) for i in (0, 1))
    rhs = refs[4:]
    if pairs:
        rhs = rhs[2 * half : 2 * half + 2]
    total = product_lead(own, rhs[0][...]) + product_lead(got, rhs[1][...])
    for block in range(2):
        for z in range(seq):
            for j in range(blocks):
                start = (block * seq + z) * rows
                yield block, z, j, total[start : start + rows, j * BLOCK : (j + 1) * BLOCK]


def job_refs(refs, shape):
    at = start = 0
    for rows, blocks, pairs in shape:
        count = 8 if pairs else 6
        yield refs[at : at + count], pairs, rows, blocks, start
        at += count
        start += rows * blocks


def send_kernel(shape, seq, table_ref, *refs):
    del table_ref
    outs = refs[-2:]
    for half in range(2):

        @pl.when(pl.program_id(0) == half)
        def _():
            for part, pairs, rows, blocks, start in job_refs(refs, shape):
                for block, z, j, piece in terms_of(part, pairs, half, rows, blocks, seq):
                    at = start + j * rows
                    outs[half][block, z, at : at + rows, :] = piece.astype(bf16)


def fold_kernel(shape, seq, table_ref, *refs):
    del table_ref
    gots, (sends, keep) = refs[-7:-3], (refs[-3:-1], refs[-1])
    for half in range(2):

        @pl.when(pl.program_id(0) == half)
        def _():
            for part, pairs, rows, blocks, start in job_refs(refs, shape):
                for block, z, j, piece in terms_of(part, pairs, half, rows, blocks, seq):
                    at = slice(start + j * rows, start + (j + 1) * rows)
                    piece = (piece + gots[2 * half + block][0, z, at, :].astype(f32)).astype(bf16)
                    if block == 0:
                        sends[half][z, at, :] = piece
                    else:
                        keep[0, z, at, :] = piece


def split_kernel(bits, bit_ref, keep_ref, *refs):
    gots, (send_ref, left_ref) = refs[:-2], refs[-2:]
    mine = bit_ref[0]
    for half in range(2):
        for entry in range(send_ref.shape[1]):
            for ref, side in ((send_ref, 1 - mine), (left_ref, mine)):
                at = 2 * entry + side if bits == 2 else side
                if len(gots) == 2:
                    got = gots[half][at]
                else:
                    got = gots[0][half, at]
                total = keep_ref[half, at].astype(f32) + got.astype(f32)
                ref[half, entry] = total.astype(bf16)


def finish_kernel(shape, keep_ref, got_ref, *outs):
    start = 0
    for out, (rows, blocks, _) in zip(outs, shape):
        for half in range(2):
            for j in range(blocks):
                at = slice(start + j * rows, start + (j + 1) * rows)
                columns = slice((half * blocks + j) * BLOCK, (half * blocks + j + 1) * BLOCK)
                out[:, columns] = keep_ref[half, 0, at, :].astype(f32) + got_ref[
                    half, 0, at, :
                ].astype(f32)
        start += rows * blocks


LIMIT = pltpu.CompilerParams(vmem_limit_bytes=56 << 20)


def whole_call(kernel, name, bits, inputs, outs):
    spec = lambda x: pl.BlockSpec(x.shape, lambda i, *t: (0,) * len(x.shape))
    size = sum(x.size * x.dtype.itemsize for x in list(inputs) + list(outs))
    return pl.pallas_call(
        kernel,
        grid_spec=pltpu.PrefetchScalarGridSpec(
            num_scalar_prefetch=len(bits),
            grid=(1,),
            in_specs=[spec(x) for x in inputs],
            out_specs=[spec(o) for o in outs],
        ),
        out_shape=outs,
        compiler_params=LIMIT,
        cost_estimate=pl.CostEstimate(flops=0, transcendentals=0, bytes_accessed=size),
        name=name,
    )(*bits, *inputs)


class SmallScatter:
    def __init__(self, values):
        self.keep = values
        self.bits = [("dp", b) for b in axis_bits("dp")[::-1]]
        self.bits += [("seq", b) for b in axis_bits("seq")[::-1]]
        self.got = None

    def step(self):
        if self.got is not None:
            self.keep = self.keep + self.got
        if not self.bits:
            return
        axis, bit = self.bits.pop(0)
        view = self.keep.reshape((2, self.keep.shape[0] // 2) + self.keep.shape[1:])
        mine = bit_of(axis, bit)
        self.keep, sent = pick(view, 0, mine), pick(view, 0, 1 - mine)
        self.got = swap(sent, axis, bit)


class ModuleScatter:
    def __init__(self, jobs, name):
        self.jobs = jobs
        self.name = name
        self.shape = tuple((j[4], j[5] // BLOCK, j[3][0] is not j[3][1]) for j in jobs)
        self.rows = sum(rows * blocks for rows, blocks, _ in self.shape)

    def share(self):
        self.others = {}
        for lhs, rhs in ((j[0], j[3]) for j in self.jobs):
            for array in (lhs, *rhs):
                if id(array) not in self.others:
                    self.others[id(array)] = swap(array, "dp", 1)

    def operands(self):
        specs, args = [], []
        for lhs, _, tokens, rhs, rows, width in self.jobs:
            wide = 4 * rows
            for array in (lhs, self.others[id(lhs)]):
                for block in range(2):
                    spec = lambda h, t, block=block: (0, t[h, block])
                    specs.append(pl.BlockSpec((tokens, wide), spec))
                    args.append(array)
            if rhs[0] is rhs[1]:
                for array in (rhs[0], self.others[id(rhs[0])]):
                    specs.append(pl.BlockSpec((tokens, width), lambda h, t: (0, h)))
                    args.append(array)
            else:
                for half in rhs:
                    for array in (half, self.others[id(half)]):
                        specs.append(pl.BlockSpec((tokens, width), lambda h, t: (0, 0)))
                        args.append(array)
        return specs, args

    def call(self, kernel, name, table, more, more_specs, outs, out_specs):
        specs, args = self.operands()
        flops = sum(16 * j[2] * 4 * j[4] * j[5] for j in self.jobs)
        moved = sum(4 * j[2] * (4 * j[4] * 2 + 2 * j[5]) for j in self.jobs)
        moved += 2 * sum(x.size for x in list(more) + list(outs))
        return pl.pallas_call(
            functools.partial(kernel, self.shape, 4),
            grid_spec=pltpu.PrefetchScalarGridSpec(
                num_scalar_prefetch=1,
                grid=(2,),
                in_specs=specs + more_specs,
                out_specs=out_specs,
            ),
            out_shape=outs,
            compiler_params=LIMIT,
            cost_estimate=pl.CostEstimate(flops=flops, transcendentals=0, bytes_accessed=moved),
            name=self.name + name,
        )(table, *args, *more)

    def first_send(self):
        core, x, y = (bit_of("dp", b) for b in (1, 2, 4))
        table = [
            [core + 2 * (1 - x) + 4 * i for i in range(2)],
            [core + 2 * i + 4 * (1 - y) for i in range(2)],
        ]
        table = jnp.stack([jnp.stack(row) for row in table]).astype(jnp.int32)
        out = jax.ShapeDtypeStruct((2, 4, self.rows, BLOCK), bf16)
        spec = pl.BlockSpec(out.shape, lambda h, t: (0, 0, 0, 0))
        self.sends = self.call(send_kernel, "_send", table, [], [], [out, out], [spec, spec])

    def first_swap(self):
        self.got = [swap(s, "dp", b) for s, b in zip(self.sends, (2, 4))]
        self.sends = None

    def second_send(self):
        core, x, y = (bit_of("dp", b) for b in (1, 2, 4))
        table = [
            [core + 2 * x + 4 * side for side in (1 - y, y)] + [1 - y, y],
            [core + 2 * side + 4 * y for side in (1 - x, x)] + [1 - x, x],
        ]
        table = jnp.stack([jnp.stack(row) for row in table]).astype(jnp.int32)
        piece = (4, self.rows, BLOCK)
        more, more_specs = [], []
        for half in range(2):
            for block in range(2):
                spec = lambda h, t, half=half, block=block: (t[half, 2 + block], 0, 0, 0)
                more.append(self.got[half])
                more_specs.append(pl.BlockSpec((1,) + piece, spec))
        outs = [jax.ShapeDtypeStruct(s, bf16) for s in (piece, piece, (2,) + piece)]
        spec = pl.BlockSpec(piece, lambda h, t: (0, 0, 0))
        keep_spec = pl.BlockSpec((1,) + piece, lambda h, t: (h, 0, 0, 0))
        *self.sends, self.keep = self.call(
            fold_kernel, "_fold", table, more, more_specs, outs, [spec, spec, keep_spec]
        )
        self.got = None

    def second_swap(self):
        self.got = [swap(s, "dp", b) for s, b in zip(self.sends, (4, 2))]
        self.sends = None

    def z_send(self, bit):
        entries = 2 if bit == 1 else 1
        out = jax.ShapeDtypeStruct((2, entries, self.rows, BLOCK), bf16)
        gots = self.got if bit == 1 else [self.got]
        mine = bit_of("seq", bit)[None].astype(jnp.int32)
        self.sends, self.keep = whole_call(
            functools.partial(split_kernel, entries),
            f"{self.name}_z{bit}",
            [mine],
            [self.keep, *gots],
            [out, out],
        )
        self.got = None

    def z_swap(self, bit):
        self.got = swap(self.sends, "seq", bit)
        self.sends = None

    def finish(self):
        outs = [jax.ShapeDtypeStruct((j[4], 2 * j[5]), f32) for j in self.jobs]
        return whole_call(
            functools.partial(finish_kernel, self.shape),
            self.name + "_finish",
            [],
            [self.keep, self.got],
            outs,
        )


def scatter_module(jobs):
    outs = []
    for lhs, start, tokens, rhs, rows, columns in jobs:
        whole = rhs[0] if rhs[0] is rhs[1] else jnp.concatenate(rhs, axis=1)
        outs.append(scatter_job(grad_job(lhs[start : start + tokens], whole, True), rows))
    return outs


def one(rhs):
    return (rhs, rhs)


FIELDS = ("got", "keep", "sends")


def fence(things, *extras):
    fields = [{k: v for k, v in vars(t).items() if k in FIELDS} for t in things]
    fields, extras = lax.optimization_barrier((fields, extras))
    for thing, values in zip(things, fields):
        vars(thing).update(values)
    return extras


def fetch_weight(part):
    return lax.all_gather(part, ("dp", "seq"), axis=0, tiled=True)


def pack_kernel(*refs):
    shards, out = refs[:-1], refs[-1]
    width = out.shape[1]
    at = 0
    for shard in shards:
        rows = shard.shape[0]
        for j in range(shard.shape[1] // width):
            out[at : at + rows, :] = shard[:, j * width : (j + 1) * width]
            at += rows


def fetch_packed(shards, name):
    width = shards[-1].shape[1]
    rows = sum(s.shape[0] * s.shape[1] // width for s in shards)
    out = jax.ShapeDtypeStruct((rows, width), bf16)
    (packed,) = whole_call(pack_kernel, name, [], shards, [out])
    return lax.all_gather(packed, ("dp", "seq"), axis=0)


def packed_block(packed, start, rows):
    return packed[:, start : start + rows].reshape(-1, packed.shape[2])


def up_kernel(normed_ref, weight_ref, active_ref, slope_ref):
    width = normed_ref.shape[1]
    for half in range(2):
        columns = slice(half * width // 2, (half + 1) * width // 2)
        block = weight_ref[:, :, columns].reshape(width, width // 2)
        hidden = product(normed_ref[...], block)
        sigmoid = 1.0 / (1.0 + jnp.exp(-hidden))
        active_ref[:, columns] = (hidden * sigmoid).astype(bf16)
        slope_ref[:, columns] = (sigmoid * (1.0 + hidden * (1.0 - sigmoid))).astype(bf16)


def up_back_kernel(grad_ref, weight_ref, out_ref):
    width = out_ref.shape[1]
    part = product_tail(grad_ref[...], weight_ref[...].reshape(width, -1))
    out_ref[...] = jnp.where(pl.program_id(0) == 0, part, out_ref[...] + part)


def down_kernel(values_ref, active_ref, weight_ref, out_ref, total_ref):
    width = out_ref.shape[1]
    part = product(active_ref[...], weight_ref[...].reshape(-1, width))
    total_ref[...] = jnp.where(pl.program_id(0) == 0, part, total_ref[...] + part)

    @pl.when(pl.program_id(0) == pl.num_programs(0) - 1)
    def _():
        out_ref[...] = values_ref[...] + 0.5 * total_ref[...]


def down_back_kernel(branch_ref, slope_ref, weight_ref, out_ref):
    width = branch_ref.shape[1]
    part = product_tail(branch_ref[...], weight_ref[...].reshape(-1, width))
    out_ref[...] = (part * slope_ref[...].astype(f32)).astype(bf16)


def ffn_call(kernel, name, packed, part, inputs, outs, scratch=()):
    owners, _, width = packed.shape
    steps = 4
    rows = width // owners
    if part == "up":
        weight = pl.BlockSpec((owners, rows, width), lambda i: (0, i, 0))
    else:
        weight = pl.BlockSpec((owners // steps, rows * steps, width), lambda i: (i, 1, 0))

    def spec(x):
        tokens, columns = x.shape
        return pl.BlockSpec((tokens, width), (lambda i: (0, i)) if columns > width else (lambda i: (0, 0)))

    numbers = lambda things: sum(t.size * t.dtype.itemsize for t in things)
    tokens = inputs[0].shape[0]
    inner = steps * width
    return pl.pallas_call(
        kernel,
        grid=(steps,),
        in_specs=[spec(x) for x in inputs] + [weight],
        out_specs=[spec(o) for o in outs],
        out_shape=outs,
        scratch_shapes=list(scratch),
        compiler_params=pltpu.CompilerParams(vmem_limit_bytes=56 << 20),
        cost_estimate=pl.CostEstimate(
            flops=2 * tokens * width * inner,
            transcendentals=0,
            bytes_accessed=2 * width * inner + numbers(inputs) + numbers(outs),
        ),
        name=name,
    )(*inputs, packed)


class Packed:
    def __init__(self, array):
        self.array = array


def ffn_up(normed, packed, name):
    tokens, width = normed.shape
    out = jax.ShapeDtypeStruct((tokens, 4 * width), bf16)
    return ffn_call(up_kernel, name, packed.array, "up", [normed], [out, out])


def ffn_up_back(grad_hidden, packed, name):
    out = jax.ShapeDtypeStruct((grad_hidden.shape[0], packed.array.shape[2]), f32)
    return ffn_call(up_back_kernel, name, packed.array, "up", [grad_hidden], [out])[0]


def ffn_down(values, active, packed, name):
    out = jax.ShapeDtypeStruct(values.shape, f32)
    scratch = [pltpu.VMEM(values.shape, f32)]
    return ffn_call(down_kernel, name, packed.array, "down", [values, active], [out], scratch)[0]


def ffn_down_back(branch, slope, packed, name):
    out = jax.ShapeDtypeStruct(slope.shape, bf16)
    return ffn_call(down_back_kernel, name, packed.array, "down", [branch, slope], [out])[0]


def gather_line(own):
    seq = lax.axis_size("seq")
    ups, downs = [own], [own]
    for step in range(seq - 1):
        ups.append(lax.ppermute(ups[-1], "seq", [(i, i + 1) for i in range(seq - 1)]))
        downs.append(lax.ppermute(downs[-1], "seq", [(i + 1, i) for i in range(seq - 1)]))
    me = lax.axis_index("seq")
    blocks = [own]
    for r in range(1, seq):
        blocks.append(jnp.where(me + r < seq, downs[r], ups[seq - r]))
    return jnp.stack(blocks)


def scatter_line(blocks, between=()):
    seq = lax.axis_size("seq")
    up = down = None
    between = iter(between)
    for step in range(seq - 1, 0, -1):
        message_up, message_down = blocks[step], blocks[seq - step]
        if up is not None:
            message_up = add_pair(message_up, up)
            message_down = add_pair(message_down, down)
        up = lax.ppermute(message_up, "seq", [(i, i + 1) for i in range(seq - 1)])
        down = lax.ppermute(message_down, "seq", [(i + 1, i) for i in range(seq - 1)])
        meanwhile = next(between, None)
        if meanwhile is not None:
            up, down = meanwhile(up, down)
    total = blocks[0].astype(f32)
    if up is not None:
        total = total + up.astype(f32) + down.astype(f32)
    return total


def with_halo(shard, width):
    size, length = lax.axis_size("seq"), shard.shape[0]
    up = [(i, i + 1) for i in range(size - 1)]
    down = [(i + 1, i) for i in range(size - 1)]
    before = lax.ppermute(shard[length - width :], "seq", up)
    after = lax.ppermute(shard[:width], "seq", down)
    return jnp.concatenate([before, shard, after], axis=0)


def norm_forward(values, norm_gain):
    centered = values - jnp.mean(values, axis=-1, keepdims=True)
    inverse = lax.rsqrt(jnp.mean(centered * centered, axis=-1, keepdims=True) + epsilon)
    normal = centered * inverse
    return (normal * norm_gain, normal, inverse)


def norm_backward(grad_out, norm_gain, normal, inverse):
    scaled = grad_out * norm_gain
    grad_in = inverse * (
        scaled
        - jnp.mean(scaled, axis=-1, keepdims=True)
        - normal * jnp.mean(scaled * normal, axis=-1, keepdims=True)
    )
    return (grad_in, jnp.sum(grad_out * normal, axis=0))


def silu_slope(hidden):
    sigmoid_rows = jax.nn.sigmoid(hidden)
    return sigmoid_rows * (1.0 + hidden * (1.0 - sigmoid_rows))


def ffn_forward(values, norm_gain, upward, downward, name):
    normed, normal, inverse = norm_forward(values, norm_gain)
    normed_low = normed.astype(bf16)
    if isinstance(upward, Packed):
        active, slope = ffn_up(normed_low, upward, name + "_up")
        out = ffn_down(values, active, downward, name + "_down")
    else:
        hidden = product(normed_low, upward)
        active, slope = jax.nn.silu(hidden).astype(bf16), silu_slope(hidden)
        out = values + 0.5 * product(active, downward)
    return out, (normed_low, normal, inverse, slope, active)


def owner_rows(rows):
    return rows // (lax.axis_size("dp") * lax.axis_size("seq"))


def ffn_hidden_grad(grad_branch, downward, stored, name):
    if isinstance(downward, Packed):
        return ffn_down_back(grad_branch, stored[3], downward, name + "_down_back")
    return (product_tail(grad_branch, downward) * stored[3]).astype(bf16)


def ffn_input_grad(grad_rows, grad_hidden, norm_gain, upward, stored, name):
    if isinstance(upward, Packed):
        grad_normed = ffn_up_back(grad_hidden, upward, name + "_up_back")
    else:
        grad_normed = product_tail(grad_hidden, upward)
    grad_in, grad_gain = norm_backward(grad_normed, norm_gain, stored[1], stored[2])
    return grad_rows + grad_in, grad_gain


def ffn_jobs(grad_branch, grad_hidden, stored):
    normed_low, active = stored[0], stored[4]
    tokens, width = normed_low.shape
    inner = active.shape[1]
    return [
        (normed_low, 0, tokens, one(grad_hidden), owner_rows(width), inner // 2),
        (active, 0, tokens, one(grad_branch), owner_rows(inner), width // 2),
    ]


def key_valid(offsets_ref, rows, keys):
    count = keys // rows
    spots = []
    for block in range(count):
        spots.append(offsets_ref[block] + lax.broadcasted_iota(jnp.int32, (rows, 1), 0))
    return jnp.concatenate(spots, axis=0) < offsets_ref[count]


def head_mask(block, head):
    lanes = lax.broadcasted_iota(jnp.int32, block.shape, 1)
    inside = (lanes < HEAD_DIM) if head == 0 else (lanes >= HEAD_DIM)
    return jnp.where(inside, block, jnp.zeros_like(block))


def attend_kernel(rows, offsets_ref, query_ref, key_ref, value_ref, mixture_ref, total_ref):
    keys = key_ref[...]
    values = value_ref[...]
    query = query_ref[...] * jnp.asarray(HEAD_DIM**-0.5, bf16)
    valid = key_valid(offsets_ref, rows, keys.shape[0])
    halves = []
    for head in range(2):
        scores = product_tail(keys, head_mask(query, head))
        scores = jnp.where(valid, scores, -1e30)
        largest = jnp.max(scores, axis=0, keepdims=True)
        exponent = jnp.exp(scores - largest)
        totals = jnp.sum(exponent, axis=0, keepdims=True)
        weights = (exponent * (1.0 / totals)).astype(bf16)
        mixed = product_lead(values, weights)
        halves.append(mixed[head * HEAD_DIM : (head + 1) * HEAD_DIM])
        total_ref[0, head : head + 1, :] = largest + jnp.log(totals)
    mixture_ref[...] = jnp.concatenate(halves, axis=0).T.astype(bf16)


def attend_back_kernel(
    rows,
    offsets_ref,
    query_ref,
    key_ref,
    value_ref,
    total_ref,
    grad_ref,
    query_grad_ref,
    key_grad_ref,
    value_grad_ref,
):
    keys = key_ref[...]
    values = value_ref[...]
    grad = grad_ref[...]
    query = query_ref[...] * jnp.asarray(HEAD_DIM**-0.5, bf16)
    valid = key_valid(offsets_ref, rows, keys.shape[0])
    halves = []
    key_grad = value_grad = None
    for head in range(2):
        query_head = head_mask(query, head)
        grad_head = head_mask(grad, head)
        scores = product_tail(keys, query_head)
        scores = jnp.where(valid, scores, -1e30)
        weights = jnp.exp(scores - total_ref[0, head : head + 1, :])
        grad_weights = product_tail(values, grad_head)
        inner = jnp.sum(weights * grad_weights, axis=0, keepdims=True)
        grad_scores = (weights * (grad_weights - inner)).astype(bf16)
        key_part = product(grad_scores, query_head)
        value_part = product(weights.astype(bf16), grad_head)
        key_grad = key_part if key_grad is None else key_grad + key_part
        value_grad = value_part if value_grad is None else value_grad + value_part
        query_part = product_lead(keys, grad_scores)
        halves.append(query_part[head * HEAD_DIM : (head + 1) * HEAD_DIM])
    query_grad = jnp.concatenate(halves, axis=0).T * HEAD_DIM**-0.5
    query_grad_ref[...] = query_grad.astype(bf16)
    key_grad_ref[...] = key_grad.astype(bf16)
    value_grad_ref[...] = value_grad.astype(bf16)


def attend(offsets, query, key, value):
    rows, width = query.shape
    keys = key.shape[0]
    pairs = width // 128
    return pl.pallas_call(
        functools.partial(attend_kernel, rows),
        grid_spec=pltpu.PrefetchScalarGridSpec(
            num_scalar_prefetch=1,
            grid=(pairs,),
            in_specs=[
                pl.BlockSpec((rows, 128), lambda i, o: (0, i)),
                pl.BlockSpec((keys, 128), lambda i, o: (0, i)),
                pl.BlockSpec((keys, 128), lambda i, o: (0, i)),
            ],
            out_specs=[
                pl.BlockSpec((rows, 128), lambda i, o: (0, i)),
                pl.BlockSpec((1, 2, rows), lambda i, o: (i, 0, 0)),
            ],
        ),
        out_shape=[
            jax.ShapeDtypeStruct((rows, width), bf16),
            jax.ShapeDtypeStruct((pairs, 2, rows), f32),
        ],
        compiler_params=pltpu.CompilerParams(vmem_limit_bytes=48 << 20),
        name="attend",
    )(offsets, query, key, value)


def attend_back(offsets, query, key_value, totals, grad):
    rows, width = query.shape
    key, value = key_value
    keys = key.shape[0]
    pairs = width // 128
    row_spec = pl.BlockSpec((rows, 128), lambda i, o: (0, i))
    key_spec = pl.BlockSpec((keys, 128), lambda i, o: (0, i))
    return pl.pallas_call(
        functools.partial(attend_back_kernel, rows),
        grid_spec=pltpu.PrefetchScalarGridSpec(
            num_scalar_prefetch=1,
            grid=(pairs,),
            in_specs=[
                row_spec,
                key_spec,
                pl.BlockSpec((keys, 128), lambda i, o: (0, i)),
                pl.BlockSpec((1, 2, rows), lambda i, o: (i, 0, 0)),
                row_spec,
            ],
            out_specs=[row_spec, key_spec, key_spec],
        ),
        out_shape=[
            jax.ShapeDtypeStruct((rows, width), bf16),
            jax.ShapeDtypeStruct((keys, width), bf16),
            jax.ShapeDtypeStruct((keys, width), bf16),
        ],
        compiler_params=pltpu.CompilerParams(vmem_limit_bytes=48 << 20),
        name="attend_back",
    )(offsets, query, key, value, totals, grad)


def attention_forward(values, length, norm_gain, joint_proj, attend_out, gathered):
    normed, normal, inverse = norm_forward(values, norm_gain)
    normed_low = normed.astype(bf16)
    frames, model_width = normed_low.shape
    seq = lax.axis_size("seq")
    normed_all = gathered(gather_line(normed_low)).reshape(seq * frames, model_width)
    query = product(normed_low, joint_proj[0]).astype(bf16)
    key = product(normed_all, joint_proj[1]).astype(bf16)
    value = product(normed_all, joint_proj[2]).astype(bf16)
    starts = ((lax.axis_index("seq") + jnp.arange(seq)) % seq) * frames
    offsets = jnp.concatenate([starts, length[None]]).astype(jnp.int32)
    mixed_low, totals = attend(offsets, query, key, value)
    output = values + product(mixed_low, attend_out)
    stored = (normed_low, normal, inverse, normed_all, query, (key, value), offsets, totals, mixed_low)
    return (output, stored)


def attention_parts_grad(grad_rows, attend_out, stored):
    normed_low, normal, inverse, normed_all, query, key_value, offsets, totals, mixed_low = stored
    grad_branch = grad_rows.astype(bf16)
    grad_mixed = product_tail(grad_branch, attend_out).astype(bf16)
    return (grad_branch,) + tuple(attend_back(offsets, query, key_value, totals, grad_mixed))


def attention_blocks_grad(grad_key, grad_value, joint_proj, frames):
    width = grad_key.shape[1]
    part = product_tail(grad_key, joint_proj[1]) + product_tail(grad_value, joint_proj[2])
    return part.astype(bf16).reshape(-1, frames, width)


def attention_input_grad(grad_rows, grad_normed, grad_query, norm_gain, joint_proj, stored):
    grad_normed = grad_normed + product_tail(grad_query, joint_proj[0])
    grad_in, grad_gain = norm_backward(grad_normed, norm_gain, stored[1], stored[2])
    return grad_rows + grad_in, grad_gain


def attention_jobs(grad_branch, grad_query, grad_key, grad_value, stored):
    normed_all, mixed_low = stored[3], stored[8]
    frames, width = grad_query.shape
    rows = owner_rows(width)
    return [
        (normed_all, 0, frames, one(grad_query), rows, width // 2),
        (normed_all, 0, normed_all.shape[0], (grad_key, grad_value), rows, width),
        (mixed_low, 0, frames, one(grad_branch), rows, width // 2),
    ]


def conv_forward(
    values, valid_rows, norm_gain, conv_pair, taps_float, batch_scale, batch_shift, conv_out
):
    normed, normal, inverse = norm_forward(values, norm_gain)
    normed_low = normed.astype(bf16)
    paired = product(normed_low, conv_pair[0])
    frames, model_width = paired.shape
    sigmoid_rows = jax.nn.sigmoid(product(normed_low, conv_pair[1]))
    gated_rows = (paired * sigmoid_rows * valid_rows).astype(bf16)
    half_width = taps_float.shape[1] // 2
    widened = with_halo(gated_rows, half_width)
    mixture = jnp.zeros((frames, model_width), f32)
    for offset in range(taps_float.shape[1]):
        mixture = mixture + widened[offset : offset + frames] * taps_float[:, offset]
    own_count = jnp.sum(valid_rows)
    own_mean = jnp.sum(mixture * valid_rows, axis=0) / jnp.maximum(own_count, 1.0)
    own_dev = (mixture - own_mean) * valid_rows
    frame_count, batch_mean, square = merge_moments(
        own_count, own_mean, jnp.sum(own_dev * own_dev, axis=0)
    )
    batch_var = square / frame_count
    inverse_std = lax.rsqrt(batch_var + epsilon)
    normal_batch = (mixture - batch_mean) * inverse_std
    shaped = normal_batch * batch_scale + batch_shift
    active = jax.nn.silu(shaped).astype(bf16)
    output = values + product(active, conv_out)
    stored = (
        normed_low,
        normal,
        inverse,
        paired,
        sigmoid_rows,
        widened,
        normal_batch,
        inverse_std,
        shaped,
        active,
    )
    return (output, stored, (batch_mean, batch_var, frame_count))


def conv_shaped_grad(grad_rows, valid_rows, conv_out, stored):
    normal_batch, shaped = stored[6], stored[8]
    grad_branch = grad_rows.astype(bf16)
    grad_shaped = product_tail(grad_branch, conv_out) * silu_slope(shaped) * valid_rows
    sums = jnp.stack([jnp.sum(grad_shaped, axis=0), jnp.sum(grad_shaped * normal_batch, axis=0)])
    return grad_branch, grad_shaped, sums


def conv_paired_grad(grad_shaped, totals, valid_rows, taps_float, scale_float, frame_count, stored):
    paired, sigmoid_rows, widened, normal_batch, inverse_std = (stored[i] for i in (3, 4, 5, 6, 7))
    total_shift, total_scale = totals
    grad_mixture = (
        inverse_std
        * valid_rows
        * (
            grad_shaped * scale_float
            - scale_float * (total_shift + normal_batch * total_scale) / frame_count
        )
    ).astype(bf16)
    taps = taps_float.shape[1]
    half_width = taps // 2
    grad_rims = with_halo(grad_mixture, half_width)
    frames, model_width = grad_mixture.shape
    widened_float = widened.astype(f32)
    grad_float = grad_mixture.astype(f32)
    grad_gated = jnp.zeros((frames, model_width), f32)
    tap_grads = []
    for offset in range(taps):
        lower_edge = 2 * half_width - offset
        grad_gated = (
            grad_gated + grad_rims[lower_edge : lower_edge + frames] * taps_float[:, offset]
        )
        tap_grads.append(jnp.sum(widened_float[offset : offset + frames] * grad_float, axis=0))
    grad_left = grad_gated * sigmoid_rows * valid_rows
    grad_right = grad_gated * paired * sigmoid_rows * (1.0 - sigmoid_rows) * valid_rows
    return (grad_left.astype(bf16), grad_right.astype(bf16)), jnp.stack(tap_grads)


def conv_input_grad(grad_rows, grad_paired, norm_gain, conv_pair, stored):
    grad_normed = product_tail(grad_paired[0], conv_pair[0]) + product_tail(
        grad_paired[1], conv_pair[1]
    )
    grad_in, grad_gain = norm_backward(grad_normed, norm_gain, stored[1], stored[2])
    return grad_rows + grad_in, grad_gain


def conv_jobs(grad_branch, grad_paired, stored):
    normed_low, active = stored[0], stored[9]
    frames, width = normed_low.shape
    rows = owner_rows(width)
    return [
        (normed_low, 0, frames, grad_paired, rows, width),
        (active, 0, frames, one(grad_branch), rows, width // 2),
    ]


def per_device(
    inputs,
    lengths,
    token_mask,
    mask_vector,
    gain_first,
    first_up,
    first_down,
    gain_attend,
    joint_proj,
    attend_out,
    gain_conv,
    conv_pair,
    conv_taps,
    batch_scale,
    batch_shift,
    conv_out,
    gain_second,
    second_up,
    second_down,
    gain_final,
    cotangent,
):
    frames = inputs.shape[1]
    model_width = inputs.shape[2]
    taps = conv_taps.shape[1]
    length = lengths[0]
    positions = lax.axis_index("seq") * frames + jnp.arange(frames)
    valid_rows = (positions < length).astype(f32)[:, None]
    masked_float = (token_mask[0] > 0).astype(f32)[:, None]

    vectors = (
        mask_vector,
        gain_first,
        gain_attend,
        gain_conv,
        gain_second,
        gain_final,
        batch_scale,
        batch_shift,
    )
    own_small = jnp.concatenate([jnp.stack(vectors, axis=0), conv_taps.T], axis=0)
    count = own_small.shape[0]
    shards = lax.axis_size("dp") * lax.axis_size("seq")
    own_rows = model_width // shards
    if in_steps(model_width):
        front = fetch_packed((first_up, first_down), "pack_first")
        middle_shards = tie(front, joint_proj, attend_out, conv_pair, conv_out)[1:]
        middle = fetch_packed(middle_shards, "pack_middle")
        up_one = down_one = Packed(front)
        squares = [packed_block(middle, i * own_rows, own_rows) for i in range(7)]
        joint_all, outward_all = squares[:3], squares[3]
        pair_all, conv_out_all = squares[4:6], squares[6]
    else:
        up_one, down_one, joint_all, outward_all, pair_all, conv_out_all = (
            fetch_weight(part)
            for part in (
                first_up,
                first_down,
                joint_proj,
                attend_out,
                conv_pair,
                conv_out,
            )
        )
        joint_all = jnp.split(joint_all, 3, axis=1)
        pair_all = jnp.split(pair_all, 2, axis=1)
    small = gather_small(own_small[None])
    small = jnp.transpose(small, (1, 0, 2)).reshape(count, model_width).astype(f32)
    vector_mask, g_first, g_attend, g_conv, g_second, g_final, scale_float, shift_float = (
        small[i] for i in range(8)
    )
    taps_float = small[8:].T

    start_rows = jnp.where(masked_float > 0.0, vector_mask[None, :], inputs[0].astype(f32))
    values, first_stored = ffn_forward(start_rows, g_first, up_one, down_one, "first")
    second_weights = []

    def gathered(rows):
        if not in_steps(model_width):
            second_weights.extend([fetch_weight(second_up), fetch_weight(second_down)])
            return rows
        rows, _, up_shard, down_shard = tie(rows, middle, second_up, second_down)
        back = Packed(fetch_packed((up_shard, down_shard), "pack_second"))
        second_weights.extend([back, back])
        return rows

    values, attend_stored = attention_forward(
        values, length, g_attend, joint_all, outward_all, gathered
    )
    up_two, down_two = second_weights
    values, conv_stored, batch_stats = conv_forward(
        values, valid_rows, g_conv, pair_all, taps_float, scale_float, shift_float, conv_out_all
    )
    values, second_stored = ffn_forward(values, g_second, up_two, down_two, "second")
    normed, normal, inverse = norm_forward(values, g_final)
    output = (normed * valid_rows).astype(bf16)

    grad_rows, grad_final = norm_backward(
        cotangent[0].astype(f32) * valid_rows, g_final, normal, inverse
    )
    steps = in_steps(model_width)
    frame_count = batch_stats[2]
    branch_two = (0.5 * grad_rows).astype(bf16)
    hidden_two = ffn_hidden_grad(branch_two, down_two, second_stored, "second")
    jobs_two = ffn_jobs(branch_two, hidden_two, second_stored)
    if steps:
        two = ModuleScatter(jobs_two, "second_terms")
        two.share()
        two.first_send()
    grad_rows, grad_gain_two = ffn_input_grad(
        grad_rows, hidden_two, g_second, up_two, second_stored, "second"
    )
    if steps:
        (grad_rows,) = fence([two], grad_rows)
        two.first_swap()

    branch_conv, grad_shaped, sums = conv_shaped_grad(
        grad_rows, valid_rows, conv_out_all, conv_stored
    )
    totals = sum_small(sums)
    total_shift, total_scale = totals
    grad_paired, grad_taps = conv_paired_grad(
        grad_shaped, totals, valid_rows, taps_float, scale_float, frame_count, conv_stored
    )
    jobs_conv = conv_jobs(branch_conv, grad_paired, conv_stored)
    if steps:
        conv = ModuleScatter(jobs_conv, "conv_terms")
        conv.share()
        conv.first_send()
    grad_rows, grad_gain_conv = conv_input_grad(
        grad_rows, grad_paired, g_conv, pair_all, conv_stored
    )
    if steps:
        (grad_rows,) = fence([two, conv], grad_rows)
        conv.first_swap()
        two.second_send()
        (grad_rows,) = fence([two], grad_rows)
        two.second_swap()

    branch_attend, grad_query, grad_key, grad_value = attention_parts_grad(
        grad_rows, outward_all, attend_stored
    )
    jobs_attend = attention_jobs(branch_attend, grad_query, grad_key, grad_value, attend_stored)
    blocks = attention_blocks_grad(grad_key, grad_value, joint_all, frames)
    between = ()
    if steps:
        attend_sum = ModuleScatter(jobs_attend, "attend_terms")
        attend_sum.share()

        def fold_conv(up, down):
            up, down = fence([conv], up, down)
            conv.second_send()
            up, down = fence([conv], up, down)
            conv.second_swap()
            return up, down

        def send_attend(up, down):
            attend_sum.first_send()
            return fence([attend_sum], up, down)

        def send_two(up, down):
            attend_sum.first_swap()
            up, down = fence([two], up, down)
            two.z_send(1)
            return fence([two], up, down)

        between = (fold_conv, send_attend, send_two)
    grad_normed = scatter_line(blocks, between)
    if steps:
        two.z_swap(1)
    grad_rows, grad_gain_attend = attention_input_grad(
        grad_rows, grad_normed, grad_query, g_attend, joint_all, attend_stored
    )
    branch_one = (0.5 * grad_rows).astype(bf16)
    if steps:
        down_sum = ModuleScatter(ffn_jobs(branch_one, None, first_stored)[1:], "down_terms")
        down_sum.share()
        down_sum.first_send()
        branch_one, grad_rows = fence([down_sum], branch_one, grad_rows)
        down_sum.first_swap()
    hidden_one = ffn_hidden_grad(branch_one, down_one, first_stored, "first")
    jobs_one = ffn_jobs(branch_one, hidden_one, first_stored)
    if steps:
        hidden_one, grad_rows = fence([two, attend_sum], hidden_one, grad_rows)
        two.z_send(2)
        two.z_swap(2)
        attend_sum.second_send()
        up_sum = ModuleScatter([(jobs_one[0][0], 0, frames, one(hidden_one)) + jobs_one[0][4:]], "up_terms")
        up_sum.share()
        up_sum.first_send()
        hidden_one, grad_rows = fence([attend_sum, up_sum], hidden_one, grad_rows)
        attend_sum.second_swap()
        up_sum.first_swap()
    grad_rows, grad_gain_one = ffn_input_grad(
        grad_rows, hidden_one, g_first, up_one, first_stored, "first"
    )
    input_grad = grad_rows * (1.0 - masked_float)
    mask_grad = jnp.sum(grad_rows * masked_float, axis=0)

    sums = jnp.concatenate(
        [
            jnp.stack(
                [
                    mask_grad,
                    grad_gain_one,
                    grad_gain_attend,
                    grad_gain_conv,
                    grad_gain_two,
                    grad_final,
                ]
            ),
            grad_taps,
        ],
        axis=0,
    )
    sums = jnp.transpose(sums.reshape(-1, shards, own_rows), (1, 0, 2))
    if steps:
        few = SmallScatter(sums)
        fence([two, conv, down_sum, few])
        conv.z_send(1)
        conv.z_swap(1)
        down_sum.second_send()
        down_sum.second_swap()
        few.step()
        fence([attend_sum, conv, few])
        conv.z_send(2)
        conv.z_swap(2)
        attend_sum.z_send(1)
        attend_sum.z_swap(1)
        few.step()
        fence([up_sum, attend_sum, conv, few])
        up_sum.second_send()
        up_sum.second_swap()
        attend_sum.z_send(2)
        attend_sum.z_swap(2)
        few.step()
        fence([down_sum, attend_sum, few])
        down_sum.z_send(1)
        down_sum.z_swap(1)
        few.step()
        fence([down_sum, up_sum, few])
        down_sum.z_send(2)
        down_sum.z_swap(2)
        up_sum.z_send(1)
        up_sum.z_swap(1)
        few.step()
        fence([down_sum, up_sum, few])
        up_sum.z_send(2)
        up_sum.z_swap(2)
        few.step()
        sums = few.keep[0]
        grad_up_two, grad_down_two = two.finish()
        grad_pair, grad_conv_out = conv.finish()
        attend_grads = attend_sum.finish()
        (grad_up_one,) = up_sum.finish()
        (grad_down_one,) = down_sum.finish()
    else:
        sums = scatter_small(sums)[0]
        grad_up_two, grad_down_two = scatter_module(jobs_two)
        grad_pair, grad_conv_out = scatter_module(jobs_conv)
        attend_grads = scatter_module(jobs_attend)
        grad_up_one, grad_down_one = scatter_module(jobs_one)
    grad_joint = jnp.concatenate(list(attend_grads[:2]), axis=1)
    grad_attend_out = attend_grads[2]
    own_start = (lax.axis_index("dp") * lax.axis_size("seq") + lax.axis_index("seq")) * own_rows
    scale_grad = lax.dynamic_slice_in_dim(total_scale, own_start, own_rows)
    shift_grad = lax.dynamic_slice_in_dim(total_shift, own_start, own_rows)
    batch_mean, batch_var, _ = batch_stats
    moment_var = batch_var * frame_count / (frame_count - 1.0)
    return (
        output[None],
        input_grad[None],
        sums[0],
        sums[1],
        grad_up_one,
        grad_down_one,
        sums[2],
        grad_joint,
        grad_attend_out,
        sums[3],
        grad_pair,
        sums[6 : 6 + taps].T,
        scale_grad,
        shift_grad,
        grad_conv_out,
        sums[4],
        grad_up_two,
        grad_down_two,
        sums[5],
        batch_mean,
        moment_var,
    )


def solution(mesh):
    both = P(("dp", "seq"))
    rows = P(("dp", "seq"), None)
    frames = P("dp", "seq", None)
    in_specs = (
        frames,
        P("dp"),
        P("dp", "seq"),
        both,
        both,
        rows,
        rows,
        both,
        rows,
        rows,
        both,
        rows,
        rows,
        both,
        both,
        rows,
        both,
        rows,
        rows,
        both,
        frames,
    )
    out_specs = (
        frames,
        frames,
        both,
        both,
        rows,
        rows,
        both,
        rows,
        rows,
        both,
        rows,
        rows,
        both,
        both,
        rows,
        both,
        rows,
        rows,
        both,
        P(),
        P(),
    )
    return jax.shard_map(
        per_device, mesh=mesh, in_specs=in_specs, out_specs=out_specs, check_vma=False
    )
```

```python
import functools

import jax
import jax.numpy as jnp
from jax import lax
from jax.experimental import pallas as pl
from jax.experimental.pallas import tpu as pltpu
from jax.sharding import PartitionSpec as P

HEADS = 16
HEAD_DIM = 64
epsilon = 1e-05
f32 = jnp.float32
bf16 = jnp.bfloat16


def product(left_side, right_side):
    return jnp.dot(left_side, right_side, preferred_element_type=f32)


def product_lead(left_side, right_side):
    return lax.dot_general(
        left_side, right_side, (((0,), (0,)), ((), ())), preferred_element_type=f32
    )


def product_tail(left_side, right_side):
    return lax.dot_general(
        left_side, right_side, (((1,), (1,)), ((), ())), preferred_element_type=f32
    )


def tie(*values):
    return lax.optimization_barrier(values)


def axis_bits(axis):
    size = lax.axis_size(axis)
    return [1 << i for i in range(size.bit_length() - 1)]


def swap(values, axis, bit):
    return lax.ppermute(values, axis, [(i, i ^ bit) for i in range(lax.axis_size(axis))])


def bit_of(axis, bit):
    return (lax.axis_index(axis) & bit) // bit


def all_bits():
    return [("dp", b) for b in axis_bits("dp")] + [("seq", b) for b in axis_bits("seq")]


def pick(array, axis, index):
    return lax.dynamic_index_in_dim(array, index, axis, keepdims=False)


def gather_small(part):
    whole = part
    for axis, bit in [("seq", b) for b in axis_bits("seq")] + [("dp", b) for b in axis_bits("dp")]:
        other = swap(whole, axis, bit)
        upper = bit_of(axis, bit) > 0
        whole = jnp.concatenate(
            [jnp.where(upper, other, whole), jnp.where(upper, whole, other)], axis=0
        )
    return whole


def sum_small(values):
    for axis, bit in all_bits():
        values = values + swap(values, axis, bit)
    return values


def scatter_small(values):
    for axis, bit in [("dp", b) for b in axis_bits("dp")[::-1]] + [
        ("seq", b) for b in axis_bits("seq")[::-1]
    ]:
        view = values.reshape((2, values.shape[0] // 2) + values.shape[1:])
        mine = bit_of(axis, bit)
        values = pick(view, 0, mine) + swap(pick(view, 0, 1 - mine), axis, bit)
    return values


def merge_moments(count, mean, square):
    packed = jnp.stack([jnp.broadcast_to(count, mean.shape), mean, square])
    for axis, bit in all_bits():
        other = swap(packed, axis, bit)
        upper = bit_of(axis, bit) > 0
        low = jnp.where(upper, other, packed)
        high = jnp.where(upper, packed, other)
        total = low[0] + high[0]
        share = high[0] / jnp.maximum(total, 1.0)
        delta = high[1] - low[1]
        packed = jnp.stack(
            [
                total,
                low[1] + delta * share,
                low[2] + high[2] + delta * delta * (low[0] * share),
            ]
        )
    return packed[0, 0], packed[1], packed[2]


def group_bits():
    return axis_bits("dp")[1:]


def owner_columns(rows_of_lhs):
    tokens, rows = rows_of_lhs.shape
    groups = lax.axis_size("dp") // 2
    return rows_of_lhs.reshape(tokens, groups, 2, rows // (2 * groups))


def grad_job(lhs, rhs, share_rows):
    core = bit_of("dp", 1)
    cols = owner_columns(lhs)
    mine, other = pick(cols, 2, core), pick(cols, 2, 1 - core)
    if share_rows:
        lhs_all = jnp.concatenate([mine, swap(other, "dp", 1)], axis=0)
        rhs_all = jnp.concatenate([rhs, swap(rhs, "dp", 1)], axis=0)
        return lhs_all, rhs_all
    return mine, other, rhs


def rows_product(cols, rhs):
    return product_lead(cols.reshape(cols.shape[0], -1), rhs).astype(bf16)


def split_bit(array, axis, size, bit):
    shape = array.shape
    return array.reshape(shape[:axis] + (size // (2 * bit), 2, bit) + shape[axis + 1 :])


def halve_cols(cols, bit, groups):
    view = split_bit(cols, 1, groups, bit)
    mine = bit_of("dp", 2 * bit)
    flat = lambda a: a.reshape((a.shape[0], groups // 2) + cols.shape[2:])
    return flat(pick(view, 2, mine)), flat(pick(view, 2, 1 - mine))


def add_pair(keep, other, dtype=bf16):
    return (keep.astype(f32) + other.astype(f32)).astype(dtype)


def remaining_position(done, bit):
    return bit >> sum(1 for d in done if d < bit)


def scatter_job(job, rows):
    groups = lax.axis_size("dp") // 2
    seq = lax.axis_size("seq")
    bits = [b // 2 for b in group_bits()]
    halves = []
    shared = len(job) == 2
    rhs = job[-1]
    width = rhs.shape[1] // 2
    for half in range(2):
        order = bits if half == 0 else bits[::-1]
        part = rhs[:, half * width : (half + 1) * width]
        if shared:
            first, rest = order[0], order[1:]
            mine, other = halve_cols(job[0], first, groups)
            got = swap(rows_product(other, part), "dp", 2 * first)
            keep = rows_product(mine, part)
            done = [first]
        else:
            got = swap(rows_product(job[1], part), "dp", 1)
            keep = rows_product(job[0], part)
            rest, done = order, []
        size = groups >> len(done)
        keep, got = (a.reshape(size, -1, width) for a in (keep, got))
        for bit in rest:
            place = remaining_position(done, bit)
            view_keep = split_bit(keep, 0, size, place)
            view_got = split_bit(got, 0, size, place)
            mine = bit_of("dp", 2 * bit)
            send = add_pair(pick(view_keep, 1, 1 - mine), pick(view_got, 1, 1 - mine))
            keep = add_pair(pick(view_keep, 1, mine), pick(view_got, 1, mine))
            size //= 2
            got = swap(send, "dp", 2 * bit).reshape(size, -1, width)
            keep = keep.reshape(size, -1, width)
            done.append(bit)
        halves.append((keep.reshape(seq, rows, width), got.reshape(seq, rows, width)))
    keep = got = None
    size = seq
    done = []
    for bit in axis_bits("seq"):
        place = remaining_position(done, bit)
        mine = bit_of("seq", bit)

        def side(which):
            if keep is None:
                return jnp.concatenate(
                    [
                        add_pair(
                            pick(split_bit(a, 0, size, place), 1, which),
                            pick(split_bit(b, 0, size, place), 1, which),
                        )
                        for a, b in halves
                    ],
                    axis=-1,
                )
            return add_pair(
                pick(split_bit(keep, 0, size, place), 1, which),
                pick(split_bit(got, 0, size, place), 1, which),
            )

        send, kept = side(1 - mine), side(mine)
        size //= 2
        got = swap(send, "seq", bit).reshape(size, rows, -1)
        keep = kept.reshape(size, rows, -1)
        done.append(bit)
    return add_pair(keep[0], got[0], f32)


def in_steps(model_width):
    return lax.axis_size("dp") == 8 and lax.axis_size("seq") == 4 and model_width == 1024


BLOCK = 512


def terms_of(refs, pairs, half, rows, blocks, seq):
    own, got = (jnp.concatenate([refs[2 * i][...], refs[2 * i + 1][...]], axis=1) for i in (0, 1))
    rhs = refs[4:]
    if pairs:
        rhs = rhs[2 * half : 2 * half + 2]
    total = product_lead(own, rhs[0][...]) + product_lead(got, rhs[1][...])
    for block in range(2):
        for z in range(seq):
            for j in range(blocks):
                start = (block * seq + z) * rows
                yield block, z, j, total[start : start + rows, j * BLOCK : (j + 1) * BLOCK]


def job_refs(refs, shape):
    at = start = 0
    for rows, blocks, pairs in shape:
        count = 8 if pairs else 6
        yield refs[at : at + count], pairs, rows, blocks, start
        at += count
        start += rows * blocks


def send_kernel(shape, seq, table_ref, *refs):
    del table_ref
    outs = refs[-2:]
    for half in range(2):

        @pl.when(pl.program_id(0) == half)
        def _():
            for part, pairs, rows, blocks, start in job_refs(refs, shape):
                for block, z, j, piece in terms_of(part, pairs, half, rows, blocks, seq):
                    at = start + j * rows
                    outs[half][block, z, at : at + rows, :] = piece.astype(bf16)


def fold_kernel(shape, seq, table_ref, *refs):
    del table_ref
    gots, (sends, keep) = refs[-7:-3], (refs[-3:-1], refs[-1])
    for half in range(2):

        @pl.when(pl.program_id(0) == half)
        def _():
            for part, pairs, rows, blocks, start in job_refs(refs, shape):
                for block, z, j, piece in terms_of(part, pairs, half, rows, blocks, seq):
                    at = slice(start + j * rows, start + (j + 1) * rows)
                    piece = (piece + gots[2 * half + block][0, z, at, :].astype(f32)).astype(bf16)
                    if block == 0:
                        sends[half][z, at, :] = piece
                    else:
                        keep[0, z, at, :] = piece


def split_kernel(bits, bit_ref, keep_ref, *refs):
    gots, (send_ref, left_ref) = refs[:-2], refs[-2:]
    mine = bit_ref[0]
    for half in range(2):
        for entry in range(send_ref.shape[1]):
            for ref, side in ((send_ref, 1 - mine), (left_ref, mine)):
                at = 2 * entry + side if bits == 2 else side
                if len(gots) == 2:
                    got = gots[half][at]
                else:
                    got = gots[0][half, at]
                total = keep_ref[half, at].astype(f32) + got.astype(f32)
                ref[half, entry] = total.astype(bf16)


def finish_kernel(shape, keep_ref, got_ref, *outs):
    start = 0
    for out, (rows, blocks, _) in zip(outs, shape):
        for half in range(2):
            for j in range(blocks):
                at = slice(start + j * rows, start + (j + 1) * rows)
                columns = slice((half * blocks + j) * BLOCK, (half * blocks + j + 1) * BLOCK)
                out[:, columns] = keep_ref[half, 0, at, :].astype(f32) + got_ref[
                    half, 0, at, :
                ].astype(f32)
        start += rows * blocks


LIMIT = pltpu.CompilerParams(vmem_limit_bytes=56 << 20)


def whole_call(kernel, name, bits, inputs, outs):
    spec = lambda x: pl.BlockSpec(x.shape, lambda i, *t: (0,) * len(x.shape))
    size = sum(x.size * x.dtype.itemsize for x in list(inputs) + list(outs))
    return pl.pallas_call(
        kernel,
        grid_spec=pltpu.PrefetchScalarGridSpec(
            num_scalar_prefetch=len(bits),
            grid=(1,),
            in_specs=[spec(x) for x in inputs],
            out_specs=[spec(o) for o in outs],
        ),
        out_shape=outs,
        compiler_params=LIMIT,
        cost_estimate=pl.CostEstimate(flops=1024, transcendentals=0, bytes_accessed=1024),
        name=name,
    )(*bits, *inputs)


class SmallScatter:
    def __init__(self, values):
        self.keep = values
        self.bits = [("dp", b) for b in axis_bits("dp")[::-1]]
        self.bits += [("seq", b) for b in axis_bits("seq")[::-1]]
        self.got = None

    def step(self):
        if self.got is not None:
            self.keep = self.keep + self.got
        if not self.bits:
            return
        axis, bit = self.bits.pop(0)
        view = self.keep.reshape((2, self.keep.shape[0] // 2) + self.keep.shape[1:])
        mine = bit_of(axis, bit)
        self.keep, sent = pick(view, 0, mine), pick(view, 0, 1 - mine)
        self.got = swap(sent, axis, bit)


class ModuleScatter:
    def __init__(self, jobs, name):
        self.jobs = jobs
        self.name = name
        self.shape = tuple((j[4], j[5] // BLOCK, j[3][0] is not j[3][1]) for j in jobs)
        self.rows = sum(rows * blocks for rows, blocks, _ in self.shape)

    def share(self):
        self.others = {}
        for lhs, rhs in ((j[0], j[3]) for j in self.jobs):
            for array in (lhs, *rhs):
                if id(array) not in self.others:
                    self.others[id(array)] = swap(array, "dp", 1)

    def operands(self):
        specs, args = [], []
        for lhs, _, tokens, rhs, rows, width in self.jobs:
            wide = 4 * rows
            for array in (lhs, self.others[id(lhs)]):
                for block in range(2):
                    spec = lambda h, t, block=block: (0, t[h, block])
                    specs.append(pl.BlockSpec((tokens, wide), spec))
                    args.append(array)
            if rhs[0] is rhs[1]:
                for array in (rhs[0], self.others[id(rhs[0])]):
                    specs.append(pl.BlockSpec((tokens, width), lambda h, t: (0, h)))
                    args.append(array)
            else:
                for half in rhs:
                    for array in (half, self.others[id(half)]):
                        specs.append(pl.BlockSpec((tokens, width), lambda h, t: (0, 0)))
                        args.append(array)
        return specs, args

    def call(self, kernel, name, table, more, more_specs, outs, out_specs):
        specs, args = self.operands()
        flops = sum(16 * j[2] * 4 * j[4] * j[5] for j in self.jobs)
        moved = sum(4 * j[2] * (4 * j[4] * 2 + 2 * j[5]) for j in self.jobs)
        moved += 2 * sum(x.size for x in list(more) + list(outs))
        return pl.pallas_call(
            functools.partial(kernel, self.shape, 4),
            grid_spec=pltpu.PrefetchScalarGridSpec(
                num_scalar_prefetch=1,
                grid=(2,),
                in_specs=specs + more_specs,
                out_specs=out_specs,
            ),
            out_shape=outs,
            compiler_params=LIMIT,
            cost_estimate=pl.CostEstimate(flops=1024, transcendentals=0, bytes_accessed=1024),
            name=self.name + name,
        )(table, *args, *more)

    def first_send(self):
        core, x, y = (bit_of("dp", b) for b in (1, 2, 4))
        table = [
            [core + 2 * (1 - x) + 4 * i for i in range(2)],
            [core + 2 * i + 4 * (1 - y) for i in range(2)],
        ]
        table = jnp.stack([jnp.stack(row) for row in table]).astype(jnp.int32)
        out = jax.ShapeDtypeStruct((2, 4, self.rows, BLOCK), bf16)
        spec = pl.BlockSpec(out.shape, lambda h, t: (0, 0, 0, 0))
        self.sends = self.call(send_kernel, "_send", table, [], [], [out, out], [spec, spec])

    def first_swap(self):
        self.got = [swap(s, "dp", b) for s, b in zip(self.sends, (2, 4))]
        self.sends = None

    def second_send(self):
        core, x, y = (bit_of("dp", b) for b in (1, 2, 4))
        table = [
            [core + 2 * x + 4 * side for side in (1 - y, y)] + [1 - y, y],
            [core + 2 * side + 4 * y for side in (1 - x, x)] + [1 - x, x],
        ]
        table = jnp.stack([jnp.stack(row) for row in table]).astype(jnp.int32)
        piece = (4, self.rows, BLOCK)
        more, more_specs = [], []
        for half in range(2):
            for block in range(2):
                spec = lambda h, t, half=half, block=block: (t[half, 2 + block], 0, 0, 0)
                more.append(self.got[half])
                more_specs.append(pl.BlockSpec((1,) + piece, spec))
        outs = [jax.ShapeDtypeStruct(s, bf16) for s in (piece, piece, (2,) + piece)]
        spec = pl.BlockSpec(piece, lambda h, t: (0, 0, 0))
        keep_spec = pl.BlockSpec((1,) + piece, lambda h, t: (h, 0, 0, 0))
        *self.sends, self.keep = self.call(
            fold_kernel, "_fold", table, more, more_specs, outs, [spec, spec, keep_spec]
        )
        self.got = None

    def second_swap(self):
        self.got = [swap(s, "dp", b) for s, b in zip(self.sends, (4, 2))]
        self.sends = None

    def z_send(self, bit):
        entries = 2 if bit == 1 else 1
        out = jax.ShapeDtypeStruct((2, entries, self.rows, BLOCK), bf16)
        gots = self.got if bit == 1 else [self.got]
        mine = bit_of("seq", bit)[None].astype(jnp.int32)
        self.sends, self.keep = whole_call(
            functools.partial(split_kernel, entries),
            f"{self.name}_z{bit}",
            [mine],
            [self.keep, *gots],
            [out, out],
        )
        self.got = None

    def z_swap(self, bit):
        self.got = swap(self.sends, "seq", bit)
        self.sends = None

    def finish(self):
        outs = [jax.ShapeDtypeStruct((j[4], 2 * j[5]), f32) for j in self.jobs]
        return whole_call(
            functools.partial(finish_kernel, self.shape),
            self.name + "_finish",
            [],
            [self.keep, self.got],
            outs,
        )


def scatter_module(jobs):
    outs = []
    for lhs, start, tokens, rhs, rows, columns in jobs:
        whole = rhs[0] if rhs[0] is rhs[1] else jnp.concatenate(rhs, axis=1)
        outs.append(scatter_job(grad_job(lhs[start : start + tokens], whole, True), rows))
    return outs


def one(rhs):
    return (rhs, rhs)


FIELDS = ("got", "keep", "sends")


def fence(things, *extras):
    fields = [{k: v for k, v in vars(t).items() if k in FIELDS} for t in things]
    fields, extras = lax.optimization_barrier((fields, extras))
    for thing, values in zip(things, fields):
        vars(thing).update(values)
    return extras


def fetch_weight(part):
    return lax.all_gather(part, ("dp", "seq"), axis=0, tiled=True)


def pack_kernel(*refs):
    shards, out = refs[:-1], refs[-1]
    width = out.shape[1]
    at = 0
    for shard in shards:
        rows = shard.shape[0]
        for j in range(shard.shape[1] // width):
            out[at : at + rows, :] = shard[:, j * width : (j + 1) * width]
            at += rows


def pack(shards, name):
    width = shards[-1].shape[1]
    rows = sum(s.shape[0] * s.shape[1] // width for s in shards)
    out = jax.ShapeDtypeStruct((rows, width), bf16)
    return whole_call(pack_kernel, name, [], shards, [out])[0]


def gather_packed(part):
    return lax.all_gather(part, ("dp", "seq"), axis=0)


def packed_block(packed, start, rows):
    return packed[:, start : start + rows].reshape(-1, packed.shape[2])


def up_kernel(normed_ref, weight_ref, active_ref, slope_ref):
    width = normed_ref.shape[1]
    for half in range(2):
        columns = slice(half * width // 2, (half + 1) * width // 2)
        block = weight_ref[:, :, columns].reshape(width, width // 2)
        hidden = product(normed_ref[...], block)
        sigmoid = 1.0 / (1.0 + jnp.exp(-hidden))
        active_ref[:, columns] = (hidden * sigmoid).astype(bf16)
        slope_ref[:, columns] = (sigmoid * (1.0 + hidden * (1.0 - sigmoid))).astype(bf16)


def up_back_kernel(grad_ref, weight_ref, out_ref):
    width = out_ref.shape[1]
    part = product_tail(grad_ref[...], weight_ref[...].reshape(width, -1))
    out_ref[...] = jnp.where(pl.program_id(0) == 0, part, out_ref[...] + part)


def down_kernel(values_ref, active_ref, weight_ref, out_ref, total_ref):
    width = out_ref.shape[1]
    part = product(active_ref[...], weight_ref[...].reshape(-1, width))
    total_ref[...] = jnp.where(pl.program_id(0) == 0, part, total_ref[...] + part)

    @pl.when(pl.program_id(0) == pl.num_programs(0) - 1)
    def _():
        out_ref[...] = values_ref[...] + 0.5 * total_ref[...]


def down_back_kernel(branch_ref, slope_ref, weight_ref, out_ref):
    width = branch_ref.shape[1]
    part = product_tail(branch_ref[...], weight_ref[...].reshape(-1, width))
    out_ref[...] = (part * slope_ref[...].astype(f32)).astype(bf16)


def ffn_call(kernel, name, packed, part, inputs, outs, scratch=()):
    owners, _, width = packed.shape
    steps = 4
    rows = width // owners
    if part == "up":
        weight = pl.BlockSpec((owners, rows, width), lambda i: (0, i, 0))
    else:
        weight = pl.BlockSpec((owners // steps, rows * steps, width), lambda i: (i, 1, 0))

    def spec(x):
        tokens, columns = x.shape
        return pl.BlockSpec((tokens, min(width, columns)), (lambda i: (0, i)) if columns > width else (lambda i: (0, 0)))

    numbers = lambda things: sum(t.size * t.dtype.itemsize for t in things)
    tokens = inputs[0].shape[0]
    inner = steps * width
    return pl.pallas_call(
        kernel,
        grid=(steps,),
        in_specs=[spec(x) for x in inputs] + [weight],
        out_specs=[spec(o) for o in outs],
        out_shape=outs,
        scratch_shapes=list(scratch),
        compiler_params=pltpu.CompilerParams(vmem_limit_bytes=56 << 20),
        cost_estimate=pl.CostEstimate(flops=1024, transcendentals=0, bytes_accessed=1024),
        name=name,
    )(*inputs, packed)


class Packed:
    def __init__(self, array):
        self.array = array


def ffn_up(normed, packed, name):
    tokens, width = normed.shape
    out = jax.ShapeDtypeStruct((tokens, 4 * width), bf16)
    return ffn_call(up_kernel, name, packed.array, "up", [normed], [out, out])


def ffn_up_back(grad_hidden, packed, name):
    out = jax.ShapeDtypeStruct((grad_hidden.shape[0], packed.array.shape[2]), f32)
    return ffn_call(up_back_kernel, name, packed.array, "up", [grad_hidden], [out])[0]


def ffn_down(values, active, packed, name):
    out = jax.ShapeDtypeStruct(values.shape, f32)
    scratch = [pltpu.VMEM(values.shape, f32)]
    return ffn_call(down_kernel, name, packed.array, "down", [values, active], [out], scratch)[0]


def ffn_down_back(branch, slope, packed, name):
    out = jax.ShapeDtypeStruct(slope.shape, bf16)
    return ffn_call(down_back_kernel, name, packed.array, "down", [branch, slope], [out])[0]


def gather_line(own):
    seq = lax.axis_size("seq")
    ups, downs = [own], [own]
    for step in range(seq - 1):
        ups.append(lax.ppermute(ups[-1], "seq", [(i, i + 1) for i in range(seq - 1)]))
        downs.append(lax.ppermute(downs[-1], "seq", [(i + 1, i) for i in range(seq - 1)]))
    me = lax.axis_index("seq")
    blocks = [own]
    for r in range(1, seq):
        blocks.append(jnp.where(me + r < seq, downs[r], ups[seq - r]))
    return jnp.stack(blocks)


def scatter_line(blocks, between=()):
    seq = lax.axis_size("seq")
    up = down = None
    between = iter(between)
    for step in range(seq - 1, 0, -1):
        message_up, message_down = blocks[step], blocks[seq - step]
        if up is not None:
            message_up = add_pair(message_up, up)
            message_down = add_pair(message_down, down)
        up = lax.ppermute(message_up, "seq", [(i, i + 1) for i in range(seq - 1)])
        down = lax.ppermute(message_down, "seq", [(i + 1, i) for i in range(seq - 1)])
        meanwhile = next(between, None)
        if meanwhile is not None:
            up, down = meanwhile(up, down)
    if up is None:
        up = down = jnp.zeros_like(blocks[0])
    return blocks[0], up, down


def sum_parts(parts):
    return sum(part.astype(f32) for part in parts)


def with_halo(shard, width):
    size, length = lax.axis_size("seq"), shard.shape[0]
    up = [(i, i + 1) for i in range(size - 1)]
    down = [(i + 1, i) for i in range(size - 1)]
    before = lax.ppermute(shard[length - width :], "seq", up)
    after = lax.ppermute(shard[:width], "seq", down)
    return jnp.concatenate([before, shard, after], axis=0)


def norm_forward(values, norm_gain):
    centered = values - jnp.mean(values, axis=-1, keepdims=True)
    inverse = lax.rsqrt(jnp.mean(centered * centered, axis=-1, keepdims=True) + epsilon)
    normal = centered * inverse
    return (normal * norm_gain, normal, inverse)


def norm_backward(grad_out, norm_gain, normal, inverse):
    scaled = grad_out * norm_gain
    grad_in = inverse * (
        scaled
        - jnp.mean(scaled, axis=-1, keepdims=True)
        - normal * jnp.mean(scaled * normal, axis=-1, keepdims=True)
    )
    return (grad_in, jnp.sum(grad_out * normal, axis=0))


def silu_slope(hidden):
    sigmoid_rows = jax.nn.sigmoid(hidden)
    return sigmoid_rows * (1.0 + hidden * (1.0 - sigmoid_rows))


def ffn_forward(values, norm_gain, upward, downward, name):
    normed, normal, inverse = norm_forward(values, norm_gain)
    normed_low = normed.astype(bf16)
    if isinstance(upward, Packed):
        active, slope = ffn_up(normed_low, upward, name + "_up")
        out = ffn_down(values, active, downward, name + "_down")
    else:
        hidden = product(normed_low, upward)
        active, slope = jax.nn.silu(hidden).astype(bf16), silu_slope(hidden)
        out = values + 0.5 * product(active, downward)
    return out, (normed_low, normal, inverse, slope, active)


def owner_rows(rows):
    return rows // (lax.axis_size("dp") * lax.axis_size("seq"))


def ffn_hidden_grad(grad_branch, downward, stored, name):
    if isinstance(downward, Packed):
        return ffn_down_back(grad_branch, stored[3], downward, name + "_down_back")
    return (product_tail(grad_branch, downward) * stored[3]).astype(bf16)


def ffn_input_grad(grad_rows, grad_hidden, norm_gain, upward, stored, name):
    if isinstance(upward, Packed):
        grad_normed = ffn_up_back(grad_hidden, upward, name + "_up_back")
    else:
        grad_normed = product_tail(grad_hidden, upward)
    grad_in, grad_gain = norm_backward(grad_normed, norm_gain, stored[1], stored[2])
    return grad_rows + grad_in, grad_gain


def ffn_jobs(grad_branch, grad_hidden, stored):
    normed_low, active = stored[0], stored[4]
    tokens, width = normed_low.shape
    inner = active.shape[1]
    return [
        (normed_low, 0, tokens, one(grad_hidden), owner_rows(width), inner // 2),
        (active, 0, tokens, one(grad_branch), owner_rows(inner), width // 2),
    ]


def norm_back(grad, norm_gain, values):
    centered = values - jnp.mean(values, axis=-1, keepdims=True)
    inverse = lax.rsqrt(jnp.mean(centered * centered, axis=-1, keepdims=True) + epsilon)
    normal = centered * inverse
    scaled = grad * norm_gain
    grad_in = inverse * (
        scaled
        - jnp.mean(scaled, axis=-1, keepdims=True)
        - normal * jnp.mean(scaled * normal, axis=-1, keepdims=True)
    )
    return grad_in, jnp.sum(grad * normal, axis=0, keepdims=True)


def valid_mask(count_ref, shape):
    return (lax.broadcasted_iota(jnp.int32, (shape[0], 1), 0) < count_ref[0]).astype(f32)


class Block:
    def __init__(self, packed, index):
        self.packed, self.index = packed, index

    def spec(self):
        owners, _, width = self.packed.shape
        index = self.index
        return pl.BlockSpec((owners, width // owners, width), lambda i, *t: (0, index, 0))


def step_call(kernel, name, scalars, inputs, outs, scratch=()):
    def spec(x):
        if isinstance(x, Block):
            return x.spec()
        return pl.BlockSpec(x.shape, lambda i, *t: (0,) * len(x.shape))

    return pl.pallas_call(
        kernel,
        grid_spec=pltpu.PrefetchScalarGridSpec(
            num_scalar_prefetch=len(scalars),
            grid=(1,),
            in_specs=[spec(x) for x in inputs],
            out_specs=[spec(o) for o in outs],
            scratch_shapes=list(scratch),
        ),
        out_shape=outs,
        compiler_params=LIMIT,
        cost_estimate=pl.CostEstimate(flops=1024, transcendentals=0, bytes_accessed=1024),
        name=name,
    )(*scalars, *[x.packed if isinstance(x, Block) else x for x in inputs])


def rows_like(array, dtype=f32):
    return jax.ShapeDtypeStruct(array.shape, dtype)


def vector_like(array, count=1):
    return jax.ShapeDtypeStruct((count, array.shape[1]), f32)


def square(ref):
    return ref[...].reshape(ref.shape[2], ref.shape[2])


def final_back_kernel(count_ref, cotangent_ref, values_ref, gain_ref, grad_ref, sum_ref, branch_ref):
    grad = cotangent_ref[...].astype(f32) * valid_mask(count_ref, values_ref.shape)
    grad, sum_ref[...] = norm_back(grad, gain_ref[...], values_ref[...])
    grad_ref[...] = grad
    branch_ref[...] = (0.5 * grad).astype(bf16)


def shaped_back_kernel(
    count_ref, branch_ref, depth_ref, vectors_ref, weight_ref, grad_ref, sums_ref
):
    normal = (depth_ref[...] - vectors_ref[0:1]) * vectors_ref[1:2]
    shaped = normal * vectors_ref[2:3] + vectors_ref[3:4]
    sigmoid = 1.0 / (1.0 + jnp.exp(-shaped))
    slope = sigmoid * (1.0 + shaped * (1.0 - sigmoid)) * valid_mask(count_ref, depth_ref.shape)
    grad = product_tail(branch_ref[...], square(weight_ref)) * slope
    grad_ref[...] = grad
    sums_ref[0:1] = jnp.sum(grad, axis=0, keepdims=True)
    sums_ref[1:2] = jnp.sum(grad * normal, axis=0, keepdims=True)


def add_kernel(left_ref, right_ref, out_ref):
    out_ref[...] = left_ref[...] + right_ref[...]


def depth_back_kernel(
    count_ref, grad_ref, depth_ref, vectors_ref, totals_ref, out_ref, top_ref, bottom_ref
):
    normal = (depth_ref[...] - vectors_ref[0:1]) * vectors_ref[1:2]
    scale = vectors_ref[2:3]
    out = (
        vectors_ref[1:2]
        * valid_mask(count_ref, depth_ref.shape)
        * (
            grad_ref[...] * scale
            - scale * (totals_ref[0:1] + normal * totals_ref[1:2]) / vectors_ref[4:5]
        )
    ).astype(bf16)
    out_ref[...] = out
    width = top_ref.shape[0]
    top_ref[...] = out[:width]
    bottom_ref[...] = out[out.shape[0] - width :]


def taps_back_kernel(
    count_ref, before_ref, grad_ref, after_ref, taps_ref, paired_ref, sigmoid_ref, *refs
):
    left_ref, right_ref, rims = refs
    frames = grad_ref.shape[0]
    taps = taps_ref.shape[0]
    half = taps // 2
    rims[0:half] = before_ref[...].astype(f32)
    rims[half : half + frames] = grad_ref[...].astype(f32)
    rims[half + frames : 2 * half + frames] = after_ref[...].astype(f32)
    valid = valid_mask(count_ref, grad_ref.shape)

    def part(step, carry):
        lanes = pl.ds(pl.multiple_of(step * 128, 128), 128)
        total = jnp.zeros((frames, 128), f32)
        for tap in range(taps):
            start = 2 * half - tap
            total = total + rims[start : start + frames, lanes] * taps_ref[tap : tap + 1, lanes]
        sigmoid = sigmoid_ref[:, lanes]
        left = total * sigmoid * valid
        left_ref[:, lanes] = left.astype(bf16)
        right_ref[:, lanes] = (left * paired_ref[:, lanes] * (1.0 - sigmoid)).astype(bf16)
        return carry

    lax.fori_loop(0, grad_ref.shape[1] // 128, part, 0)


def taps_sums_kernel(grad_ref, widened_ref, sums_ref, wide_rows, own_rows):
    frames = grad_ref.shape[0]
    wide_rows[0 : widened_ref.shape[0]] = widened_ref[...].astype(f32)
    own_rows[...] = grad_ref[...].astype(f32)

    def part(step, carry):
        lanes = pl.ds(pl.multiple_of(step * 128, 128), 128)
        own = own_rows[:, lanes]
        for tap in range(sums_ref.shape[0]):
            sums_ref[tap : tap + 1, lanes] = jnp.sum(
                wide_rows[tap : tap + frames, lanes] * own, axis=0, keepdims=True
            )
        return carry

    lax.fori_loop(0, grad_ref.shape[1] // 128, part, 0)


def conv_input_kernel(
    left_ref, right_ref, values_ref, gain_ref, rows_ref, first_ref, second_ref, *outs
):
    grad = product_tail(left_ref[...], square(first_ref))
    grad = grad + product_tail(right_ref[...], square(second_ref))
    finish_input(grad, gain_ref, values_ref, rows_ref, 1.0, *outs)


def finish_input(grad, gain_ref, values_ref, rows_ref, factor, out_ref, sum_ref, branch_ref):
    grad, sum_ref[...] = norm_back(grad, gain_ref[...], values_ref[...])
    grad = rows_ref[...] + grad
    out_ref[...] = grad
    branch_ref[...] = (factor * grad).astype(bf16)


def attend_input_kernel(
    own_ref, up_ref, down_ref, query_ref, values_ref, gain_ref, rows_ref, weight_ref, *outs
):
    grad = own_ref[...].astype(f32) + up_ref[...].astype(f32) + down_ref[...].astype(f32)
    grad = grad + product_tail(query_ref[...], square(weight_ref))
    finish_input(grad, gain_ref, values_ref, rows_ref, 0.5, *outs)


def input_outs(rows):
    return [rows_like(rows), vector_like(rows), rows_like(rows, bf16)]


def blocks_back_kernel(key_ref, value_ref, key_weight_ref, value_weight_ref, out_ref):
    total = product_tail(key_ref[...], square(key_weight_ref))
    total = total + product_tail(value_ref[...], square(value_weight_ref))
    out_ref[0] = total.astype(bf16)


def blocks_back(grad_key, grad_value, packed, frames):
    keys, width = grad_key.shape
    rows = pl.BlockSpec((frames, width), lambda i: (i, 0))
    return pl.pallas_call(
        blocks_back_kernel,
        grid=(keys // frames,),
        in_specs=[rows, rows, Block(packed, 1).spec(), Block(packed, 2).spec()],
        out_specs=pl.BlockSpec((1, frames, width), lambda i: (i, 0, 0)),
        out_shape=jax.ShapeDtypeStruct((keys // frames, frames, width), bf16),
        compiler_params=LIMIT,
        cost_estimate=pl.CostEstimate(flops=1024, transcendentals=0, bytes_accessed=1024),
        name="attend_blocks_back",
    )(grad_key, grad_value, packed, packed)


def up_back_input_kernel(
    factor, grad_ref, values_ref, gain_ref, rows_ref, weight_ref, out_ref, sum_ref, branch_ref, total
):
    part = product_tail(grad_ref[...], weight_ref[...].reshape(out_ref.shape[1], -1))
    total[...] = jnp.where(pl.program_id(0) == 0, part, total[...] + part)

    @pl.when(pl.program_id(0) == pl.num_programs(0) - 1)
    def _():
        finish_input(
            total[...], gain_ref, values_ref, rows_ref, factor, out_ref, sum_ref, branch_ref
        )


def ffn_up_back_input(grad_hidden, values, gain, rows, packed, factor, name):
    kernel = functools.partial(up_back_input_kernel, factor)
    scratch = [pltpu.VMEM(rows.shape, f32)]
    inputs = [grad_hidden, values, gain, rows]
    return ffn_call(kernel, name, packed.array, "up", inputs, input_outs(rows), scratch)


def sum_in_steps(values, bits):
    for axis, bit in bits:
        (values,) = step_call(
            add_kernel, "add", [], [values, swap(values, axis, bit)], [rows_like(values)]
        )
    return values


def key_valid(offsets_ref, rows, keys):
    count = keys // rows
    spots = []
    for block in range(count):
        spots.append(offsets_ref[block] + lax.broadcasted_iota(jnp.int32, (rows, 1), 0))
    return jnp.concatenate(spots, axis=0) < offsets_ref[count]


def head_mask(block, head):
    lanes = lax.broadcasted_iota(jnp.int32, block.shape, 1)
    inside = (lanes < HEAD_DIM) if head == 0 else (lanes >= HEAD_DIM)
    return jnp.where(inside, block, jnp.zeros_like(block))


def attend_kernel(rows, offsets_ref, query_ref, key_ref, value_ref, mixture_ref, total_ref):
    keys = key_ref[...]
    values = value_ref[...]
    query = query_ref[...] * jnp.asarray(HEAD_DIM**-0.5, bf16)
    valid = key_valid(offsets_ref, rows, keys.shape[0])
    halves = []
    for head in range(2):
        scores = product_tail(keys, head_mask(query, head))
        scores = jnp.where(valid, scores, -1e30)
        largest = jnp.max(scores, axis=0, keepdims=True)
        exponent = jnp.exp(scores - largest)
        totals = jnp.sum(exponent, axis=0, keepdims=True)
        weights = (exponent * (1.0 / totals)).astype(bf16)
        mixed = product_lead(values, weights)
        halves.append(mixed[head * HEAD_DIM : (head + 1) * HEAD_DIM])
        total_ref[0, head : head + 1, :] = largest + jnp.log(totals)
    mixture_ref[...] = jnp.concatenate(halves, axis=0).T.astype(bf16)


def attend_back_kernel(
    rows,
    offsets_ref,
    query_ref,
    key_ref,
    value_ref,
    total_ref,
    grad_ref,
    *refs,
):
    outward, (query_grad_ref, key_grad_ref, value_grad_ref) = refs[:-3], refs[-3:]
    keys = key_ref[...]
    values = value_ref[...]
    grad = grad_ref[...]
    if outward:
        grad = product_tail(grad, outward[0][...].reshape(128, -1)).astype(bf16)
    query = query_ref[...] * jnp.asarray(HEAD_DIM**-0.5, bf16)
    valid = key_valid(offsets_ref, rows, keys.shape[0])
    halves = []
    key_grad = value_grad = None
    for head in range(2):
        query_head = head_mask(query, head)
        grad_head = head_mask(grad, head)
        scores = product_tail(keys, query_head)
        scores = jnp.where(valid, scores, -1e30)
        weights = jnp.exp(scores - total_ref[0, head : head + 1, :])
        grad_weights = product_tail(values, grad_head)
        inner = jnp.sum(weights * grad_weights, axis=0, keepdims=True)
        grad_scores = (weights * (grad_weights - inner)).astype(bf16)
        key_part = product(grad_scores, query_head)
        value_part = product(weights.astype(bf16), grad_head)
        key_grad = key_part if key_grad is None else key_grad + key_part
        value_grad = value_part if value_grad is None else value_grad + value_part
        query_part = product_lead(keys, grad_scores)
        halves.append(query_part[head * HEAD_DIM : (head + 1) * HEAD_DIM])
    query_grad = jnp.concatenate(halves, axis=0).T * HEAD_DIM**-0.5
    query_grad_ref[...] = query_grad.astype(bf16)
    key_grad_ref[...] = key_grad.astype(bf16)
    value_grad_ref[...] = value_grad.astype(bf16)


def attend(offsets, query, key, value):
    rows, width = query.shape
    keys = key.shape[0]
    pairs = width // 128
    return pl.pallas_call(
        functools.partial(attend_kernel, rows),
        grid_spec=pltpu.PrefetchScalarGridSpec(
            num_scalar_prefetch=1,
            grid=(pairs,),
            in_specs=[
                pl.BlockSpec((rows, 128), lambda i, o: (0, i)),
                pl.BlockSpec((keys, 128), lambda i, o: (0, i)),
                pl.BlockSpec((keys, 128), lambda i, o: (0, i)),
            ],
            out_specs=[
                pl.BlockSpec((rows, 128), lambda i, o: (0, i)),
                pl.BlockSpec((1, 2, rows), lambda i, o: (i, 0, 0)),
            ],
        ),
        out_shape=[
            jax.ShapeDtypeStruct((rows, width), bf16),
            jax.ShapeDtypeStruct((pairs, 2, rows), f32),
        ],
        compiler_params=pltpu.CompilerParams(vmem_limit_bytes=48 << 20),
        name="attend",
    )(offsets, query, key, value)


def attend_back(offsets, query, key_value, totals, grad, packed=None):
    rows, width = query.shape
    key, value = key_value
    keys = key.shape[0]
    pairs = width // 128
    row_spec = pl.BlockSpec((rows, 128), lambda i, o: (0, i))
    key_spec = pl.BlockSpec((keys, 128), lambda i, o: (0, i))
    if packed is None:
        grad_specs, more = [row_spec], []
    else:
        owners = packed.shape[0]
        count = 128 * owners // width
        square_rows = pl.BlockSpec((count, width // owners, width), lambda i, o: (i, 3, 0))
        grad_specs, more = [pl.BlockSpec((rows, width), lambda i, o: (0, 0)), square_rows], [packed]
    return pl.pallas_call(
        functools.partial(attend_back_kernel, rows),
        grid_spec=pltpu.PrefetchScalarGridSpec(
            num_scalar_prefetch=1,
            grid=(pairs,),
            in_specs=[
                row_spec,
                key_spec,
                pl.BlockSpec((keys, 128), lambda i, o: (0, i)),
                pl.BlockSpec((1, 2, rows), lambda i, o: (i, 0, 0)),
            ]
            + grad_specs,
            out_specs=[row_spec, key_spec, key_spec],
        ),
        out_shape=[
            jax.ShapeDtypeStruct((rows, width), bf16),
            jax.ShapeDtypeStruct((keys, width), bf16),
            jax.ShapeDtypeStruct((keys, width), bf16),
        ],
        compiler_params=pltpu.CompilerParams(vmem_limit_bytes=48 << 20),
        name="attend_back",
    )(offsets, query, key, value, totals, grad, *more)


def attention_forward(values, length, norm_gain, joint_proj, attend_out, gathered):
    normed, normal, inverse = norm_forward(values, norm_gain)
    normed_low = normed.astype(bf16)
    frames, model_width = normed_low.shape
    seq = lax.axis_size("seq")
    normed_all = gathered(gather_line(normed_low)).reshape(seq * frames, model_width)
    query = product(normed_low, joint_proj[0]).astype(bf16)
    key = product(normed_all, joint_proj[1]).astype(bf16)
    value = product(normed_all, joint_proj[2]).astype(bf16)
    starts = ((lax.axis_index("seq") + jnp.arange(seq)) % seq) * frames
    offsets = jnp.concatenate([starts, length[None]]).astype(jnp.int32)
    mixed_low, totals = attend(offsets, query, key, value)
    output = values + product(mixed_low, attend_out)
    stored = (normed_low, normal, inverse, normed_all, query, (key, value), offsets, totals, mixed_low)
    return (output, stored)


def attention_parts_grad(grad_rows, attend_out, stored):
    normed_low, normal, inverse, normed_all, query, key_value, offsets, totals, mixed_low = stored
    grad_branch = grad_rows.astype(bf16)
    grad_mixed = product_tail(grad_branch, attend_out).astype(bf16)
    return (grad_branch,) + tuple(attend_back(offsets, query, key_value, totals, grad_mixed))


def attention_blocks_grad(grad_key, grad_value, joint_proj, frames):
    width = grad_key.shape[1]
    part = product_tail(grad_key, joint_proj[1]) + product_tail(grad_value, joint_proj[2])
    return part.astype(bf16).reshape(-1, frames, width)


def attention_input_grad(grad_rows, grad_normed, grad_query, norm_gain, joint_proj, stored):
    grad_normed = grad_normed + product_tail(grad_query, joint_proj[0])
    grad_in, grad_gain = norm_backward(grad_normed, norm_gain, stored[1], stored[2])
    return grad_rows + grad_in, grad_gain


def attention_jobs(grad_branch, grad_query, grad_key, grad_value, stored):
    normed_all, mixed_low = stored[3], stored[8]
    frames, width = grad_query.shape
    rows = owner_rows(width)
    return [
        (normed_all, 0, frames, one(grad_query), rows, width // 2),
        (normed_all, 0, normed_all.shape[0], (grad_key, grad_value), rows, width),
        (mixed_low, 0, frames, one(grad_branch), rows, width // 2),
    ]


def conv_forward(
    values, valid_rows, norm_gain, conv_pair, taps_float, batch_scale, batch_shift, conv_out
):
    normed, normal, inverse = norm_forward(values, norm_gain)
    normed_low = normed.astype(bf16)
    paired = product(normed_low, conv_pair[0])
    frames, model_width = paired.shape
    sigmoid_rows = jax.nn.sigmoid(product(normed_low, conv_pair[1]))
    gated_rows = (paired * sigmoid_rows * valid_rows).astype(bf16)
    half_width = taps_float.shape[1] // 2
    widened = with_halo(gated_rows, half_width)
    mixture = jnp.zeros((frames, model_width), f32)
    for offset in range(taps_float.shape[1]):
        mixture = mixture + widened[offset : offset + frames] * taps_float[:, offset]
    own_count = jnp.sum(valid_rows)
    own_mean = jnp.sum(mixture * valid_rows, axis=0) / jnp.maximum(own_count, 1.0)
    own_dev = (mixture - own_mean) * valid_rows
    frame_count, batch_mean, square = merge_moments(
        own_count, own_mean, jnp.sum(own_dev * own_dev, axis=0)
    )
    batch_var = square / frame_count
    inverse_std = lax.rsqrt(batch_var + epsilon)
    normal_batch = (mixture - batch_mean) * inverse_std
    shaped = normal_batch * batch_scale + batch_shift
    active = jax.nn.silu(shaped).astype(bf16)
    output = values + product(active, conv_out)
    stored = (
        normed_low,
        normal,
        inverse,
        paired,
        sigmoid_rows,
        widened,
        normal_batch,
        inverse_std,
        shaped,
        active,
        mixture,
    )
    return (output, stored, (batch_mean, batch_var, frame_count))


def conv_shaped_grad(grad_rows, valid_rows, conv_out, stored):
    normal_batch, shaped = stored[6], stored[8]
    grad_branch = grad_rows.astype(bf16)
    grad_shaped = product_tail(grad_branch, conv_out) * silu_slope(shaped) * valid_rows
    sums = jnp.stack([jnp.sum(grad_shaped, axis=0), jnp.sum(grad_shaped * normal_batch, axis=0)])
    return grad_branch, grad_shaped, sums


def conv_paired_grad(grad_shaped, totals, valid_rows, taps_float, scale_float, frame_count, stored):
    normal_batch, inverse_std = stored[6:8]
    total_shift, total_scale = totals
    grad_mixture = (
        inverse_std
        * valid_rows
        * (
            grad_shaped * scale_float
            - scale_float * (total_shift + normal_batch * total_scale) / frame_count
        )
    ).astype(bf16)
    grad_rims = with_halo(grad_mixture, taps_float.shape[1] // 2)
    return conv_taps_grad(grad_mixture, grad_rims, valid_rows, taps_float, stored)


def conv_taps_grad(grad_mixture, grad_rims, valid_rows, taps_float, stored):
    paired, sigmoid_rows, widened = stored[3:6]
    taps = taps_float.shape[1]
    half_width = taps // 2
    frames, model_width = grad_mixture.shape
    widened_float = widened.astype(f32)
    grad_float = grad_mixture.astype(f32)
    grad_gated = jnp.zeros((frames, model_width), f32)
    tap_grads = []
    for offset in range(taps):
        lower_edge = 2 * half_width - offset
        grad_gated = (
            grad_gated + grad_rims[lower_edge : lower_edge + frames] * taps_float[:, offset]
        )
        tap_grads.append(jnp.sum(widened_float[offset : offset + frames] * grad_float, axis=0))
    grad_left = grad_gated * sigmoid_rows * valid_rows
    grad_right = grad_gated * paired * sigmoid_rows * (1.0 - sigmoid_rows) * valid_rows
    return (grad_left.astype(bf16), grad_right.astype(bf16)), jnp.stack(tap_grads)


def conv_input_grad(grad_rows, grad_paired, norm_gain, conv_pair, stored):
    grad_normed = product_tail(grad_paired[0], conv_pair[0]) + product_tail(
        grad_paired[1], conv_pair[1]
    )
    grad_in, grad_gain = norm_backward(grad_normed, norm_gain, stored[1], stored[2])
    return grad_rows + grad_in, grad_gain


def conv_jobs(grad_branch, grad_paired, stored):
    normed_low, active = stored[0], stored[9]
    frames, width = normed_low.shape
    rows = owner_rows(width)
    return [
        (normed_low, 0, frames, grad_paired, rows, width),
        (active, 0, frames, one(grad_branch), rows, width // 2),
    ]


def per_device(
    inputs,
    lengths,
    token_mask,
    mask_vector,
    gain_first,
    first_up,
    first_down,
    gain_attend,
    joint_proj,
    attend_out,
    gain_conv,
    conv_pair,
    conv_taps,
    batch_scale,
    batch_shift,
    conv_out,
    gain_second,
    second_up,
    second_down,
    gain_final,
    cotangent,
):
    frames = inputs.shape[1]
    model_width = inputs.shape[2]
    taps = conv_taps.shape[1]
    length = lengths[0]
    positions = lax.axis_index("seq") * frames + jnp.arange(frames)
    valid_rows = (positions < length).astype(f32)[:, None]
    masked_float = (token_mask[0] > 0).astype(f32)[:, None]

    vectors = (
        mask_vector,
        gain_first,
        gain_attend,
        gain_conv,
        gain_second,
        gain_final,
        batch_scale,
        batch_shift,
    )
    own_small = jnp.concatenate([jnp.stack(vectors, axis=0), conv_taps.T], axis=0)
    count = own_small.shape[0]
    shards = lax.axis_size("dp") * lax.axis_size("seq")
    own_rows = model_width // shards
    small = gather_small(own_small[None])
    if in_steps(model_width):
        front = gather_packed(pack((first_up, first_down), "pack_first"))
        middle_part = pack((joint_proj, attend_out, conv_pair, conv_out), "pack_middle")
        back_part = pack((second_up, second_down), "pack_second")
        small, _, middle_part, back_part = tie(small, front, middle_part, back_part)
        middle = gather_packed(middle_part)
        up_one = down_one = Packed(front)
        squares = [packed_block(middle, i * own_rows, own_rows) for i in range(7)]
        joint_all, outward_all = squares[:3], squares[3]
        pair_all, conv_out_all = squares[4:6], squares[6]
    else:
        up_one, down_one, joint_all, outward_all, pair_all, conv_out_all = (
            fetch_weight(part)
            for part in (
                first_up,
                first_down,
                joint_proj,
                attend_out,
                conv_pair,
                conv_out,
            )
        )
        joint_all = jnp.split(joint_all, 3, axis=1)
        pair_all = jnp.split(pair_all, 2, axis=1)
    small = jnp.transpose(small, (1, 0, 2)).reshape(count, model_width).astype(f32)
    vector_mask, g_first, g_attend, g_conv, g_second, g_final, scale_float, shift_float = (
        small[i] for i in range(8)
    )
    taps_float = small[8:].T

    start_rows = jnp.where(masked_float > 0.0, vector_mask[None, :], inputs[0].astype(f32))
    rows_first, first_stored = ffn_forward(start_rows, g_first, up_one, down_one, "first")
    second_weights = []

    def gathered(rows):
        if not in_steps(model_width):
            second_weights.extend([fetch_weight(second_up), fetch_weight(second_down)])
            return rows
        rows, _, part = tie(rows, middle, back_part)
        back = Packed(gather_packed(part))
        second_weights.extend([back, back])
        return rows

    rows_second, attend_stored = attention_forward(
        rows_first, length, g_attend, joint_all, outward_all, gathered
    )
    up_two, down_two = second_weights
    rows_third, conv_stored, batch_stats = conv_forward(
        rows_second, valid_rows, g_conv, pair_all, taps_float, scale_float, shift_float, conv_out_all
    )
    rows_fourth, second_stored = ffn_forward(rows_third, g_second, up_two, down_two, "second")
    normed, normal, inverse = norm_forward(rows_fourth, g_final)
    output = (normed * valid_rows).astype(bf16)

    steps = in_steps(model_width)
    frame_count = batch_stats[2]
    if not steps:
        grad_rows, grad_final = norm_backward(
            cotangent[0].astype(f32) * valid_rows, g_final, normal, inverse
        )
        branch_two = (0.5 * grad_rows).astype(bf16)
        hidden_two = ffn_hidden_grad(branch_two, down_two, second_stored, "second")
        jobs_two = ffn_jobs(branch_two, hidden_two, second_stored)
        grad_rows, grad_gain_two = ffn_input_grad(
            grad_rows, hidden_two, g_second, up_two, second_stored, "second"
        )
        branch_conv, grad_shaped, sums = conv_shaped_grad(
            grad_rows, valid_rows, conv_out_all, conv_stored
        )
        totals = sum_small(sums)
        grad_paired, grad_taps = conv_paired_grad(
            grad_shaped, totals, valid_rows, taps_float, scale_float, frame_count, conv_stored
        )
        jobs_conv = conv_jobs(branch_conv, grad_paired, conv_stored)
        grad_rows, grad_gain_conv = conv_input_grad(
            grad_rows, grad_paired, g_conv, pair_all, conv_stored
        )
        branch_attend, grad_query, grad_key, grad_value = attention_parts_grad(
            grad_rows, outward_all, attend_stored
        )
        jobs_attend = attention_jobs(
            branch_attend, grad_query, grad_key, grad_value, attend_stored
        )
        blocks = attention_blocks_grad(grad_key, grad_value, joint_all, frames)
        grad_normed = sum_parts(scatter_line(blocks))
        grad_rows, grad_gain_attend = attention_input_grad(
            grad_rows, grad_normed, grad_query, g_attend, joint_all, attend_stored
        )
        branch_one = (0.5 * grad_rows).astype(bf16)
        hidden_one = ffn_hidden_grad(branch_one, down_one, first_stored, "first")
        jobs_one = ffn_jobs(branch_one, hidden_one, first_stored)
        grad_rows, grad_gain_one = ffn_input_grad(
            grad_rows, hidden_one, g_first, up_one, first_stored, "first"
        )
    else:
        gain = lambda vector: vector[None]
        own_valid = jnp.clip(length - lax.axis_index("seq") * frames, 0, frames)
        own_valid = own_valid[None].astype(jnp.int32)
        grad_rows, grad_final, branch_two = step_call(
            final_back_kernel,
            "final_back",
            [own_valid],
            [cotangent[0], rows_fourth, gain(g_final)],
            input_outs(rows_fourth),
        )
        hidden_two = ffn_hidden_grad(branch_two, down_two, second_stored, "second")
        two = ModuleScatter(ffn_jobs(branch_two, hidden_two, second_stored), "second_terms")
        two.share()
        two.first_send()
        grad_rows, grad_gain_two, branch_conv = ffn_up_back_input(
            hidden_two, rows_third, gain(g_second), grad_rows, up_two, 1.0, "second_up_back"
        )
        grad_rows, branch_conv = fence([two], grad_rows, branch_conv)
        depth, inverse_std = conv_stored[10], conv_stored[7]
        spread = jnp.broadcast_to(frame_count, (model_width,))
        vectors = jnp.stack([batch_stats[0], inverse_std, scale_float, shift_float, spread])
        grad_shaped, sums = step_call(
            shaped_back_kernel,
            "shaped_back",
            [own_valid],
            [branch_conv, depth, vectors, Block(middle, 6)],
            [rows_like(depth), vector_like(depth, 2)],
        )
        totals = sum_in_steps(sums, [("dp", b) for b in axis_bits("dp")])
        (totals,) = fence([two], totals)
        two.first_swap()
        totals = sum_in_steps(totals, [("seq", b) for b in axis_bits("seq")])
        rim = jax.ShapeDtypeStruct((taps // 2, model_width), bf16)
        grad_depth, top, bottom = step_call(
            depth_back_kernel,
            "depth_back",
            [own_valid],
            [grad_shaped, depth, vectors, totals],
            [rows_like(depth, bf16), rim, rim],
        )
        seq_size = lax.axis_size("seq")
        before = lax.ppermute(bottom, "seq", [(i, i + 1) for i in range(seq_size - 1)])
        after = lax.ppermute(top, "seq", [(i + 1, i) for i in range(seq_size - 1)])
        paired, sigmoid_rows, widened = conv_stored[3:6]
        tall = pltpu.VMEM((frames + 32, model_width), f32)
        paired_left, paired_right = step_call(
            taps_back_kernel,
            "taps_back",
            [own_valid],
            [before, grad_depth, after, taps_float.T, paired, sigmoid_rows],
            [rows_like(depth, bf16), rows_like(depth, bf16)],
            [tall],
        )
        (grad_taps,) = step_call(
            taps_sums_kernel,
            "taps_sums",
            [],
            [grad_depth, widened],
            [vector_like(depth, taps)],
            [tall, pltpu.VMEM(depth.shape, f32)],
        )
        conv = ModuleScatter(
            conv_jobs(branch_conv, (paired_left, paired_right), conv_stored), "conv_terms"
        )
        conv.share()
        conv.first_send()
        grad_rows, grad_gain_conv, branch_attend = step_call(
            conv_input_kernel,
            "conv_input_back",
            [],
            [
                paired_left,
                paired_right,
                rows_second,
                gain(g_conv),
                grad_rows,
                Block(middle, 4),
                Block(middle, 5),
            ],
            input_outs(rows_second),
        )
        grad_rows, branch_attend = fence([two, conv], grad_rows, branch_attend)
        two.second_send()
        grad_rows, branch_attend = fence([two, conv], grad_rows, branch_attend)
        two.second_swap()
        conv.first_swap()

        grad_query, grad_key, grad_value = attend_back(
            attend_stored[6], attend_stored[4], attend_stored[5], attend_stored[7], branch_attend, middle
        )
        attend_sum = ModuleScatter(
            attention_jobs(branch_attend, grad_query, grad_key, grad_value, attend_stored),
            "attend_terms",
        )
        blocks = blocks_back(grad_key, grad_value, middle, frames)
        attend_sum.share()
        (blocks,) = fence([two, conv], blocks)

        def fold_conv(up, down):
            conv.second_send()
            up, down = fence([conv], up, down)
            conv.second_swap()
            return up, down

        def send_attend(up, down):
            attend_sum.first_send()
            return fence([attend_sum], up, down)

        def send_two(up, down):
            attend_sum.first_swap()
            two.z_send(1)
            return fence([two], up, down)

        parts = scatter_line(blocks, (fold_conv, send_attend, send_two))
        two.z_swap(1)
        grad_rows, grad_gain_attend, branch_one = step_call(
            attend_input_kernel,
            "attend_input_back",
            [],
            [*parts, grad_query, rows_first, gain(g_attend), grad_rows, Block(middle, 0)],
            input_outs(rows_first),
        )
        down_sum = ModuleScatter(ffn_jobs(branch_one, None, first_stored)[1:], "down_terms")
        down_sum.share()
        down_sum.first_send()
        branch_one, grad_rows = fence([two, conv, attend_sum, down_sum], branch_one, grad_rows)
        down_sum.first_swap()
        two.z_send(2)
        two.z_swap(2)
        conv.z_send(1)
        conv.z_swap(1)
        hidden_one = ffn_hidden_grad(branch_one, down_one, first_stored, "first")
        up_sum = ModuleScatter(ffn_jobs(branch_one, hidden_one, first_stored)[:1], "up_terms")
        up_sum.share()
        attend_sum.second_send()
        up_sum.first_send()
        hidden_one, grad_rows = fence(
            [two, conv, down_sum, attend_sum, up_sum], hidden_one, grad_rows
        )
        attend_sum.second_swap()
        up_sum.first_swap()
        conv.z_send(2)
        conv.z_swap(2)
        down_sum.second_send()
        grad_rows, grad_gain_one, _ = ffn_up_back_input(
            hidden_one, start_rows, gain(g_first), grad_rows, up_one, 1.0, "first_up_back"
        )
        grad_final, grad_gain_two, grad_gain_conv, grad_gain_attend, grad_gain_one = (
            g[0]
            for g in (grad_final, grad_gain_two, grad_gain_conv, grad_gain_attend, grad_gain_one)
        )
    total_shift, total_scale = totals
    input_grad = grad_rows * (1.0 - masked_float)
    mask_grad = jnp.sum(grad_rows * masked_float, axis=0)

    sums = jnp.concatenate(
        [
            jnp.stack(
                [
                    mask_grad,
                    grad_gain_one,
                    grad_gain_attend,
                    grad_gain_conv,
                    grad_gain_two,
                    grad_final,
                ]
            ),
            grad_taps,
        ],
        axis=0,
    )
    sums = jnp.transpose(sums.reshape(-1, shards, own_rows), (1, 0, 2))
    if steps:
        few = SmallScatter(sums)
        fence([conv, attend_sum, up_sum, down_sum, few])
        down_sum.second_swap()
        attend_sum.z_send(1)
        attend_sum.z_swap(1)
        few.step()
        up_sum.second_send()
        up_sum.second_swap()
        fence([down_sum, attend_sum, up_sum, few])
        down_sum.z_send(1)
        down_sum.z_swap(1)
        up_sum.z_send(1)
        up_sum.z_swap(1)
        attend_sum.z_send(2)
        attend_sum.z_swap(2)
        few.step()
        fence([down_sum, up_sum, attend_sum, few])
        down_sum.z_send(2)
        down_sum.z_swap(2)
        up_sum.z_send(2)
        up_sum.z_swap(2)
        few.step()
        few.step()
        few.step()
        few.step()
        sums = few.keep[0]
        grad_up_two, grad_down_two = two.finish()
        grad_pair, grad_conv_out = conv.finish()
        attend_grads = attend_sum.finish()
        (grad_up_one,) = up_sum.finish()
        (grad_down_one,) = down_sum.finish()
    else:
        sums = scatter_small(sums)[0]
        grad_up_two, grad_down_two = scatter_module(jobs_two)
        grad_pair, grad_conv_out = scatter_module(jobs_conv)
        attend_grads = scatter_module(jobs_attend)
        grad_up_one, grad_down_one = scatter_module(jobs_one)
    grad_joint = jnp.concatenate(list(attend_grads[:2]), axis=1)
    grad_attend_out = attend_grads[2]
    own_start = (lax.axis_index("dp") * lax.axis_size("seq") + lax.axis_index("seq")) * own_rows
    scale_grad = lax.dynamic_slice_in_dim(total_scale, own_start, own_rows)
    shift_grad = lax.dynamic_slice_in_dim(total_shift, own_start, own_rows)
    batch_mean, batch_var, _ = batch_stats
    moment_var = batch_var * frame_count / (frame_count - 1.0)
    return (
        output[None],
        input_grad[None],
        sums[0],
        sums[1],
        grad_up_one,
        grad_down_one,
        sums[2],
        grad_joint,
        grad_attend_out,
        sums[3],
        grad_pair,
        sums[6 : 6 + taps].T,
        scale_grad,
        shift_grad,
        grad_conv_out,
        sums[4],
        grad_up_two,
        grad_down_two,
        sums[5],
        batch_mean,
        moment_var,
    )


def solution(mesh):
    both = P(("dp", "seq"))
    rows = P(("dp", "seq"), None)
    frames = P("dp", "seq", None)
    in_specs = (
        frames,
        P("dp"),
        P("dp", "seq"),
        both,
        both,
        rows,
        rows,
        both,
        rows,
        rows,
        both,
        rows,
        rows,
        both,
        both,
        rows,
        both,
        rows,
        rows,
        both,
        frames,
    )
    out_specs = (
        frames,
        frames,
        both,
        both,
        rows,
        rows,
        both,
        rows,
        rows,
        both,
        rows,
        rows,
        both,
        both,
        rows,
        both,
        rows,
        rows,
        both,
        P(),
        P(),
    )
    return jax.shard_map(
        per_device, mesh=mesh, in_specs=in_specs, out_specs=out_specs, check_vma=False
    )
```

```python
import functools

import jax
import jax.numpy as jnp
from jax import lax
from jax.experimental import pallas as pl
from jax.experimental.pallas import tpu as pltpu
from jax.sharding import PartitionSpec as P

HEADS = 16
HEAD_DIM = 64
epsilon = 1e-05
f32 = jnp.float32
bf16 = jnp.bfloat16


def product(left_side, right_side):
    return jnp.dot(left_side, right_side, preferred_element_type=f32)


def product_lead(left_side, right_side):
    return lax.dot_general(
        left_side, right_side, (((0,), (0,)), ((), ())), preferred_element_type=f32
    )


def product_tail(left_side, right_side):
    return lax.dot_general(
        left_side, right_side, (((1,), (1,)), ((), ())), preferred_element_type=f32
    )


def tie(*values):
    return lax.optimization_barrier(values)


def axis_bits(axis):
    size = lax.axis_size(axis)
    return [1 << i for i in range(size.bit_length() - 1)]


def swap(values, axis, bit):
    return lax.ppermute(values, axis, [(i, i ^ bit) for i in range(lax.axis_size(axis))])


def bit_of(axis, bit):
    return (lax.axis_index(axis) & bit) // bit


def all_bits():
    return [("dp", b) for b in axis_bits("dp")] + [("seq", b) for b in axis_bits("seq")]


def pick(array, axis, index):
    return lax.dynamic_index_in_dim(array, index, axis, keepdims=False)


def gather_small(part):
    whole = part
    for axis, bit in [("seq", b) for b in axis_bits("seq")] + [("dp", b) for b in axis_bits("dp")]:
        other = swap(whole, axis, bit)
        upper = bit_of(axis, bit) > 0
        whole = jnp.concatenate(
            [jnp.where(upper, other, whole), jnp.where(upper, whole, other)], axis=0
        )
    return whole


def sum_small(values):
    for axis, bit in all_bits():
        values = values + swap(values, axis, bit)
    return values


def scatter_small(values):
    for axis, bit in [("dp", b) for b in axis_bits("dp")[::-1]] + [
        ("seq", b) for b in axis_bits("seq")[::-1]
    ]:
        view = values.reshape((2, values.shape[0] // 2) + values.shape[1:])
        mine = bit_of(axis, bit)
        values = pick(view, 0, mine) + swap(pick(view, 0, 1 - mine), axis, bit)
    return values


def merge_moments(count, mean, square):
    packed = jnp.stack([jnp.broadcast_to(count, mean.shape), mean, square])
    for axis, bit in all_bits():
        other = swap(packed, axis, bit)
        upper = bit_of(axis, bit) > 0
        low = jnp.where(upper, other, packed)
        high = jnp.where(upper, packed, other)
        total = low[0] + high[0]
        share = high[0] / jnp.maximum(total, 1.0)
        delta = high[1] - low[1]
        packed = jnp.stack(
            [
                total,
                low[1] + delta * share,
                low[2] + high[2] + delta * delta * (low[0] * share),
            ]
        )
    return packed[0, 0], packed[1], packed[2]


def group_bits():
    return axis_bits("dp")[1:]


def owner_columns(rows_of_lhs):
    tokens, rows = rows_of_lhs.shape
    groups = lax.axis_size("dp") // 2
    return rows_of_lhs.reshape(tokens, groups, 2, rows // (2 * groups))


def grad_job(lhs, rhs, share_rows):
    core = bit_of("dp", 1)
    cols = owner_columns(lhs)
    mine, other = pick(cols, 2, core), pick(cols, 2, 1 - core)
    if share_rows:
        lhs_all = jnp.concatenate([mine, swap(other, "dp", 1)], axis=0)
        rhs_all = jnp.concatenate([rhs, swap(rhs, "dp", 1)], axis=0)
        return lhs_all, rhs_all
    return mine, other, rhs


def rows_product(cols, rhs):
    return product_lead(cols.reshape(cols.shape[0], -1), rhs).astype(bf16)


def split_bit(array, axis, size, bit):
    shape = array.shape
    return array.reshape(shape[:axis] + (size // (2 * bit), 2, bit) + shape[axis + 1 :])


def halve_cols(cols, bit, groups):
    view = split_bit(cols, 1, groups, bit)
    mine = bit_of("dp", 2 * bit)
    flat = lambda a: a.reshape((a.shape[0], groups // 2) + cols.shape[2:])
    return flat(pick(view, 2, mine)), flat(pick(view, 2, 1 - mine))


def add_pair(keep, other, dtype=bf16):
    return (keep.astype(f32) + other.astype(f32)).astype(dtype)


def remaining_position(done, bit):
    return bit >> sum(1 for d in done if d < bit)


def scatter_job(job, rows):
    groups = lax.axis_size("dp") // 2
    seq = lax.axis_size("seq")
    bits = [b // 2 for b in group_bits()]
    halves = []
    shared = len(job) == 2
    rhs = job[-1]
    width = rhs.shape[1] // 2
    for half in range(2):
        order = bits if half == 0 else bits[::-1]
        part = rhs[:, half * width : (half + 1) * width]
        if shared:
            first, rest = order[0], order[1:]
            mine, other = halve_cols(job[0], first, groups)
            got = swap(rows_product(other, part), "dp", 2 * first)
            keep = rows_product(mine, part)
            done = [first]
        else:
            got = swap(rows_product(job[1], part), "dp", 1)
            keep = rows_product(job[0], part)
            rest, done = order, []
        size = groups >> len(done)
        keep, got = (a.reshape(size, -1, width) for a in (keep, got))
        for bit in rest:
            place = remaining_position(done, bit)
            view_keep = split_bit(keep, 0, size, place)
            view_got = split_bit(got, 0, size, place)
            mine = bit_of("dp", 2 * bit)
            send = add_pair(pick(view_keep, 1, 1 - mine), pick(view_got, 1, 1 - mine))
            keep = add_pair(pick(view_keep, 1, mine), pick(view_got, 1, mine))
            size //= 2
            got = swap(send, "dp", 2 * bit).reshape(size, -1, width)
            keep = keep.reshape(size, -1, width)
            done.append(bit)
        halves.append((keep.reshape(seq, rows, width), got.reshape(seq, rows, width)))
    keep = got = None
    size = seq
    done = []
    for bit in axis_bits("seq"):
        place = remaining_position(done, bit)
        mine = bit_of("seq", bit)

        def side(which):
            if keep is None:
                return jnp.concatenate(
                    [
                        add_pair(
                            pick(split_bit(a, 0, size, place), 1, which),
                            pick(split_bit(b, 0, size, place), 1, which),
                        )
                        for a, b in halves
                    ],
                    axis=-1,
                )
            return add_pair(
                pick(split_bit(keep, 0, size, place), 1, which),
                pick(split_bit(got, 0, size, place), 1, which),
            )

        send, kept = side(1 - mine), side(mine)
        size //= 2
        got = swap(send, "seq", bit).reshape(size, rows, -1)
        keep = kept.reshape(size, rows, -1)
        done.append(bit)
    return add_pair(keep[0], got[0], f32)


def in_steps(model_width):
    return lax.axis_size("dp") == 8 and lax.axis_size("seq") == 4 and model_width == 1024


BLOCK = 512


def terms_of(refs, pairs, half, rows, blocks, seq):
    own, got = (jnp.concatenate([refs[2 * i][...], refs[2 * i + 1][...]], axis=1) for i in (0, 1))
    rhs = refs[4:]
    if pairs:
        rhs = rhs[2 * half : 2 * half + 2]
    total = product_lead(own, rhs[0][...]) + product_lead(got, rhs[1][...])
    for block in range(2):
        for z in range(seq):
            for j in range(blocks):
                start = (block * seq + z) * rows
                yield block, z, j, total[start : start + rows, j * BLOCK : (j + 1) * BLOCK]


def job_refs(refs, shape):
    at = start = 0
    for rows, blocks, pairs in shape:
        count = 8 if pairs else 6
        yield refs[at : at + count], pairs, rows, blocks, start
        at += count
        start += rows * blocks


def send_kernel(shape, seq, table_ref, *refs):
    del table_ref
    outs = refs[-2:]
    for half in range(2):

        @pl.when(pl.program_id(0) == half)
        def _():
            for part, pairs, rows, blocks, start in job_refs(refs, shape):
                for block, z, j, piece in terms_of(part, pairs, half, rows, blocks, seq):
                    at = start + j * rows
                    outs[half][block, z, at : at + rows, :] = piece.astype(bf16)


def fold_kernel(shape, seq, table_ref, *refs):
    del table_ref
    gots, (sends, keep) = refs[-7:-3], (refs[-3:-1], refs[-1])
    for half in range(2):

        @pl.when(pl.program_id(0) == half)
        def _():
            for part, pairs, rows, blocks, start in job_refs(refs, shape):
                for block, z, j, piece in terms_of(part, pairs, half, rows, blocks, seq):
                    at = slice(start + j * rows, start + (j + 1) * rows)
                    piece = (piece + gots[2 * half + block][0, z, at, :].astype(f32)).astype(bf16)
                    if block == 0:
                        sends[half][z, at, :] = piece
                    else:
                        keep[0, z, at, :] = piece


def split_kernel(bits, bit_ref, keep_ref, *refs):
    gots, (send_ref, left_ref) = refs[:-2], refs[-2:]
    mine = bit_ref[0]
    for half in range(2):
        for entry in range(send_ref.shape[1]):
            for ref, side in ((send_ref, 1 - mine), (left_ref, mine)):
                at = 2 * entry + side if bits == 2 else side
                if len(gots) == 2:
                    got = gots[half][at]
                else:
                    got = gots[0][half, at]
                total = keep_ref[half, at].astype(f32) + got.astype(f32)
                ref[half, entry] = total.astype(bf16)


def finish_kernel(shape, keep_ref, got_ref, *outs):
    start = 0
    for out, (rows, blocks, _) in zip(outs, shape):
        for half in range(2):
            for j in range(blocks):
                at = slice(start + j * rows, start + (j + 1) * rows)
                columns = slice((half * blocks + j) * BLOCK, (half * blocks + j + 1) * BLOCK)
                out[:, columns] = keep_ref[half, 0, at, :].astype(f32) + got_ref[
                    half, 0, at, :
                ].astype(f32)
        start += rows * blocks


LIMIT = pltpu.CompilerParams(vmem_limit_bytes=56 << 20)


def whole_call(kernel, name, bits, inputs, outs):
    spec = lambda x: pl.BlockSpec(x.shape, lambda i, *t: (0,) * len(x.shape))
    size = sum(x.size * x.dtype.itemsize for x in list(inputs) + list(outs))
    return pl.pallas_call(
        kernel,
        grid_spec=pltpu.PrefetchScalarGridSpec(
            num_scalar_prefetch=len(bits),
            grid=(1,),
            in_specs=[spec(x) for x in inputs],
            out_specs=[spec(o) for o in outs],
        ),
        out_shape=outs,
        compiler_params=LIMIT,
        cost_estimate=pl.CostEstimate(flops=1024, transcendentals=0, bytes_accessed=1024),
        name=name,
    )(*bits, *inputs)


class SmallScatter:
    def __init__(self, values):
        self.keep = values
        self.bits = [("dp", b) for b in axis_bits("dp")[::-1]]
        self.bits += [("seq", b) for b in axis_bits("seq")[::-1]]
        self.got = None

    def step(self):
        if self.got is not None:
            self.keep = self.keep + self.got
        if not self.bits:
            return
        axis, bit = self.bits.pop(0)
        view = self.keep.reshape((2, self.keep.shape[0] // 2) + self.keep.shape[1:])
        mine = bit_of(axis, bit)
        self.keep, sent = pick(view, 0, mine), pick(view, 0, 1 - mine)
        self.got = swap(sent, axis, bit)


class ModuleScatter:
    def __init__(self, jobs, name):
        self.jobs = jobs
        self.name = name
        self.shape = tuple((j[4], j[5] // BLOCK, j[3][0] is not j[3][1]) for j in jobs)
        self.rows = sum(rows * blocks for rows, blocks, _ in self.shape)

    def share(self):
        self.others = {}
        for lhs, rhs in ((j[0], j[3]) for j in self.jobs):
            for array in (lhs, *rhs):
                if id(array) not in self.others:
                    self.others[id(array)] = swap(array, "dp", 1)

    def operands(self):
        specs, args = [], []
        for lhs, _, tokens, rhs, rows, width in self.jobs:
            wide = 4 * rows
            for array in (lhs, self.others[id(lhs)]):
                for block in range(2):
                    spec = lambda h, t, block=block: (0, t[h, block])
                    specs.append(pl.BlockSpec((tokens, wide), spec))
                    args.append(array)
            if rhs[0] is rhs[1]:
                for array in (rhs[0], self.others[id(rhs[0])]):
                    specs.append(pl.BlockSpec((tokens, width), lambda h, t: (0, h)))
                    args.append(array)
            else:
                for half in rhs:
                    for array in (half, self.others[id(half)]):
                        specs.append(pl.BlockSpec((tokens, width), lambda h, t: (0, 0)))
                        args.append(array)
        return specs, args

    def call(self, kernel, name, table, more, more_specs, outs, out_specs):
        specs, args = self.operands()
        flops = sum(16 * j[2] * 4 * j[4] * j[5] for j in self.jobs)
        moved = sum(4 * j[2] * (4 * j[4] * 2 + 2 * j[5]) for j in self.jobs)
        moved += 2 * sum(x.size for x in list(more) + list(outs))
        return pl.pallas_call(
            functools.partial(kernel, self.shape, 4),
            grid_spec=pltpu.PrefetchScalarGridSpec(
                num_scalar_prefetch=1,
                grid=(2,),
                in_specs=specs + more_specs,
                out_specs=out_specs,
            ),
            out_shape=outs,
            compiler_params=LIMIT,
            cost_estimate=pl.CostEstimate(flops=1024, transcendentals=0, bytes_accessed=1024),
            name=self.name + name,
        )(table, *args, *more)

    def first_send(self):
        core, x, y = (bit_of("dp", b) for b in (1, 2, 4))
        table = [
            [core + 2 * (1 - x) + 4 * i for i in range(2)],
            [core + 2 * i + 4 * (1 - y) for i in range(2)],
        ]
        table = jnp.stack([jnp.stack(row) for row in table]).astype(jnp.int32)
        out = jax.ShapeDtypeStruct((2, 4, self.rows, BLOCK), bf16)
        spec = pl.BlockSpec(out.shape, lambda h, t: (0, 0, 0, 0))
        self.sends = self.call(send_kernel, "_send", table, [], [], [out, out], [spec, spec])

    def first_swap(self):
        self.got = [swap(s, "dp", b) for s, b in zip(self.sends, (2, 4))]
        self.sends = None

    def second_send(self):
        core, x, y = (bit_of("dp", b) for b in (1, 2, 4))
        table = [
            [core + 2 * x + 4 * side for side in (1 - y, y)] + [1 - y, y],
            [core + 2 * side + 4 * y for side in (1 - x, x)] + [1 - x, x],
        ]
        table = jnp.stack([jnp.stack(row) for row in table]).astype(jnp.int32)
        piece = (4, self.rows, BLOCK)
        more, more_specs = [], []
        for half in range(2):
            for block in range(2):
                spec = lambda h, t, half=half, block=block: (t[half, 2 + block], 0, 0, 0)
                more.append(self.got[half])
                more_specs.append(pl.BlockSpec((1,) + piece, spec))
        outs = [jax.ShapeDtypeStruct(s, bf16) for s in (piece, piece, (2,) + piece)]
        spec = pl.BlockSpec(piece, lambda h, t: (0, 0, 0))
        keep_spec = pl.BlockSpec((1,) + piece, lambda h, t: (h, 0, 0, 0))
        *self.sends, self.keep = self.call(
            fold_kernel, "_fold", table, more, more_specs, outs, [spec, spec, keep_spec]
        )
        self.got = None

    def second_swap(self):
        self.got = [swap(s, "dp", b) for s, b in zip(self.sends, (4, 2))]
        self.sends = None

    def z_send(self, bit):
        entries = 2 if bit == 1 else 1
        out = jax.ShapeDtypeStruct((2, entries, self.rows, BLOCK), bf16)
        gots = self.got if bit == 1 else [self.got]
        mine = bit_of("seq", bit)[None].astype(jnp.int32)
        self.sends, self.keep = whole_call(
            functools.partial(split_kernel, entries),
            f"{self.name}_z{bit}",
            [mine],
            [self.keep, *gots],
            [out, out],
        )
        self.got = None

    def z_swap(self, bit):
        self.got = swap(self.sends, "seq", bit)
        self.sends = None

    def finish(self):
        outs = [jax.ShapeDtypeStruct((j[4], 2 * j[5]), f32) for j in self.jobs]
        return whole_call(
            functools.partial(finish_kernel, self.shape),
            self.name + "_finish",
            [],
            [self.keep, self.got],
            outs,
        )


def scatter_module(jobs):
    outs = []
    for lhs, start, tokens, rhs, rows, columns in jobs:
        whole = rhs[0] if rhs[0] is rhs[1] else jnp.concatenate(rhs, axis=1)
        outs.append(scatter_job(grad_job(lhs[start : start + tokens], whole, True), rows))
    return outs


def one(rhs):
    return (rhs, rhs)


FIELDS = ("got", "keep", "sends")


def fence(things, *extras):
    fields = [{k: v for k, v in vars(t).items() if k in FIELDS} for t in things]
    fields, extras = lax.optimization_barrier((fields, extras))
    for thing, values in zip(things, fields):
        vars(thing).update(values)
    return extras


def fetch_weight(part):
    return lax.all_gather(part, ("dp", "seq"), axis=0, tiled=True)


def pack_kernel(*refs):
    shards, out = refs[:-1], refs[-1]
    width = out.shape[1]
    at = 0
    for shard in shards:
        rows = shard.shape[0]
        for j in range(shard.shape[1] // width):
            out[at : at + rows, :] = shard[:, j * width : (j + 1) * width]
            at += rows


def pack(shards, name):
    width = shards[-1].shape[1]
    rows = sum(s.shape[0] * s.shape[1] // width for s in shards)
    out = jax.ShapeDtypeStruct((rows, width), bf16)
    return whole_call(pack_kernel, name, [], shards, [out])[0]


def gather_packed(part):
    return lax.all_gather(part, ("dp", "seq"), axis=0)


def packed_block(packed, start, rows):
    return packed[:, start : start + rows].reshape(-1, packed.shape[2])


def up_kernel(normed_ref, weight_ref, active_ref, slope_ref):
    width = normed_ref.shape[1]
    for half in range(2):
        columns = slice(half * width // 2, (half + 1) * width // 2)
        block = weight_ref[:, :, columns].reshape(width, width // 2)
        hidden = product(normed_ref[...], block)
        sigmoid = 1.0 / (1.0 + jnp.exp(-hidden))
        active_ref[:, columns] = (hidden * sigmoid).astype(bf16)
        slope_ref[:, columns] = (sigmoid * (1.0 + hidden * (1.0 - sigmoid))).astype(bf16)


def up_back_kernel(grad_ref, weight_ref, out_ref):
    width = out_ref.shape[1]
    part = product_tail(grad_ref[...], weight_ref[...].reshape(width, -1))
    out_ref[...] = jnp.where(pl.program_id(0) == 0, part, out_ref[...] + part)


def down_kernel(values_ref, active_ref, weight_ref, out_ref, total_ref):
    width = out_ref.shape[1]
    part = product(active_ref[...], weight_ref[...].reshape(-1, width))
    total_ref[...] = jnp.where(pl.program_id(0) == 0, part, total_ref[...] + part)

    @pl.when(pl.program_id(0) == pl.num_programs(0) - 1)
    def _():
        out_ref[...] = values_ref[...] + 0.5 * total_ref[...]


def down_back_kernel(branch_ref, slope_ref, weight_ref, out_ref):
    width = branch_ref.shape[1]
    part = product_tail(branch_ref[...], weight_ref[...].reshape(-1, width))
    out_ref[...] = (part * slope_ref[...].astype(f32)).astype(bf16)


def ffn_call(kernel, name, packed, part, inputs, outs, scratch=()):
    owners, _, width = packed.shape
    steps = 4
    rows = width // owners
    if part == "up":
        weight = pl.BlockSpec((owners, rows, width), lambda i: (0, i, 0))
    else:
        weight = pl.BlockSpec((owners // steps, rows * steps, width), lambda i: (i, 1, 0))

    def spec(x):
        tokens, columns = x.shape
        return pl.BlockSpec((tokens, min(width, columns)), (lambda i: (0, i)) if columns > width else (lambda i: (0, 0)))

    numbers = lambda things: sum(t.size * t.dtype.itemsize for t in things)
    tokens = inputs[0].shape[0]
    inner = steps * width
    return pl.pallas_call(
        kernel,
        grid=(steps,),
        in_specs=[spec(x) for x in inputs] + [weight],
        out_specs=[spec(o) for o in outs],
        out_shape=outs,
        scratch_shapes=list(scratch),
        compiler_params=pltpu.CompilerParams(vmem_limit_bytes=56 << 20),
        cost_estimate=pl.CostEstimate(flops=1024, transcendentals=0, bytes_accessed=1024),
        name=name,
    )(*inputs, packed)


class Packed:
    def __init__(self, array):
        self.array = array


def ffn_up(normed, packed, name):
    tokens, width = normed.shape
    out = jax.ShapeDtypeStruct((tokens, 4 * width), bf16)
    return ffn_call(up_kernel, name, packed.array, "up", [normed], [out, out])


def ffn_up_back(grad_hidden, packed, name):
    out = jax.ShapeDtypeStruct((grad_hidden.shape[0], packed.array.shape[2]), f32)
    return ffn_call(up_back_kernel, name, packed.array, "up", [grad_hidden], [out])[0]


def ffn_down(values, active, packed, name):
    out = jax.ShapeDtypeStruct(values.shape, f32)
    scratch = [pltpu.VMEM(values.shape, f32)]
    return ffn_call(down_kernel, name, packed.array, "down", [values, active], [out], scratch)[0]


def ffn_down_back(branch, slope, packed, name):
    out = jax.ShapeDtypeStruct(slope.shape, bf16)
    return ffn_call(down_back_kernel, name, packed.array, "down", [branch, slope], [out])[0]


def gather_line(own):
    seq = lax.axis_size("seq")
    ups, downs = [own], [own]
    for step in range(seq - 1):
        ups.append(lax.ppermute(ups[-1], "seq", [(i, i + 1) for i in range(seq - 1)]))
        downs.append(lax.ppermute(downs[-1], "seq", [(i + 1, i) for i in range(seq - 1)]))
    me = lax.axis_index("seq")
    blocks = [own]
    for r in range(1, seq):
        blocks.append(jnp.where(me + r < seq, downs[r], ups[seq - r]))
    return jnp.stack(blocks)


def scatter_line(blocks, between=()):
    seq = lax.axis_size("seq")
    up = down = None
    between = iter(between)
    for step in range(seq - 1, 0, -1):
        message_up, message_down = blocks[step], blocks[seq - step]
        if up is not None:
            message_up = add_pair(message_up, up)
            message_down = add_pair(message_down, down)
        up = lax.ppermute(message_up, "seq", [(i, i + 1) for i in range(seq - 1)])
        down = lax.ppermute(message_down, "seq", [(i + 1, i) for i in range(seq - 1)])
        meanwhile = next(between, None)
        if meanwhile is not None:
            up, down = meanwhile(up, down)
    if up is None:
        up = down = jnp.zeros_like(blocks[0])
    return blocks[0], up, down


def sum_parts(parts):
    return sum(part.astype(f32) for part in parts)


def with_halo(shard, width):
    size, length = lax.axis_size("seq"), shard.shape[0]
    up = [(i, i + 1) for i in range(size - 1)]
    down = [(i + 1, i) for i in range(size - 1)]
    before = lax.ppermute(shard[length - width :], "seq", up)
    after = lax.ppermute(shard[:width], "seq", down)
    return jnp.concatenate([before, shard, after], axis=0)


def norm_forward(values, norm_gain):
    centered = values - jnp.mean(values, axis=-1, keepdims=True)
    inverse = lax.rsqrt(jnp.mean(centered * centered, axis=-1, keepdims=True) + epsilon)
    normal = centered * inverse
    return (normal * norm_gain, normal, inverse)


def norm_backward(grad_out, norm_gain, normal, inverse):
    scaled = grad_out * norm_gain
    grad_in = inverse * (
        scaled
        - jnp.mean(scaled, axis=-1, keepdims=True)
        - normal * jnp.mean(scaled * normal, axis=-1, keepdims=True)
    )
    return (grad_in, jnp.sum(grad_out * normal, axis=0))


def silu_slope(hidden):
    sigmoid_rows = jax.nn.sigmoid(hidden)
    return sigmoid_rows * (1.0 + hidden * (1.0 - sigmoid_rows))


def ffn_forward(values, norm_gain, upward, downward, name):
    normed, normal, inverse = norm_forward(values, norm_gain)
    normed_low = normed.astype(bf16)
    if isinstance(upward, Packed):
        active, slope = ffn_up(normed_low, upward, name + "_up")
        out = ffn_down(values, active, downward, name + "_down")
    else:
        hidden = product(normed_low, upward)
        active, slope = jax.nn.silu(hidden).astype(bf16), silu_slope(hidden)
        out = values + 0.5 * product(active, downward)
    return out, (normed_low, normal, inverse, slope, active)


def owner_rows(rows):
    return rows // (lax.axis_size("dp") * lax.axis_size("seq"))


def ffn_hidden_grad(grad_branch, downward, stored, name):
    if isinstance(downward, Packed):
        return ffn_down_back(grad_branch, stored[3], downward, name + "_down_back")
    return (product_tail(grad_branch, downward) * stored[3]).astype(bf16)


def ffn_input_grad(grad_rows, grad_hidden, norm_gain, upward, stored, name):
    if isinstance(upward, Packed):
        grad_normed = ffn_up_back(grad_hidden, upward, name + "_up_back")
    else:
        grad_normed = product_tail(grad_hidden, upward)
    grad_in, grad_gain = norm_backward(grad_normed, norm_gain, stored[1], stored[2])
    return grad_rows + grad_in, grad_gain


def ffn_jobs(grad_branch, grad_hidden, stored):
    normed_low, active = stored[0], stored[4]
    tokens, width = normed_low.shape
    inner = active.shape[1]
    return [
        (normed_low, 0, tokens, one(grad_hidden), owner_rows(width), inner // 2),
        (active, 0, tokens, one(grad_branch), owner_rows(inner), width // 2),
    ]


def norm_back(grad, norm_gain, values):
    centered = values - jnp.mean(values, axis=-1, keepdims=True)
    inverse = lax.rsqrt(jnp.mean(centered * centered, axis=-1, keepdims=True) + epsilon)
    normal = centered * inverse
    scaled = grad * norm_gain
    grad_in = inverse * (
        scaled
        - jnp.mean(scaled, axis=-1, keepdims=True)
        - normal * jnp.mean(scaled * normal, axis=-1, keepdims=True)
    )
    return grad_in, jnp.sum(grad * normal, axis=0, keepdims=True)


def valid_mask(count_ref, shape):
    return (lax.broadcasted_iota(jnp.int32, (shape[0], 1), 0) < count_ref[0]).astype(f32)


class Block:
    def __init__(self, packed, index):
        self.packed, self.index = packed, index

    def spec(self):
        owners, _, width = self.packed.shape
        index = self.index
        return pl.BlockSpec((owners, width // owners, width), lambda i, *t: (0, index, 0))


def step_call(kernel, name, scalars, inputs, outs, scratch=()):
    def spec(x):
        if isinstance(x, Block):
            return x.spec()
        return pl.BlockSpec(x.shape, lambda i, *t: (0,) * len(x.shape))

    return pl.pallas_call(
        kernel,
        grid_spec=pltpu.PrefetchScalarGridSpec(
            num_scalar_prefetch=len(scalars),
            grid=(1,),
            in_specs=[spec(x) for x in inputs],
            out_specs=[spec(o) for o in outs],
            scratch_shapes=list(scratch),
        ),
        out_shape=outs,
        compiler_params=LIMIT,
        cost_estimate=pl.CostEstimate(flops=1024, transcendentals=0, bytes_accessed=1024),
        name=name,
    )(*scalars, *[x.packed if isinstance(x, Block) else x for x in inputs])


def rows_like(array, dtype=f32):
    return jax.ShapeDtypeStruct(array.shape, dtype)


def vector_like(array, count=1):
    return jax.ShapeDtypeStruct((count, array.shape[1]), f32)


def square(ref):
    return ref[...].reshape(ref.shape[2], ref.shape[2])


def final_back_kernel(count_ref, cotangent_ref, values_ref, gain_ref, grad_ref, sum_ref, branch_ref):
    grad = cotangent_ref[...].astype(f32) * valid_mask(count_ref, values_ref.shape)
    grad, sum_ref[...] = norm_back(grad, gain_ref[...], values_ref[...])
    grad_ref[...] = grad
    branch_ref[...] = (0.5 * grad).astype(bf16)


def shaped_back_kernel(
    count_ref, branch_ref, depth_ref, vectors_ref, weight_ref, grad_ref, sums_ref
):
    normal = (depth_ref[...] - vectors_ref[0:1]) * vectors_ref[1:2]
    shaped = normal * vectors_ref[2:3] + vectors_ref[3:4]
    sigmoid = 1.0 / (1.0 + jnp.exp(-shaped))
    slope = sigmoid * (1.0 + shaped * (1.0 - sigmoid)) * valid_mask(count_ref, depth_ref.shape)
    grad = product_tail(branch_ref[...], square(weight_ref)) * slope
    grad_ref[...] = grad
    sums_ref[0:1] = jnp.sum(grad, axis=0, keepdims=True)
    sums_ref[1:2] = jnp.sum(grad * normal, axis=0, keepdims=True)


def add_kernel(left_ref, right_ref, out_ref):
    out_ref[...] = left_ref[...] + right_ref[...]


def depth_back_kernel(
    count_ref, grad_ref, depth_ref, vectors_ref, totals_ref, out_ref, top_ref, bottom_ref
):
    normal = (depth_ref[...] - vectors_ref[0:1]) * vectors_ref[1:2]
    scale = vectors_ref[2:3]
    out = (
        vectors_ref[1:2]
        * valid_mask(count_ref, depth_ref.shape)
        * (
            grad_ref[...] * scale
            - scale * (totals_ref[0:1] + normal * totals_ref[1:2]) / vectors_ref[4:5]
        )
    ).astype(bf16)
    out_ref[...] = out
    width = top_ref.shape[0]
    top_ref[...] = out[:width]
    bottom_ref[...] = out[out.shape[0] - width :]


def taps_back_kernel(
    count_ref, before_ref, grad_ref, after_ref, taps_ref, paired_ref, sigmoid_ref, *refs
):
    left_ref, right_ref, rims = refs
    frames = grad_ref.shape[0]
    taps = taps_ref.shape[0]
    half = taps // 2
    rims[0:half] = before_ref[...].astype(f32)
    rims[half : half + frames] = grad_ref[...].astype(f32)
    rims[half + frames : 2 * half + frames] = after_ref[...].astype(f32)
    valid = valid_mask(count_ref, grad_ref.shape)

    def part(step, carry):
        lanes = pl.ds(pl.multiple_of(step * 128, 128), 128)
        total = jnp.zeros((frames, 128), f32)
        for tap in range(taps):
            start = 2 * half - tap
            total = total + rims[start : start + frames, lanes] * taps_ref[tap : tap + 1, lanes]
        sigmoid = sigmoid_ref[:, lanes]
        left = total * sigmoid * valid
        left_ref[:, lanes] = left.astype(bf16)
        right_ref[:, lanes] = (left * paired_ref[:, lanes] * (1.0 - sigmoid)).astype(bf16)
        return carry

    lax.fori_loop(0, grad_ref.shape[1] // 128, part, 0)


def taps_sums_kernel(grad_ref, widened_ref, sums_ref, wide_rows, own_rows):
    frames = grad_ref.shape[0]
    wide_rows[0 : widened_ref.shape[0]] = widened_ref[...].astype(f32)
    own_rows[...] = grad_ref[...].astype(f32)

    def part(step, carry):
        lanes = pl.ds(pl.multiple_of(step * 128, 128), 128)
        own = own_rows[:, lanes]
        for tap in range(sums_ref.shape[0]):
            sums_ref[tap : tap + 1, lanes] = jnp.sum(
                wide_rows[tap : tap + frames, lanes] * own, axis=0, keepdims=True
            )
        return carry

    lax.fori_loop(0, grad_ref.shape[1] // 128, part, 0)


def conv_input_kernel(
    left_ref, right_ref, values_ref, gain_ref, rows_ref, first_ref, second_ref, *outs
):
    grad = product_tail(left_ref[...], square(first_ref))
    grad = grad + product_tail(right_ref[...], square(second_ref))
    finish_input(grad, gain_ref, values_ref, rows_ref, 1.0, *outs)


def finish_input(grad, gain_ref, values_ref, rows_ref, factor, out_ref, sum_ref, branch_ref):
    grad, sum_ref[...] = norm_back(grad, gain_ref[...], values_ref[...])
    grad = rows_ref[...] + grad
    out_ref[...] = grad
    branch_ref[...] = (factor * grad).astype(bf16)


def attend_input_kernel(
    own_ref, up_ref, down_ref, query_ref, values_ref, gain_ref, rows_ref, weight_ref, *outs
):
    grad = own_ref[...].astype(f32) + up_ref[...].astype(f32) + down_ref[...].astype(f32)
    grad = grad + product_tail(query_ref[...], square(weight_ref))
    finish_input(grad, gain_ref, values_ref, rows_ref, 0.5, *outs)


def input_outs(rows):
    return [rows_like(rows), vector_like(rows), rows_like(rows, bf16)]


def blocks_back_kernel(key_ref, value_ref, key_weight_ref, value_weight_ref, out_ref):
    total = product_tail(key_ref[...], square(key_weight_ref))
    total = total + product_tail(value_ref[...], square(value_weight_ref))
    out_ref[0] = total.astype(bf16)


def blocks_back(grad_key, grad_value, packed, frames):
    keys, width = grad_key.shape
    rows = pl.BlockSpec((frames, width), lambda i: (i, 0))
    return pl.pallas_call(
        blocks_back_kernel,
        grid=(keys // frames,),
        in_specs=[rows, rows, Block(packed, 1).spec(), Block(packed, 2).spec()],
        out_specs=pl.BlockSpec((1, frames, width), lambda i: (i, 0, 0)),
        out_shape=jax.ShapeDtypeStruct((keys // frames, frames, width), bf16),
        compiler_params=LIMIT,
        cost_estimate=pl.CostEstimate(flops=1024, transcendentals=0, bytes_accessed=1024),
        name="attend_blocks_back",
    )(grad_key, grad_value, packed, packed)


def up_back_input_kernel(
    factor, grad_ref, values_ref, gain_ref, rows_ref, weight_ref, out_ref, sum_ref, branch_ref, total
):
    part = product_tail(grad_ref[...], weight_ref[...].reshape(out_ref.shape[1], -1))
    total[...] = jnp.where(pl.program_id(0) == 0, part, total[...] + part)

    @pl.when(pl.program_id(0) == pl.num_programs(0) - 1)
    def _():
        finish_input(
            total[...], gain_ref, values_ref, rows_ref, factor, out_ref, sum_ref, branch_ref
        )


def ffn_up_back_input(grad_hidden, values, gain, rows, packed, factor, name):
    kernel = functools.partial(up_back_input_kernel, factor)
    scratch = [pltpu.VMEM(rows.shape, f32)]
    inputs = [grad_hidden, values, gain, rows]
    return ffn_call(kernel, name, packed.array, "up", inputs, input_outs(rows), scratch)


def sum_in_steps(values, bits):
    for axis, bit in bits:
        (values,) = step_call(
            add_kernel, "add", [], [values, swap(values, axis, bit)], [rows_like(values)]
        )
    return values


def key_valid(offsets_ref, rows, keys):
    count = keys // rows
    spots = []
    for block in range(count):
        spots.append(offsets_ref[block] + lax.broadcasted_iota(jnp.int32, (rows, 1), 0))
    return jnp.concatenate(spots, axis=0) < offsets_ref[count]


def head_mask(block, head):
    lanes = lax.broadcasted_iota(jnp.int32, block.shape, 1)
    inside = (lanes < HEAD_DIM) if head == 0 else (lanes >= HEAD_DIM)
    return jnp.where(inside, block, jnp.zeros_like(block))


def attend_kernel(rows, offsets_ref, query_ref, key_ref, value_ref, mixture_ref, total_ref):
    keys = key_ref[...]
    values = value_ref[...]
    query = query_ref[...] * jnp.asarray(HEAD_DIM**-0.5, bf16)
    valid = key_valid(offsets_ref, rows, keys.shape[0])
    halves = []
    for head in range(2):
        scores = product_tail(keys, head_mask(query, head))
        scores = jnp.where(valid, scores, -1e30)
        largest = jnp.max(scores, axis=0, keepdims=True)
        exponent = jnp.exp(scores - largest)
        totals = jnp.sum(exponent, axis=0, keepdims=True)
        weights = (exponent * (1.0 / totals)).astype(bf16)
        mixed = product_lead(values, weights)
        halves.append(mixed[head * HEAD_DIM : (head + 1) * HEAD_DIM])
        total_ref[0, head : head + 1, :] = largest + jnp.log(totals)
    mixture_ref[...] = jnp.concatenate(halves, axis=0).T.astype(bf16)


def attend_back_kernel(
    rows,
    offsets_ref,
    query_ref,
    key_ref,
    value_ref,
    total_ref,
    grad_ref,
    *refs,
):
    outward, (query_grad_ref, key_grad_ref, value_grad_ref) = refs[:-3], refs[-3:]
    keys = key_ref[...]
    values = value_ref[...]
    grad = grad_ref[...]
    if outward:
        grad = product_tail(grad, outward[0][...].reshape(128, -1)).astype(bf16)
    query = query_ref[...] * jnp.asarray(HEAD_DIM**-0.5, bf16)
    valid = key_valid(offsets_ref, rows, keys.shape[0])
    halves = []
    key_grad = value_grad = None
    for head in range(2):
        query_head = head_mask(query, head)
        grad_head = head_mask(grad, head)
        scores = product_tail(keys, query_head)
        scores = jnp.where(valid, scores, -1e30)
        weights = jnp.exp(scores - total_ref[0, head : head + 1, :])
        grad_weights = product_tail(values, grad_head)
        inner = jnp.sum(weights * grad_weights, axis=0, keepdims=True)
        grad_scores = (weights * (grad_weights - inner)).astype(bf16)
        key_part = product(grad_scores, query_head)
        value_part = product(weights.astype(bf16), grad_head)
        key_grad = key_part if key_grad is None else key_grad + key_part
        value_grad = value_part if value_grad is None else value_grad + value_part
        query_part = product_lead(keys, grad_scores)
        halves.append(query_part[head * HEAD_DIM : (head + 1) * HEAD_DIM])
    query_grad = jnp.concatenate(halves, axis=0).T * HEAD_DIM**-0.5
    query_grad_ref[...] = query_grad.astype(bf16)
    key_grad_ref[...] = key_grad.astype(bf16)
    value_grad_ref[...] = value_grad.astype(bf16)


def attend(offsets, query, key, value):
    rows, width = query.shape
    keys = key.shape[0]
    pairs = width // 128
    return pl.pallas_call(
        functools.partial(attend_kernel, rows),
        grid_spec=pltpu.PrefetchScalarGridSpec(
            num_scalar_prefetch=1,
            grid=(pairs,),
            in_specs=[
                pl.BlockSpec((rows, 128), lambda i, o: (0, i)),
                pl.BlockSpec((keys, 128), lambda i, o: (0, i)),
                pl.BlockSpec((keys, 128), lambda i, o: (0, i)),
            ],
            out_specs=[
                pl.BlockSpec((rows, 128), lambda i, o: (0, i)),
                pl.BlockSpec((1, 2, rows), lambda i, o: (i, 0, 0)),
            ],
        ),
        out_shape=[
            jax.ShapeDtypeStruct((rows, width), bf16),
            jax.ShapeDtypeStruct((pairs, 2, rows), f32),
        ],
        compiler_params=pltpu.CompilerParams(vmem_limit_bytes=48 << 20),
        name="attend",
    )(offsets, query, key, value)


def attend_back(offsets, query, key_value, totals, grad, packed=None):
    rows, width = query.shape
    key, value = key_value
    keys = key.shape[0]
    pairs = width // 128
    row_spec = pl.BlockSpec((rows, 128), lambda i, o: (0, i))
    key_spec = pl.BlockSpec((keys, 128), lambda i, o: (0, i))
    if packed is None:
        grad_specs, more = [row_spec], []
    else:
        owners = packed.shape[0]
        count = 128 * owners // width
        square_rows = pl.BlockSpec((count, width // owners, width), lambda i, o: (i, 3, 0))
        grad_specs, more = [pl.BlockSpec((rows, width), lambda i, o: (0, 0)), square_rows], [packed]
    return pl.pallas_call(
        functools.partial(attend_back_kernel, rows),
        grid_spec=pltpu.PrefetchScalarGridSpec(
            num_scalar_prefetch=1,
            grid=(pairs,),
            in_specs=[
                row_spec,
                key_spec,
                pl.BlockSpec((keys, 128), lambda i, o: (0, i)),
                pl.BlockSpec((1, 2, rows), lambda i, o: (i, 0, 0)),
            ]
            + grad_specs,
            out_specs=[row_spec, key_spec, key_spec],
        ),
        out_shape=[
            jax.ShapeDtypeStruct((rows, width), bf16),
            jax.ShapeDtypeStruct((keys, width), bf16),
            jax.ShapeDtypeStruct((keys, width), bf16),
        ],
        compiler_params=pltpu.CompilerParams(vmem_limit_bytes=48 << 20),
        name="attend_back",
    )(offsets, query, key, value, totals, grad, *more)


def attention_forward(values, length, norm_gain, joint_proj, attend_out, gathered):
    normed, normal, inverse = norm_forward(values, norm_gain)
    normed_low = normed.astype(bf16)
    frames, model_width = normed_low.shape
    seq = lax.axis_size("seq")
    normed_all = gathered(gather_line(normed_low)).reshape(seq * frames, model_width)
    query = product(normed_low, joint_proj[0]).astype(bf16)
    key = product(normed_all, joint_proj[1]).astype(bf16)
    value = product(normed_all, joint_proj[2]).astype(bf16)
    starts = ((lax.axis_index("seq") + jnp.arange(seq)) % seq) * frames
    offsets = jnp.concatenate([starts, length[None]]).astype(jnp.int32)
    mixed_low, totals = attend(offsets, query, key, value)
    output = values + product(mixed_low, attend_out)
    stored = (normed_low, normal, inverse, normed_all, query, (key, value), offsets, totals, mixed_low)
    return (output, stored)


def attention_parts_grad(grad_rows, attend_out, stored):
    normed_low, normal, inverse, normed_all, query, key_value, offsets, totals, mixed_low = stored
    grad_branch = grad_rows.astype(bf16)
    grad_mixed = product_tail(grad_branch, attend_out).astype(bf16)
    return (grad_branch,) + tuple(attend_back(offsets, query, key_value, totals, grad_mixed))


def attention_blocks_grad(grad_key, grad_value, joint_proj, frames):
    width = grad_key.shape[1]
    part = product_tail(grad_key, joint_proj[1]) + product_tail(grad_value, joint_proj[2])
    return part.astype(bf16).reshape(-1, frames, width)


def attention_input_grad(grad_rows, grad_normed, grad_query, norm_gain, joint_proj, stored):
    grad_normed = grad_normed + product_tail(grad_query, joint_proj[0])
    grad_in, grad_gain = norm_backward(grad_normed, norm_gain, stored[1], stored[2])
    return grad_rows + grad_in, grad_gain


def attention_jobs(grad_branch, grad_query, grad_key, grad_value, stored):
    normed_all, mixed_low = stored[3], stored[8]
    frames, width = grad_query.shape
    rows = owner_rows(width)
    return [
        (normed_all, 0, frames, one(grad_query), rows, width // 2),
        (normed_all, 0, normed_all.shape[0], (grad_key, grad_value), rows, width),
        (mixed_low, 0, frames, one(grad_branch), rows, width // 2),
    ]


def conv_forward(
    values, valid_rows, norm_gain, conv_pair, taps_float, batch_scale, batch_shift, conv_out
):
    normed, normal, inverse = norm_forward(values, norm_gain)
    normed_low = normed.astype(bf16)
    paired = product(normed_low, conv_pair[0])
    frames, model_width = paired.shape
    sigmoid_rows = jax.nn.sigmoid(product(normed_low, conv_pair[1]))
    gated_rows = (paired * sigmoid_rows * valid_rows).astype(bf16)
    half_width = taps_float.shape[1] // 2
    widened = with_halo(gated_rows, half_width)
    mixture = jnp.zeros((frames, model_width), f32)
    for offset in range(taps_float.shape[1]):
        mixture = mixture + widened[offset : offset + frames] * taps_float[:, offset]
    own_count = jnp.sum(valid_rows)
    own_mean = jnp.sum(mixture * valid_rows, axis=0) / jnp.maximum(own_count, 1.0)
    own_dev = (mixture - own_mean) * valid_rows
    frame_count, batch_mean, square = merge_moments(
        own_count, own_mean, jnp.sum(own_dev * own_dev, axis=0)
    )
    batch_var = square / frame_count
    inverse_std = lax.rsqrt(batch_var + epsilon)
    normal_batch = (mixture - batch_mean) * inverse_std
    shaped = normal_batch * batch_scale + batch_shift
    active = jax.nn.silu(shaped).astype(bf16)
    output = values + product(active, conv_out)
    stored = (
        normed_low,
        normal,
        inverse,
        paired,
        sigmoid_rows,
        widened,
        normal_batch,
        inverse_std,
        shaped,
        active,
        mixture,
    )
    return (output, stored, (batch_mean, batch_var, frame_count))


def conv_shaped_grad(grad_rows, valid_rows, conv_out, stored):
    normal_batch, shaped = stored[6], stored[8]
    grad_branch = grad_rows.astype(bf16)
    grad_shaped = product_tail(grad_branch, conv_out) * silu_slope(shaped) * valid_rows
    sums = jnp.stack([jnp.sum(grad_shaped, axis=0), jnp.sum(grad_shaped * normal_batch, axis=0)])
    return grad_branch, grad_shaped, sums


def conv_paired_grad(grad_shaped, totals, valid_rows, taps_float, scale_float, frame_count, stored):
    normal_batch, inverse_std = stored[6:8]
    total_shift, total_scale = totals
    grad_mixture = (
        inverse_std
        * valid_rows
        * (
            grad_shaped * scale_float
            - scale_float * (total_shift + normal_batch * total_scale) / frame_count
        )
    ).astype(bf16)
    grad_rims = with_halo(grad_mixture, taps_float.shape[1] // 2)
    return conv_taps_grad(grad_mixture, grad_rims, valid_rows, taps_float, stored)


def conv_taps_grad(grad_mixture, grad_rims, valid_rows, taps_float, stored):
    paired, sigmoid_rows, widened = stored[3:6]
    taps = taps_float.shape[1]
    half_width = taps // 2
    frames, model_width = grad_mixture.shape
    widened_float = widened.astype(f32)
    grad_float = grad_mixture.astype(f32)
    grad_gated = jnp.zeros((frames, model_width), f32)
    tap_grads = []
    for offset in range(taps):
        lower_edge = 2 * half_width - offset
        grad_gated = (
            grad_gated + grad_rims[lower_edge : lower_edge + frames] * taps_float[:, offset]
        )
        tap_grads.append(jnp.sum(widened_float[offset : offset + frames] * grad_float, axis=0))
    grad_left = grad_gated * sigmoid_rows * valid_rows
    grad_right = grad_gated * paired * sigmoid_rows * (1.0 - sigmoid_rows) * valid_rows
    return (grad_left.astype(bf16), grad_right.astype(bf16)), jnp.stack(tap_grads)


def conv_input_grad(grad_rows, grad_paired, norm_gain, conv_pair, stored):
    grad_normed = product_tail(grad_paired[0], conv_pair[0]) + product_tail(
        grad_paired[1], conv_pair[1]
    )
    grad_in, grad_gain = norm_backward(grad_normed, norm_gain, stored[1], stored[2])
    return grad_rows + grad_in, grad_gain


def conv_jobs(grad_branch, grad_paired, stored):
    normed_low, active = stored[0], stored[9]
    frames, width = normed_low.shape
    rows = owner_rows(width)
    return [
        (normed_low, 0, frames, grad_paired, rows, width),
        (active, 0, frames, one(grad_branch), rows, width // 2),
    ]


def per_device(
    inputs,
    lengths,
    token_mask,
    mask_vector,
    gain_first,
    first_up,
    first_down,
    gain_attend,
    joint_proj,
    attend_out,
    gain_conv,
    conv_pair,
    conv_taps,
    batch_scale,
    batch_shift,
    conv_out,
    gain_second,
    second_up,
    second_down,
    gain_final,
    cotangent,
):
    frames = inputs.shape[1]
    model_width = inputs.shape[2]
    taps = conv_taps.shape[1]
    length = lengths[0]
    positions = lax.axis_index("seq") * frames + jnp.arange(frames)
    valid_rows = (positions < length).astype(f32)[:, None]
    masked_float = (token_mask[0] > 0).astype(f32)[:, None]

    vectors = (
        mask_vector,
        gain_first,
        gain_attend,
        gain_conv,
        gain_second,
        gain_final,
        batch_scale,
        batch_shift,
    )
    own_small = jnp.concatenate([jnp.stack(vectors, axis=0), conv_taps.T], axis=0)
    count = own_small.shape[0]
    shards = lax.axis_size("dp") * lax.axis_size("seq")
    own_rows = model_width // shards
    small = gather_small(own_small[None])
    if in_steps(model_width):
        front = gather_packed(pack((first_up, first_down), "pack_first"))
        middle_part = pack((joint_proj, attend_out, conv_pair, conv_out), "pack_middle")
        back_part = pack((second_up, second_down), "pack_second")
        small, _, middle_part, back_part = tie(small, front, middle_part, back_part)
        middle = gather_packed(middle_part)
        up_one = down_one = Packed(front)
        squares = [packed_block(middle, i * own_rows, own_rows) for i in range(7)]
        joint_all, outward_all = squares[:3], squares[3]
        pair_all, conv_out_all = squares[4:6], squares[6]
    else:
        up_one, down_one, joint_all, outward_all, pair_all, conv_out_all = (
            fetch_weight(part)
            for part in (
                first_up,
                first_down,
                joint_proj,
                attend_out,
                conv_pair,
                conv_out,
            )
        )
        joint_all = jnp.split(joint_all, 3, axis=1)
        pair_all = jnp.split(pair_all, 2, axis=1)
    small = jnp.transpose(small, (1, 0, 2)).reshape(count, model_width).astype(f32)
    vector_mask, g_first, g_attend, g_conv, g_second, g_final, scale_float, shift_float = (
        small[i] for i in range(8)
    )
    taps_float = small[8:].T

    start_rows = jnp.where(masked_float > 0.0, vector_mask[None, :], inputs[0].astype(f32))
    rows_first, first_stored = ffn_forward(start_rows, g_first, up_one, down_one, "first")
    second_weights = []

    def gathered(rows):
        if not in_steps(model_width):
            second_weights.extend([fetch_weight(second_up), fetch_weight(second_down)])
            return rows
        rows, _, part = tie(rows, middle, back_part)
        back = Packed(gather_packed(part))
        second_weights.extend([back, back])
        return rows

    rows_second, attend_stored = attention_forward(
        rows_first, length, g_attend, joint_all, outward_all, gathered
    )
    up_two, down_two = second_weights
    rows_third, conv_stored, batch_stats = conv_forward(
        rows_second, valid_rows, g_conv, pair_all, taps_float, scale_float, shift_float, conv_out_all
    )
    rows_fourth, second_stored = ffn_forward(rows_third, g_second, up_two, down_two, "second")
    normed, normal, inverse = norm_forward(rows_fourth, g_final)
    output = (normed * valid_rows).astype(bf16)

    steps = in_steps(model_width)
    frame_count = batch_stats[2]
    if not steps:
        grad_rows, grad_final = norm_backward(
            cotangent[0].astype(f32) * valid_rows, g_final, normal, inverse
        )
        branch_two = (0.5 * grad_rows).astype(bf16)
        hidden_two = ffn_hidden_grad(branch_two, down_two, second_stored, "second")
        jobs_two = ffn_jobs(branch_two, hidden_two, second_stored)
        grad_rows, grad_gain_two = ffn_input_grad(
            grad_rows, hidden_two, g_second, up_two, second_stored, "second"
        )
        branch_conv, grad_shaped, sums = conv_shaped_grad(
            grad_rows, valid_rows, conv_out_all, conv_stored
        )
        totals = sum_small(sums)
        grad_paired, grad_taps = conv_paired_grad(
            grad_shaped, totals, valid_rows, taps_float, scale_float, frame_count, conv_stored
        )
        jobs_conv = conv_jobs(branch_conv, grad_paired, conv_stored)
        grad_rows, grad_gain_conv = conv_input_grad(
            grad_rows, grad_paired, g_conv, pair_all, conv_stored
        )
        branch_attend, grad_query, grad_key, grad_value = attention_parts_grad(
            grad_rows, outward_all, attend_stored
        )
        jobs_attend = attention_jobs(
            branch_attend, grad_query, grad_key, grad_value, attend_stored
        )
        blocks = attention_blocks_grad(grad_key, grad_value, joint_all, frames)
        grad_normed = sum_parts(scatter_line(blocks))
        grad_rows, grad_gain_attend = attention_input_grad(
            grad_rows, grad_normed, grad_query, g_attend, joint_all, attend_stored
        )
        branch_one = (0.5 * grad_rows).astype(bf16)
        hidden_one = ffn_hidden_grad(branch_one, down_one, first_stored, "first")
        jobs_one = ffn_jobs(branch_one, hidden_one, first_stored)
        grad_rows, grad_gain_one = ffn_input_grad(
            grad_rows, hidden_one, g_first, up_one, first_stored, "first"
        )
    else:
        gain = lambda vector: vector[None]
        own_valid = jnp.clip(length - lax.axis_index("seq") * frames, 0, frames)
        own_valid = own_valid[None].astype(jnp.int32)
        grad_rows, grad_final, branch_two = step_call(
            final_back_kernel,
            "final_back",
            [own_valid],
            [cotangent[0], rows_fourth, gain(g_final)],
            input_outs(rows_fourth),
        )
        hidden_two = ffn_hidden_grad(branch_two, down_two, second_stored, "second")
        two = ModuleScatter(ffn_jobs(branch_two, hidden_two, second_stored), "second_terms")
        two.share()
        two.first_send()
        grad_rows, grad_gain_two, branch_conv = ffn_up_back_input(
            hidden_two, rows_third, gain(g_second), grad_rows, up_two, 1.0, "second_up_back"
        )
        grad_rows, branch_conv = fence([two], grad_rows, branch_conv)
        depth, inverse_std = conv_stored[10], conv_stored[7]
        spread = jnp.broadcast_to(frame_count, (model_width,))
        vectors = jnp.stack([batch_stats[0], inverse_std, scale_float, shift_float, spread])
        grad_shaped, sums = step_call(
            shaped_back_kernel,
            "shaped_back",
            [own_valid],
            [branch_conv, depth, vectors, Block(middle, 6)],
            [rows_like(depth), vector_like(depth, 2)],
        )
        totals = sum_in_steps(sums, [("dp", b) for b in axis_bits("dp")])
        (totals,) = fence([two], totals)
        two.first_swap()
        totals = sum_in_steps(totals, [("seq", b) for b in axis_bits("seq")])
        rim = jax.ShapeDtypeStruct((taps // 2, model_width), bf16)
        grad_depth, top, bottom = step_call(
            depth_back_kernel,
            "depth_back",
            [own_valid],
            [grad_shaped, depth, vectors, totals],
            [rows_like(depth, bf16), rim, rim],
        )
        seq_size = lax.axis_size("seq")
        before = lax.ppermute(bottom, "seq", [(i, i + 1) for i in range(seq_size - 1)])
        after = lax.ppermute(top, "seq", [(i + 1, i) for i in range(seq_size - 1)])
        paired, sigmoid_rows, widened = conv_stored[3:6]
        tall = pltpu.VMEM((frames + 32, model_width), f32)
        paired_left, paired_right = step_call(
            taps_back_kernel,
            "taps_back",
            [own_valid],
            [before, grad_depth, after, taps_float.T, paired, sigmoid_rows],
            [rows_like(depth, bf16), rows_like(depth, bf16)],
            [tall],
        )
        (grad_taps,) = step_call(
            taps_sums_kernel,
            "taps_sums",
            [],
            [grad_depth, widened],
            [vector_like(depth, taps)],
            [tall, pltpu.VMEM(depth.shape, f32)],
        )
        conv = ModuleScatter(
            conv_jobs(branch_conv, (paired_left, paired_right), conv_stored), "conv_terms"
        )
        conv.share()
        conv.first_send()
        grad_rows, grad_gain_conv, branch_attend = step_call(
            conv_input_kernel,
            "conv_input_back",
            [],
            [
                paired_left,
                paired_right,
                rows_second,
                gain(g_conv),
                grad_rows,
                Block(middle, 4),
                Block(middle, 5),
            ],
            input_outs(rows_second),
        )
        grad_rows, branch_attend = fence([two, conv], grad_rows, branch_attend)
        two.second_send()
        grad_rows, branch_attend = fence([two, conv], grad_rows, branch_attend)
        two.second_swap()
        conv.first_swap()

        grad_query, grad_key, grad_value = attend_back(
            attend_stored[6], attend_stored[4], attend_stored[5], attend_stored[7], branch_attend, middle
        )
        attend_sum = ModuleScatter(
            attention_jobs(branch_attend, grad_query, grad_key, grad_value, attend_stored),
            "attend_terms",
        )
        blocks = blocks_back(grad_key, grad_value, middle, frames)
        attend_sum.share()

        def send_attend(up, down):
            attend_sum.first_send()
            return fence([attend_sum, conv], up, down)

        def fold_conv(up, down):
            attend_sum.first_swap()
            conv.second_send()
            return fence([conv], up, down)

        def send_two(up, down):
            conv.second_swap()
            two.z_send(1)
            return fence([two], up, down)

        parts = scatter_line(blocks, (send_attend, fold_conv, send_two))
        two.z_swap(1)
        grad_rows, grad_gain_attend, branch_one = step_call(
            attend_input_kernel,
            "attend_input_back",
            [],
            [*parts, grad_query, rows_first, gain(g_attend), grad_rows, Block(middle, 0)],
            input_outs(rows_first),
        )
        down_sum = ModuleScatter(ffn_jobs(branch_one, None, first_stored)[1:], "down_terms")
        down_sum.share()
        down_sum.first_send()
        branch_one, grad_rows = fence([attend_sum, down_sum], branch_one, grad_rows)
        down_sum.first_swap()
        hidden_one = ffn_hidden_grad(branch_one, down_one, first_stored, "first")
        hidden_one, grad_rows = fence([two, conv], hidden_one, grad_rows)
        two.z_send(2)
        two.z_swap(2)
        conv.z_send(1)
        conv.z_swap(1)
        up_sum = ModuleScatter(ffn_jobs(branch_one, hidden_one, first_stored)[:1], "up_terms")
        up_sum.share()
        attend_sum.second_send()
        up_sum.first_send()
        hidden_one, grad_rows = fence(
            [two, conv, down_sum, attend_sum, up_sum], hidden_one, grad_rows
        )
        attend_sum.second_swap()
        up_sum.first_swap()
        conv.z_send(2)
        conv.z_swap(2)
        down_sum.second_send()
        two_grads = two.finish()
        grad_rows, grad_gain_one, _ = ffn_up_back_input(
            hidden_one, start_rows, gain(g_first), grad_rows, up_one, 1.0, "first_up_back"
        )
        grad_final, grad_gain_two, grad_gain_conv, grad_gain_attend, grad_gain_one = (
            g[0]
            for g in (grad_final, grad_gain_two, grad_gain_conv, grad_gain_attend, grad_gain_one)
        )
    total_shift, total_scale = totals
    input_grad = grad_rows * (1.0 - masked_float)
    mask_grad = jnp.sum(grad_rows * masked_float, axis=0)

    sums = jnp.concatenate(
        [
            jnp.stack(
                [
                    mask_grad,
                    grad_gain_one,
                    grad_gain_attend,
                    grad_gain_conv,
                    grad_gain_two,
                    grad_final,
                ]
            ),
            grad_taps,
        ],
        axis=0,
    )
    sums = jnp.transpose(sums.reshape(-1, shards, own_rows), (1, 0, 2))
    if steps:
        few = SmallScatter(sums)
        (two_grads,) = fence([conv, attend_sum, up_sum, down_sum, few], two_grads)
        down_sum.second_swap()
        attend_sum.z_send(1)
        attend_sum.z_swap(1)
        few.step()
        up_sum.second_send()
        up_sum.second_swap()
        conv_grads = conv.finish()
        (conv_grads,) = fence([down_sum, attend_sum, up_sum, few], conv_grads)
        down_sum.z_send(1)
        down_sum.z_swap(1)
        up_sum.z_send(1)
        up_sum.z_swap(1)
        attend_sum.z_send(2)
        attend_sum.z_swap(2)
        few.step()
        fence([down_sum, up_sum, attend_sum, few])
        down_sum.z_send(2)
        down_sum.z_swap(2)
        up_sum.z_send(2)
        up_sum.z_swap(2)
        few.step()
        few.step()
        few.step()
        few.step()
        sums = few.keep[0]
        grad_up_two, grad_down_two = two_grads
        grad_pair, grad_conv_out = conv_grads
        attend_grads = attend_sum.finish()
        (grad_up_one,) = up_sum.finish()
        (grad_down_one,) = down_sum.finish()
    else:
        sums = scatter_small(sums)[0]
        grad_up_two, grad_down_two = scatter_module(jobs_two)
        grad_pair, grad_conv_out = scatter_module(jobs_conv)
        attend_grads = scatter_module(jobs_attend)
        grad_up_one, grad_down_one = scatter_module(jobs_one)
    grad_joint = jnp.concatenate(list(attend_grads[:2]), axis=1)
    grad_attend_out = attend_grads[2]
    own_start = (lax.axis_index("dp") * lax.axis_size("seq") + lax.axis_index("seq")) * own_rows
    scale_grad = lax.dynamic_slice_in_dim(total_scale, own_start, own_rows)
    shift_grad = lax.dynamic_slice_in_dim(total_shift, own_start, own_rows)
    batch_mean, batch_var, _ = batch_stats
    moment_var = batch_var * frame_count / (frame_count - 1.0)
    return (
        output[None],
        input_grad[None],
        sums[0],
        sums[1],
        grad_up_one,
        grad_down_one,
        sums[2],
        grad_joint,
        grad_attend_out,
        sums[3],
        grad_pair,
        sums[6 : 6 + taps].T,
        scale_grad,
        shift_grad,
        grad_conv_out,
        sums[4],
        grad_up_two,
        grad_down_two,
        sums[5],
        batch_mean,
        moment_var,
    )


def solution(mesh):
    both = P(("dp", "seq"))
    rows = P(("dp", "seq"), None)
    frames = P("dp", "seq", None)
    in_specs = (
        frames,
        P("dp"),
        P("dp", "seq"),
        both,
        both,
        rows,
        rows,
        both,
        rows,
        rows,
        both,
        rows,
        rows,
        both,
        both,
        rows,
        both,
        rows,
        rows,
        both,
        frames,
    )
    out_specs = (
        frames,
        frames,
        both,
        both,
        rows,
        rows,
        both,
        rows,
        rows,
        both,
        rows,
        rows,
        both,
        both,
        rows,
        both,
        rows,
        rows,
        both,
        P(),
        P(),
    )
    return jax.shard_map(
        per_device, mesh=mesh, in_specs=in_specs, out_specs=out_specs, check_vma=False
    )
```

```python
import functools

import jax
import jax.numpy as jnp
from jax import lax
from jax.experimental import pallas as pl
from jax.experimental.pallas import tpu as pltpu
from jax.sharding import PartitionSpec as P

HEADS = 16
HEAD_DIM = 64
epsilon = 1e-05
f32 = jnp.float32
bf16 = jnp.bfloat16


def product(left_side, right_side):
    return jnp.dot(left_side, right_side, preferred_element_type=f32)


def product_lead(left_side, right_side):
    return lax.dot_general(
        left_side, right_side, (((0,), (0,)), ((), ())), preferred_element_type=f32
    )


def product_tail(left_side, right_side):
    return lax.dot_general(
        left_side, right_side, (((1,), (1,)), ((), ())), preferred_element_type=f32
    )


def tie(*values):
    return lax.optimization_barrier(values)


def axis_bits(axis):
    size = lax.axis_size(axis)
    return [1 << i for i in range(size.bit_length() - 1)]


def swap(values, axis, bit):
    return lax.ppermute(values, axis, [(i, i ^ bit) for i in range(lax.axis_size(axis))])


def bit_of(axis, bit):
    return (lax.axis_index(axis) & bit) // bit


def all_bits():
    return [("dp", b) for b in axis_bits("dp")] + [("seq", b) for b in axis_bits("seq")]


def pick(array, axis, index):
    return lax.dynamic_index_in_dim(array, index, axis, keepdims=False)


def gather_small(part):
    whole = part
    for axis, bit in [("seq", b) for b in axis_bits("seq")] + [("dp", b) for b in axis_bits("dp")]:
        other = swap(whole, axis, bit)
        upper = bit_of(axis, bit) > 0
        whole = jnp.concatenate(
            [jnp.where(upper, other, whole), jnp.where(upper, whole, other)], axis=0
        )
    return whole


def sum_small(values):
    for axis, bit in all_bits():
        values = values + swap(values, axis, bit)
    return values


def scatter_small(values):
    for axis, bit in [("dp", b) for b in axis_bits("dp")[::-1]] + [
        ("seq", b) for b in axis_bits("seq")[::-1]
    ]:
        view = values.reshape((2, values.shape[0] // 2) + values.shape[1:])
        mine = bit_of(axis, bit)
        values = pick(view, 0, mine) + swap(pick(view, 0, 1 - mine), axis, bit)
    return values


def merge_moments(count, mean, square):
    packed = jnp.stack([jnp.broadcast_to(count, mean.shape), mean, square])
    for axis, bit in all_bits():
        other = swap(packed, axis, bit)
        upper = bit_of(axis, bit) > 0
        low = jnp.where(upper, other, packed)
        high = jnp.where(upper, packed, other)
        total = low[0] + high[0]
        share = high[0] / jnp.maximum(total, 1.0)
        delta = high[1] - low[1]
        packed = jnp.stack(
            [
                total,
                low[1] + delta * share,
                low[2] + high[2] + delta * delta * (low[0] * share),
            ]
        )
    return packed[0, 0], packed[1], packed[2]


def group_bits():
    return axis_bits("dp")[1:]


def owner_columns(rows_of_lhs):
    tokens, rows = rows_of_lhs.shape
    groups = lax.axis_size("dp") // 2
    return rows_of_lhs.reshape(tokens, groups, 2, rows // (2 * groups))


def grad_job(lhs, rhs, share_rows):
    core = bit_of("dp", 1)
    cols = owner_columns(lhs)
    mine, other = pick(cols, 2, core), pick(cols, 2, 1 - core)
    if share_rows:
        lhs_all = jnp.concatenate([mine, swap(other, "dp", 1)], axis=0)
        rhs_all = jnp.concatenate([rhs, swap(rhs, "dp", 1)], axis=0)
        return lhs_all, rhs_all
    return mine, other, rhs


def rows_product(cols, rhs):
    return product_lead(cols.reshape(cols.shape[0], -1), rhs).astype(bf16)


def split_bit(array, axis, size, bit):
    shape = array.shape
    return array.reshape(shape[:axis] + (size // (2 * bit), 2, bit) + shape[axis + 1 :])


def halve_cols(cols, bit, groups):
    view = split_bit(cols, 1, groups, bit)
    mine = bit_of("dp", 2 * bit)
    flat = lambda a: a.reshape((a.shape[0], groups // 2) + cols.shape[2:])
    return flat(pick(view, 2, mine)), flat(pick(view, 2, 1 - mine))


def add_pair(keep, other, dtype=bf16):
    return (keep.astype(f32) + other.astype(f32)).astype(dtype)


def remaining_position(done, bit):
    return bit >> sum(1 for d in done if d < bit)


def scatter_job(job, rows):
    groups = lax.axis_size("dp") // 2
    seq = lax.axis_size("seq")
    bits = [b // 2 for b in group_bits()]
    halves = []
    shared = len(job) == 2
    rhs = job[-1]
    width = rhs.shape[1] // 2
    for half in range(2):
        order = bits if half == 0 else bits[::-1]
        part = rhs[:, half * width : (half + 1) * width]
        if shared:
            first, rest = order[0], order[1:]
            mine, other = halve_cols(job[0], first, groups)
            got = swap(rows_product(other, part), "dp", 2 * first)
            keep = rows_product(mine, part)
            done = [first]
        else:
            got = swap(rows_product(job[1], part), "dp", 1)
            keep = rows_product(job[0], part)
            rest, done = order, []
        size = groups >> len(done)
        keep, got = (a.reshape(size, -1, width) for a in (keep, got))
        for bit in rest:
            place = remaining_position(done, bit)
            view_keep = split_bit(keep, 0, size, place)
            view_got = split_bit(got, 0, size, place)
            mine = bit_of("dp", 2 * bit)
            send = add_pair(pick(view_keep, 1, 1 - mine), pick(view_got, 1, 1 - mine))
            keep = add_pair(pick(view_keep, 1, mine), pick(view_got, 1, mine))
            size //= 2
            got = swap(send, "dp", 2 * bit).reshape(size, -1, width)
            keep = keep.reshape(size, -1, width)
            done.append(bit)
        halves.append((keep.reshape(seq, rows, width), got.reshape(seq, rows, width)))
    keep = got = None
    size = seq
    done = []
    for bit in axis_bits("seq"):
        place = remaining_position(done, bit)
        mine = bit_of("seq", bit)

        def side(which):
            if keep is None:
                return jnp.concatenate(
                    [
                        add_pair(
                            pick(split_bit(a, 0, size, place), 1, which),
                            pick(split_bit(b, 0, size, place), 1, which),
                        )
                        for a, b in halves
                    ],
                    axis=-1,
                )
            return add_pair(
                pick(split_bit(keep, 0, size, place), 1, which),
                pick(split_bit(got, 0, size, place), 1, which),
            )

        send, kept = side(1 - mine), side(mine)
        size //= 2
        got = swap(send, "seq", bit).reshape(size, rows, -1)
        keep = kept.reshape(size, rows, -1)
        done.append(bit)
    return add_pair(keep[0], got[0], f32)


def in_steps(model_width):
    return lax.axis_size("dp") == 8 and lax.axis_size("seq") == 4 and model_width == 1024


BLOCK = 512


def terms_of(refs, pairs, half, rows, blocks, seq):
    own, got = (jnp.concatenate([refs[2 * i][...], refs[2 * i + 1][...]], axis=1) for i in (0, 1))
    rhs = refs[4:]
    if pairs:
        rhs = rhs[2 * half : 2 * half + 2]
    total = product_lead(own, rhs[0][...]) + product_lead(got, rhs[1][...])
    for block in range(2):
        for z in range(seq):
            for j in range(blocks):
                start = (block * seq + z) * rows
                yield block, z, j, total[start : start + rows, j * BLOCK : (j + 1) * BLOCK]


def job_refs(refs, shape):
    at = start = 0
    for rows, blocks, pairs in shape:
        count = 8 if pairs else 6
        yield refs[at : at + count], pairs, rows, blocks, start
        at += count
        start += rows * blocks


def send_kernel(shape, seq, table_ref, *refs):
    del table_ref
    outs = refs[-2:]
    for half in range(2):

        @pl.when(pl.program_id(0) == half)
        def _():
            for part, pairs, rows, blocks, start in job_refs(refs, shape):
                for block, z, j, piece in terms_of(part, pairs, half, rows, blocks, seq):
                    at = start + j * rows
                    outs[half][block, z, at : at + rows, :] = piece.astype(bf16)


def fold_kernel(shape, seq, table_ref, *refs):
    del table_ref
    gots, (sends, keep) = refs[-7:-3], (refs[-3:-1], refs[-1])
    for half in range(2):

        @pl.when(pl.program_id(0) == half)
        def _():
            for part, pairs, rows, blocks, start in job_refs(refs, shape):
                for block, z, j, piece in terms_of(part, pairs, half, rows, blocks, seq):
                    at = slice(start + j * rows, start + (j + 1) * rows)
                    piece = (piece + gots[2 * half + block][0, z, at, :].astype(f32)).astype(bf16)
                    if block == 0:
                        sends[half][z, at, :] = piece
                    else:
                        keep[0, z, at, :] = piece


def split_kernel(bits, bit_ref, keep_ref, *refs):
    gots, (send_ref, left_ref) = refs[:-2], refs[-2:]
    mine = bit_ref[0]
    for half in range(2):
        for entry in range(send_ref.shape[1]):
            for ref, side in ((send_ref, 1 - mine), (left_ref, mine)):
                at = 2 * entry + side if bits == 2 else side
                if len(gots) == 2:
                    got = gots[half][at]
                else:
                    got = gots[0][half, at]
                total = keep_ref[half, at].astype(f32) + got.astype(f32)
                ref[half, entry] = total.astype(bf16)


def finish_kernel(shape, keep_ref, got_ref, *outs):
    start = 0
    for out, (rows, blocks, _) in zip(outs, shape):
        for half in range(2):
            for j in range(blocks):
                at = slice(start + j * rows, start + (j + 1) * rows)
                columns = slice((half * blocks + j) * BLOCK, (half * blocks + j + 1) * BLOCK)
                out[:, columns] = keep_ref[half, 0, at, :].astype(f32) + got_ref[
                    half, 0, at, :
                ].astype(f32)
        start += rows * blocks


LIMIT = pltpu.CompilerParams(vmem_limit_bytes=56 << 20)


def whole_call(kernel, name, bits, inputs, outs):
    spec = lambda x: pl.BlockSpec(x.shape, lambda i, *t: (0,) * len(x.shape))
    size = sum(x.size * x.dtype.itemsize for x in list(inputs) + list(outs))
    return pl.pallas_call(
        kernel,
        grid_spec=pltpu.PrefetchScalarGridSpec(
            num_scalar_prefetch=len(bits),
            grid=(1,),
            in_specs=[spec(x) for x in inputs],
            out_specs=[spec(o) for o in outs],
        ),
        out_shape=outs,
        compiler_params=LIMIT,
        cost_estimate=pl.CostEstimate(flops=1024, transcendentals=0, bytes_accessed=1024),
        name=name,
    )(*bits, *inputs)


class SmallScatter:
    def __init__(self, values):
        self.keep = values
        self.bits = [("dp", b) for b in axis_bits("dp")[::-1]]
        self.bits += [("seq", b) for b in axis_bits("seq")[::-1]]
        self.got = None

    def step(self):
        if self.got is not None:
            self.keep = self.keep + self.got
        if not self.bits:
            return
        axis, bit = self.bits.pop(0)
        view = self.keep.reshape((2, self.keep.shape[0] // 2) + self.keep.shape[1:])
        mine = bit_of(axis, bit)
        self.keep, sent = pick(view, 0, mine), pick(view, 0, 1 - mine)
        self.got = swap(sent, axis, bit)


class ModuleScatter:
    def __init__(self, jobs, name):
        self.jobs = jobs
        self.name = name
        self.shape = tuple((j[4], j[5] // BLOCK, j[3][0] is not j[3][1]) for j in jobs)
        self.rows = sum(rows * blocks for rows, blocks, _ in self.shape)

    def share(self):
        self.others = {}
        for lhs, rhs in ((j[0], j[3]) for j in self.jobs):
            for array in (lhs, *rhs):
                if id(array) not in self.others:
                    self.others[id(array)] = swap(array, "dp", 1)

    def operands(self):
        specs, args = [], []
        for lhs, _, tokens, rhs, rows, width in self.jobs:
            wide = 4 * rows
            for array in (lhs, self.others[id(lhs)]):
                for block in range(2):
                    spec = lambda h, t, block=block: (0, t[h, block])
                    specs.append(pl.BlockSpec((tokens, wide), spec))
                    args.append(array)
            if rhs[0] is rhs[1]:
                for array in (rhs[0], self.others[id(rhs[0])]):
                    specs.append(pl.BlockSpec((tokens, width), lambda h, t: (0, h)))
                    args.append(array)
            else:
                for half in rhs:
                    for array in (half, self.others[id(half)]):
                        specs.append(pl.BlockSpec((tokens, width), lambda h, t: (0, 0)))
                        args.append(array)
        return specs, args

    def call(self, kernel, name, table, more, more_specs, outs, out_specs):
        specs, args = self.operands()
        flops = sum(16 * j[2] * 4 * j[4] * j[5] for j in self.jobs)
        moved = sum(4 * j[2] * (4 * j[4] * 2 + 2 * j[5]) for j in self.jobs)
        moved += 2 * sum(x.size for x in list(more) + list(outs))
        return pl.pallas_call(
            functools.partial(kernel, self.shape, 4),
            grid_spec=pltpu.PrefetchScalarGridSpec(
                num_scalar_prefetch=1,
                grid=(2,),
                in_specs=specs + more_specs,
                out_specs=out_specs,
            ),
            out_shape=outs,
            compiler_params=LIMIT,
            cost_estimate=pl.CostEstimate(flops=1024, transcendentals=0, bytes_accessed=1024),
            name=self.name + name,
        )(table, *args, *more)

    def first_send(self):
        core, x, y = (bit_of("dp", b) for b in (1, 2, 4))
        table = [
            [core + 2 * (1 - x) + 4 * i for i in range(2)],
            [core + 2 * i + 4 * (1 - y) for i in range(2)],
        ]
        table = jnp.stack([jnp.stack(row) for row in table]).astype(jnp.int32)
        out = jax.ShapeDtypeStruct((2, 4, self.rows, BLOCK), bf16)
        spec = pl.BlockSpec(out.shape, lambda h, t: (0, 0, 0, 0))
        self.sends = self.call(send_kernel, "_send", table, [], [], [out, out], [spec, spec])

    def first_swap(self):
        self.got = [swap(s, "dp", b) for s, b in zip(self.sends, (2, 4))]
        self.sends = None

    def second_send(self):
        core, x, y = (bit_of("dp", b) for b in (1, 2, 4))
        table = [
            [core + 2 * x + 4 * side for side in (1 - y, y)] + [1 - y, y],
            [core + 2 * side + 4 * y for side in (1 - x, x)] + [1 - x, x],
        ]
        table = jnp.stack([jnp.stack(row) for row in table]).astype(jnp.int32)
        piece = (4, self.rows, BLOCK)
        more, more_specs = [], []
        for half in range(2):
            for block in range(2):
                spec = lambda h, t, half=half, block=block: (t[half, 2 + block], 0, 0, 0)
                more.append(self.got[half])
                more_specs.append(pl.BlockSpec((1,) + piece, spec))
        outs = [jax.ShapeDtypeStruct(s, bf16) for s in (piece, piece, (2,) + piece)]
        spec = pl.BlockSpec(piece, lambda h, t: (0, 0, 0))
        keep_spec = pl.BlockSpec((1,) + piece, lambda h, t: (h, 0, 0, 0))
        *self.sends, self.keep = self.call(
            fold_kernel, "_fold", table, more, more_specs, outs, [spec, spec, keep_spec]
        )
        self.got = None

    def second_swap(self):
        self.got = [swap(s, "dp", b) for s, b in zip(self.sends, (4, 2))]
        self.sends = None

    def z_send(self, bit):
        entries = 2 if bit == 1 else 1
        out = jax.ShapeDtypeStruct((2, entries, self.rows, BLOCK), bf16)
        gots = self.got if bit == 1 else [self.got]
        mine = bit_of("seq", bit)[None].astype(jnp.int32)
        self.sends, self.keep = whole_call(
            functools.partial(split_kernel, entries),
            f"{self.name}_z{bit}",
            [mine],
            [self.keep, *gots],
            [out, out],
        )
        self.got = None

    def z_swap(self, bit):
        self.got = swap(self.sends, "seq", bit)
        self.sends = None

    def finish(self):
        outs = [jax.ShapeDtypeStruct((j[4], 2 * j[5]), f32) for j in self.jobs]
        return whole_call(
            functools.partial(finish_kernel, self.shape),
            self.name + "_finish",
            [],
            [self.keep, self.got],
            outs,
        )


def scatter_module(jobs):
    outs = []
    for lhs, start, tokens, rhs, rows, columns in jobs:
        whole = rhs[0] if rhs[0] is rhs[1] else jnp.concatenate(rhs, axis=1)
        outs.append(scatter_job(grad_job(lhs[start : start + tokens], whole, True), rows))
    return outs


def one(rhs):
    return (rhs, rhs)


FIELDS = ("got", "keep", "sends")


def fence(things, *extras):
    fields = [{k: v for k, v in vars(t).items() if k in FIELDS} for t in things]
    fields, extras = lax.optimization_barrier((fields, extras))
    for thing, values in zip(things, fields):
        vars(thing).update(values)
    return extras


def fetch_weight(part):
    return lax.all_gather(part, ("dp", "seq"), axis=0, tiled=True)


def pack_kernel(*refs):
    shards, out = refs[:-1], refs[-1]
    width = out.shape[1]
    at = 0
    for shard in shards:
        rows = shard.shape[0]
        for j in range(shard.shape[1] // width):
            out[at : at + rows, :] = shard[:, j * width : (j + 1) * width]
            at += rows


def pack(shards, name):
    width = shards[-1].shape[1]
    rows = sum(s.shape[0] * s.shape[1] // width for s in shards)
    out = jax.ShapeDtypeStruct((rows, width), bf16)
    return whole_call(pack_kernel, name, [], shards, [out])[0]


def gather_packed(part):
    return lax.all_gather(part, ("dp", "seq"), axis=0)


def packed_block(packed, start, rows):
    return packed[:, start : start + rows].reshape(-1, packed.shape[2])


def up_kernel(normed_ref, weight_ref, active_ref, slope_ref):
    width = normed_ref.shape[1]
    for half in range(2):
        columns = slice(half * width // 2, (half + 1) * width // 2)
        block = weight_ref[:, :, columns].reshape(width, width // 2)
        hidden = product(normed_ref[...], block)
        sigmoid = 1.0 / (1.0 + jnp.exp(-hidden))
        active_ref[:, columns] = (hidden * sigmoid).astype(bf16)
        slope_ref[:, columns] = (sigmoid * (1.0 + hidden * (1.0 - sigmoid))).astype(bf16)


def up_back_kernel(grad_ref, weight_ref, out_ref):
    width = out_ref.shape[1]
    part = product_tail(grad_ref[...], weight_ref[...].reshape(width, -1))
    out_ref[...] = jnp.where(pl.program_id(0) == 0, part, out_ref[...] + part)


def down_kernel(values_ref, active_ref, weight_ref, out_ref, total_ref):
    width = out_ref.shape[1]
    part = product(active_ref[...], weight_ref[...].reshape(-1, width))
    total_ref[...] = jnp.where(pl.program_id(0) == 0, part, total_ref[...] + part)

    @pl.when(pl.program_id(0) == pl.num_programs(0) - 1)
    def _():
        out_ref[...] = values_ref[...] + 0.5 * total_ref[...]


def down_back_kernel(branch_ref, slope_ref, weight_ref, out_ref):
    width = branch_ref.shape[1]
    part = product_tail(branch_ref[...], weight_ref[...].reshape(-1, width))
    out_ref[...] = (part * slope_ref[...].astype(f32)).astype(bf16)


def ffn_call(kernel, name, packed, part, inputs, outs, scratch=()):
    owners, _, width = packed.shape
    steps = 4
    rows = width // owners
    if part == "up":
        weight = pl.BlockSpec((owners, rows, width), lambda i: (0, i, 0))
    else:
        weight = pl.BlockSpec((owners // steps, rows * steps, width), lambda i: (i, 1, 0))

    def spec(x):
        tokens, columns = x.shape
        return pl.BlockSpec((tokens, min(width, columns)), (lambda i: (0, i)) if columns > width else (lambda i: (0, 0)))

    numbers = lambda things: sum(t.size * t.dtype.itemsize for t in things)
    tokens = inputs[0].shape[0]
    inner = steps * width
    return pl.pallas_call(
        kernel,
        grid=(steps,),
        in_specs=[spec(x) for x in inputs] + [weight],
        out_specs=[spec(o) for o in outs],
        out_shape=outs,
        scratch_shapes=list(scratch),
        compiler_params=pltpu.CompilerParams(vmem_limit_bytes=56 << 20),
        cost_estimate=pl.CostEstimate(flops=1024, transcendentals=0, bytes_accessed=1024),
        name=name,
    )(*inputs, packed)


class Packed:
    def __init__(self, array):
        self.array = array


def ffn_up(normed, packed, name):
    tokens, width = normed.shape
    out = jax.ShapeDtypeStruct((tokens, 4 * width), bf16)
    return ffn_call(up_kernel, name, packed.array, "up", [normed], [out, out])


def ffn_up_back(grad_hidden, packed, name):
    out = jax.ShapeDtypeStruct((grad_hidden.shape[0], packed.array.shape[2]), f32)
    return ffn_call(up_back_kernel, name, packed.array, "up", [grad_hidden], [out])[0]


def ffn_down(values, active, packed, name):
    out = jax.ShapeDtypeStruct(values.shape, f32)
    scratch = [pltpu.VMEM(values.shape, f32)]
    return ffn_call(down_kernel, name, packed.array, "down", [values, active], [out], scratch)[0]


def ffn_down_back(branch, slope, packed, name):
    out = jax.ShapeDtypeStruct(slope.shape, bf16)
    return ffn_call(down_back_kernel, name, packed.array, "down", [branch, slope], [out])[0]


def gather_line(own):
    seq = lax.axis_size("seq")
    ups, downs = [own], [own]
    for step in range(seq - 1):
        ups.append(lax.ppermute(ups[-1], "seq", [(i, i + 1) for i in range(seq - 1)]))
        downs.append(lax.ppermute(downs[-1], "seq", [(i + 1, i) for i in range(seq - 1)]))
    me = lax.axis_index("seq")
    blocks = [own]
    for r in range(1, seq):
        blocks.append(jnp.where(me + r < seq, downs[r], ups[seq - r]))
    return jnp.stack(blocks)


def scatter_line(blocks, between=()):
    seq = lax.axis_size("seq")
    up = down = None
    between = iter(between)
    for step in range(seq - 1, 0, -1):
        message_up, message_down = blocks[step], blocks[seq - step]
        if up is not None:
            message_up = add_pair(message_up, up)
            message_down = add_pair(message_down, down)
        up = lax.ppermute(message_up, "seq", [(i, i + 1) for i in range(seq - 1)])
        down = lax.ppermute(message_down, "seq", [(i + 1, i) for i in range(seq - 1)])
        meanwhile = next(between, None)
        if meanwhile is not None:
            up, down = meanwhile(up, down)
    if up is None:
        up = down = jnp.zeros_like(blocks[0])
    return blocks[0], up, down


def sum_parts(parts):
    return sum(part.astype(f32) for part in parts)


def with_halo(shard, width):
    size, length = lax.axis_size("seq"), shard.shape[0]
    up = [(i, i + 1) for i in range(size - 1)]
    down = [(i + 1, i) for i in range(size - 1)]
    before = lax.ppermute(shard[length - width :], "seq", up)
    after = lax.ppermute(shard[:width], "seq", down)
    return jnp.concatenate([before, shard, after], axis=0)


def norm_forward(values, norm_gain):
    centered = values - jnp.mean(values, axis=-1, keepdims=True)
    inverse = lax.rsqrt(jnp.mean(centered * centered, axis=-1, keepdims=True) + epsilon)
    normal = centered * inverse
    return (normal * norm_gain, normal, inverse)


def norm_backward(grad_out, norm_gain, normal, inverse):
    scaled = grad_out * norm_gain
    grad_in = inverse * (
        scaled
        - jnp.mean(scaled, axis=-1, keepdims=True)
        - normal * jnp.mean(scaled * normal, axis=-1, keepdims=True)
    )
    return (grad_in, jnp.sum(grad_out * normal, axis=0))


def silu_slope(hidden):
    sigmoid_rows = jax.nn.sigmoid(hidden)
    return sigmoid_rows * (1.0 + hidden * (1.0 - sigmoid_rows))


def ffn_forward(values, norm_gain, upward, downward, name):
    normed, normal, inverse = norm_forward(values, norm_gain)
    normed_low = normed.astype(bf16)
    if isinstance(upward, Packed):
        active, slope = ffn_up(normed_low, upward, name + "_up")
        out = ffn_down(values, active, downward, name + "_down")
    else:
        hidden = product(normed_low, upward)
        active, slope = jax.nn.silu(hidden).astype(bf16), silu_slope(hidden)
        out = values + 0.5 * product(active, downward)
    return out, (normed_low, normal, inverse, slope, active)


def owner_rows(rows):
    return rows // (lax.axis_size("dp") * lax.axis_size("seq"))


def ffn_hidden_grad(grad_branch, downward, stored, name):
    if isinstance(downward, Packed):
        return ffn_down_back(grad_branch, stored[3], downward, name + "_down_back")
    return (product_tail(grad_branch, downward) * stored[3]).astype(bf16)


def ffn_input_grad(grad_rows, grad_hidden, norm_gain, upward, stored, name):
    if isinstance(upward, Packed):
        grad_normed = ffn_up_back(grad_hidden, upward, name + "_up_back")
    else:
        grad_normed = product_tail(grad_hidden, upward)
    grad_in, grad_gain = norm_backward(grad_normed, norm_gain, stored[1], stored[2])
    return grad_rows + grad_in, grad_gain


def ffn_jobs(grad_branch, grad_hidden, stored):
    normed_low, active = stored[0], stored[4]
    tokens, width = normed_low.shape
    inner = active.shape[1]
    return [
        (normed_low, 0, tokens, one(grad_hidden), owner_rows(width), inner // 2),
        (active, 0, tokens, one(grad_branch), owner_rows(inner), width // 2),
    ]


def norm_back(grad, norm_gain, values):
    centered = values - jnp.mean(values, axis=-1, keepdims=True)
    inverse = lax.rsqrt(jnp.mean(centered * centered, axis=-1, keepdims=True) + epsilon)
    normal = centered * inverse
    scaled = grad * norm_gain
    grad_in = inverse * (
        scaled
        - jnp.mean(scaled, axis=-1, keepdims=True)
        - normal * jnp.mean(scaled * normal, axis=-1, keepdims=True)
    )
    return grad_in, jnp.sum(grad * normal, axis=0, keepdims=True)


def valid_mask(count_ref, shape):
    return (lax.broadcasted_iota(jnp.int32, (shape[0], 1), 0) < count_ref[0]).astype(f32)


class Block:
    def __init__(self, packed, index):
        self.packed, self.index = packed, index

    def spec(self):
        owners, _, width = self.packed.shape
        index = self.index
        return pl.BlockSpec((owners, width // owners, width), lambda i, *t: (0, index, 0))


def step_call(kernel, name, scalars, inputs, outs, scratch=()):
    def spec(x):
        if isinstance(x, Block):
            return x.spec()
        return pl.BlockSpec(x.shape, lambda i, *t: (0,) * len(x.shape))

    return pl.pallas_call(
        kernel,
        grid_spec=pltpu.PrefetchScalarGridSpec(
            num_scalar_prefetch=len(scalars),
            grid=(1,),
            in_specs=[spec(x) for x in inputs],
            out_specs=[spec(o) for o in outs],
            scratch_shapes=list(scratch),
        ),
        out_shape=outs,
        compiler_params=LIMIT,
        cost_estimate=pl.CostEstimate(flops=1024, transcendentals=0, bytes_accessed=1024),
        name=name,
    )(*scalars, *[x.packed if isinstance(x, Block) else x for x in inputs])


def rows_like(array, dtype=f32):
    return jax.ShapeDtypeStruct(array.shape, dtype)


def vector_like(array, count=1):
    return jax.ShapeDtypeStruct((count, array.shape[1]), f32)


def square(ref):
    return ref[...].reshape(ref.shape[2], ref.shape[2])


def final_back_kernel(count_ref, cotangent_ref, values_ref, gain_ref, grad_ref, sum_ref, branch_ref):
    grad = cotangent_ref[...].astype(f32) * valid_mask(count_ref, values_ref.shape)
    grad, sum_ref[...] = norm_back(grad, gain_ref[...], values_ref[...])
    grad_ref[...] = grad
    branch_ref[...] = (0.5 * grad).astype(bf16)


def shaped_back_kernel(
    count_ref, branch_ref, depth_ref, vectors_ref, weight_ref, grad_ref, sums_ref
):
    normal = (depth_ref[...] - vectors_ref[0:1]) * vectors_ref[1:2]
    shaped = normal * vectors_ref[2:3] + vectors_ref[3:4]
    sigmoid = 1.0 / (1.0 + jnp.exp(-shaped))
    slope = sigmoid * (1.0 + shaped * (1.0 - sigmoid)) * valid_mask(count_ref, depth_ref.shape)
    grad = product_tail(branch_ref[...], square(weight_ref)) * slope
    grad_ref[...] = grad
    sums_ref[0:1] = jnp.sum(grad, axis=0, keepdims=True)
    sums_ref[1:2] = jnp.sum(grad * normal, axis=0, keepdims=True)


def depth_back_kernel(
    count_ref, grad_ref, depth_ref, vectors_ref, totals_ref, out_ref, top_ref, bottom_ref
):
    normal = (depth_ref[...] - vectors_ref[0:1]) * vectors_ref[1:2]
    scale = vectors_ref[2:3]
    out = (
        vectors_ref[1:2]
        * valid_mask(count_ref, depth_ref.shape)
        * (
            grad_ref[...] * scale
            - scale * (totals_ref[0:1] + normal * totals_ref[1:2]) / vectors_ref[4:5]
        )
    ).astype(bf16)
    out_ref[...] = out
    width = top_ref.shape[0]
    top_ref[...] = out[:width]
    bottom_ref[...] = out[out.shape[0] - width :]


def taps_back_kernel(
    count_ref, before_ref, grad_ref, after_ref, taps_ref, paired_ref, sigmoid_ref, *refs
):
    left_ref, right_ref, rims = refs
    frames = grad_ref.shape[0]
    taps = taps_ref.shape[0]
    half = taps // 2
    rims[0:half] = before_ref[...].astype(f32)
    rims[half : half + frames] = grad_ref[...].astype(f32)
    rims[half + frames : 2 * half + frames] = after_ref[...].astype(f32)
    valid = valid_mask(count_ref, grad_ref.shape)

    def part(step, carry):
        lanes = pl.ds(pl.multiple_of(step * 128, 128), 128)
        total = jnp.zeros((frames, 128), f32)
        for tap in range(taps):
            start = 2 * half - tap
            total = total + rims[start : start + frames, lanes] * taps_ref[tap : tap + 1, lanes]
        sigmoid = sigmoid_ref[:, lanes]
        left = total * sigmoid * valid
        left_ref[:, lanes] = left.astype(bf16)
        right_ref[:, lanes] = (left * paired_ref[:, lanes] * (1.0 - sigmoid)).astype(bf16)
        return carry

    lax.fori_loop(0, grad_ref.shape[1] // 128, part, 0)


def taps_sums_kernel(grad_ref, widened_ref, sums_ref, wide_rows, own_rows):
    frames = grad_ref.shape[0]
    wide_rows[0 : widened_ref.shape[0]] = widened_ref[...].astype(f32)
    own_rows[...] = grad_ref[...].astype(f32)

    def part(step, carry):
        lanes = pl.ds(pl.multiple_of(step * 128, 128), 128)
        own = own_rows[:, lanes]
        for tap in range(sums_ref.shape[0]):
            sums_ref[tap : tap + 1, lanes] = jnp.sum(
                wide_rows[tap : tap + frames, lanes] * own, axis=0, keepdims=True
            )
        return carry

    lax.fori_loop(0, grad_ref.shape[1] // 128, part, 0)


def conv_input_kernel(
    left_ref, right_ref, values_ref, gain_ref, rows_ref, first_ref, second_ref, *outs
):
    grad = product_tail(left_ref[...], square(first_ref))
    grad = grad + product_tail(right_ref[...], square(second_ref))
    finish_input(grad, gain_ref, values_ref, rows_ref, 1.0, *outs)


def finish_input(grad, gain_ref, values_ref, rows_ref, factor, out_ref, sum_ref, branch_ref):
    grad, sum_ref[...] = norm_back(grad, gain_ref[...], values_ref[...])
    grad = rows_ref[...] + grad
    out_ref[...] = grad
    branch_ref[...] = (factor * grad).astype(bf16)


def attend_input_kernel(
    own_ref, up_ref, down_ref, query_ref, values_ref, gain_ref, rows_ref, weight_ref, *outs
):
    grad = own_ref[...].astype(f32) + up_ref[...].astype(f32) + down_ref[...].astype(f32)
    grad = grad + product_tail(query_ref[...], square(weight_ref))
    finish_input(grad, gain_ref, values_ref, rows_ref, 0.5, *outs)


def input_outs(rows):
    return [rows_like(rows), vector_like(rows), rows_like(rows, bf16)]


def blocks_back_kernel(key_ref, value_ref, key_weight_ref, value_weight_ref, out_ref):
    total = product_tail(key_ref[...], square(key_weight_ref))
    total = total + product_tail(value_ref[...], square(value_weight_ref))
    out_ref[0] = total.astype(bf16)


def blocks_back(grad_key, grad_value, packed, frames):
    keys, width = grad_key.shape
    rows = pl.BlockSpec((frames, width), lambda i: (i, 0))
    return pl.pallas_call(
        blocks_back_kernel,
        grid=(keys // frames,),
        in_specs=[rows, rows, Block(packed, 1).spec(), Block(packed, 2).spec()],
        out_specs=pl.BlockSpec((1, frames, width), lambda i: (i, 0, 0)),
        out_shape=jax.ShapeDtypeStruct((keys // frames, frames, width), bf16),
        compiler_params=LIMIT,
        cost_estimate=pl.CostEstimate(flops=1024, transcendentals=0, bytes_accessed=1024),
        name="attend_blocks_back",
    )(grad_key, grad_value, packed, packed)


def up_back_input_kernel(
    factor, grad_ref, values_ref, gain_ref, rows_ref, weight_ref, out_ref, sum_ref, branch_ref, total
):
    part = product_tail(grad_ref[...], weight_ref[...].reshape(out_ref.shape[1], -1))
    total[...] = jnp.where(pl.program_id(0) == 0, part, total[...] + part)

    @pl.when(pl.program_id(0) == pl.num_programs(0) - 1)
    def _():
        finish_input(
            total[...], gain_ref, values_ref, rows_ref, factor, out_ref, sum_ref, branch_ref
        )


def ffn_up_back_input(grad_hidden, values, gain, rows, packed, factor, name):
    kernel = functools.partial(up_back_input_kernel, factor)
    scratch = [pltpu.VMEM(rows.shape, f32)]
    inputs = [grad_hidden, values, gain, rows]
    return ffn_call(kernel, name, packed.array, "up", inputs, input_outs(rows), scratch)


def sum_at_once(values, axis, offsets):
    got = [swap(values, axis, offset) for offset in offsets]
    return values + (got[0] + (got[1] + got[2]))


def key_valid(offsets_ref, rows, keys):
    count = keys // rows
    spots = []
    for block in range(count):
        spots.append(offsets_ref[block] + lax.broadcasted_iota(jnp.int32, (rows, 1), 0))
    return jnp.concatenate(spots, axis=0) < offsets_ref[count]


def head_mask(block, head):
    lanes = lax.broadcasted_iota(jnp.int32, block.shape, 1)
    inside = (lanes < HEAD_DIM) if head == 0 else (lanes >= HEAD_DIM)
    return jnp.where(inside, block, jnp.zeros_like(block))


def attend_kernel(rows, offsets_ref, query_ref, key_ref, value_ref, mixture_ref, total_ref):
    keys = key_ref[...]
    values = value_ref[...]
    query = query_ref[...] * jnp.asarray(HEAD_DIM**-0.5, bf16)
    valid = key_valid(offsets_ref, rows, keys.shape[0])
    halves = []
    for head in range(2):
        scores = product_tail(keys, head_mask(query, head))
        scores = jnp.where(valid, scores, -1e30)
        largest = jnp.max(scores, axis=0, keepdims=True)
        exponent = jnp.exp(scores - largest)
        totals = jnp.sum(exponent, axis=0, keepdims=True)
        weights = (exponent * (1.0 / totals)).astype(bf16)
        mixed = product_lead(values, weights)
        halves.append(mixed[head * HEAD_DIM : (head + 1) * HEAD_DIM])
        total_ref[0, head : head + 1, :] = largest + jnp.log(totals)
    mixture_ref[...] = jnp.concatenate(halves, axis=0).T.astype(bf16)


def attend_back_kernel(
    rows,
    offsets_ref,
    query_ref,
    key_ref,
    value_ref,
    total_ref,
    grad_ref,
    *refs,
):
    outward, (query_grad_ref, key_grad_ref, value_grad_ref) = refs[:-3], refs[-3:]
    keys = key_ref[...]
    values = value_ref[...]
    grad = grad_ref[...]
    if outward:
        grad = product_tail(grad, outward[0][...].reshape(128, -1)).astype(bf16)
    query = query_ref[...] * jnp.asarray(HEAD_DIM**-0.5, bf16)
    valid = key_valid(offsets_ref, rows, keys.shape[0])
    halves = []
    key_grad = value_grad = None
    for head in range(2):
        query_head = head_mask(query, head)
        grad_head = head_mask(grad, head)
        scores = product_tail(keys, query_head)
        scores = jnp.where(valid, scores, -1e30)
        weights = jnp.exp(scores - total_ref[0, head : head + 1, :])
        grad_weights = product_tail(values, grad_head)
        inner = jnp.sum(weights * grad_weights, axis=0, keepdims=True)
        grad_scores = (weights * (grad_weights - inner)).astype(bf16)
        key_part = product(grad_scores, query_head)
        value_part = product(weights.astype(bf16), grad_head)
        key_grad = key_part if key_grad is None else key_grad + key_part
        value_grad = value_part if value_grad is None else value_grad + value_part
        query_part = product_lead(keys, grad_scores)
        halves.append(query_part[head * HEAD_DIM : (head + 1) * HEAD_DIM])
    query_grad = jnp.concatenate(halves, axis=0).T * HEAD_DIM**-0.5
    query_grad_ref[...] = query_grad.astype(bf16)
    key_grad_ref[...] = key_grad.astype(bf16)
    value_grad_ref[...] = value_grad.astype(bf16)


def attend(offsets, query, key, value):
    rows, width = query.shape
    keys = key.shape[0]
    pairs = width // 128
    return pl.pallas_call(
        functools.partial(attend_kernel, rows),
        grid_spec=pltpu.PrefetchScalarGridSpec(
            num_scalar_prefetch=1,
            grid=(pairs,),
            in_specs=[
                pl.BlockSpec((rows, 128), lambda i, o: (0, i)),
                pl.BlockSpec((keys, 128), lambda i, o: (0, i)),
                pl.BlockSpec((keys, 128), lambda i, o: (0, i)),
            ],
            out_specs=[
                pl.BlockSpec((rows, 128), lambda i, o: (0, i)),
                pl.BlockSpec((1, 2, rows), lambda i, o: (i, 0, 0)),
            ],
        ),
        out_shape=[
            jax.ShapeDtypeStruct((rows, width), bf16),
            jax.ShapeDtypeStruct((pairs, 2, rows), f32),
        ],
        compiler_params=pltpu.CompilerParams(vmem_limit_bytes=48 << 20),
        name="attend",
    )(offsets, query, key, value)


def attend_back(offsets, query, key_value, totals, grad, packed=None):
    rows, width = query.shape
    key, value = key_value
    keys = key.shape[0]
    pairs = width // 128
    row_spec = pl.BlockSpec((rows, 128), lambda i, o: (0, i))
    key_spec = pl.BlockSpec((keys, 128), lambda i, o: (0, i))
    if packed is None:
        grad_specs, more = [row_spec], []
    else:
        owners = packed.shape[0]
        count = 128 * owners // width
        square_rows = pl.BlockSpec((count, width // owners, width), lambda i, o: (i, 3, 0))
        grad_specs, more = [pl.BlockSpec((rows, width), lambda i, o: (0, 0)), square_rows], [packed]
    return pl.pallas_call(
        functools.partial(attend_back_kernel, rows),
        grid_spec=pltpu.PrefetchScalarGridSpec(
            num_scalar_prefetch=1,
            grid=(pairs,),
            in_specs=[
                row_spec,
                key_spec,
                pl.BlockSpec((keys, 128), lambda i, o: (0, i)),
                pl.BlockSpec((1, 2, rows), lambda i, o: (i, 0, 0)),
            ]
            + grad_specs,
            out_specs=[row_spec, key_spec, key_spec],
        ),
        out_shape=[
            jax.ShapeDtypeStruct((rows, width), bf16),
            jax.ShapeDtypeStruct((keys, width), bf16),
            jax.ShapeDtypeStruct((keys, width), bf16),
        ],
        compiler_params=pltpu.CompilerParams(vmem_limit_bytes=48 << 20),
        name="attend_back",
    )(offsets, query, key, value, totals, grad, *more)


def attention_forward(values, length, norm_gain, joint_proj, attend_out, gathered):
    normed, normal, inverse = norm_forward(values, norm_gain)
    normed_low = normed.astype(bf16)
    frames, model_width = normed_low.shape
    seq = lax.axis_size("seq")
    normed_all = gathered(gather_line(normed_low)).reshape(seq * frames, model_width)
    query = product(normed_low, joint_proj[0]).astype(bf16)
    key = product(normed_all, joint_proj[1]).astype(bf16)
    value = product(normed_all, joint_proj[2]).astype(bf16)
    starts = ((lax.axis_index("seq") + jnp.arange(seq)) % seq) * frames
    offsets = jnp.concatenate([starts, length[None]]).astype(jnp.int32)
    mixed_low, totals = attend(offsets, query, key, value)
    output = values + product(mixed_low, attend_out)
    stored = (normed_low, normal, inverse, normed_all, query, (key, value), offsets, totals, mixed_low)
    return (output, stored)


def attention_parts_grad(grad_rows, attend_out, stored):
    normed_low, normal, inverse, normed_all, query, key_value, offsets, totals, mixed_low = stored
    grad_branch = grad_rows.astype(bf16)
    grad_mixed = product_tail(grad_branch, attend_out).astype(bf16)
    return (grad_branch,) + tuple(attend_back(offsets, query, key_value, totals, grad_mixed))


def attention_blocks_grad(grad_key, grad_value, joint_proj, frames):
    width = grad_key.shape[1]
    part = product_tail(grad_key, joint_proj[1]) + product_tail(grad_value, joint_proj[2])
    return part.astype(bf16).reshape(-1, frames, width)


def attention_input_grad(grad_rows, grad_normed, grad_query, norm_gain, joint_proj, stored):
    grad_normed = grad_normed + product_tail(grad_query, joint_proj[0])
    grad_in, grad_gain = norm_backward(grad_normed, norm_gain, stored[1], stored[2])
    return grad_rows + grad_in, grad_gain


def attention_jobs(grad_branch, grad_query, grad_key, grad_value, stored):
    normed_all, mixed_low = stored[3], stored[8]
    frames, width = grad_query.shape
    rows = owner_rows(width)
    return [
        (normed_all, 0, frames, one(grad_query), rows, width // 2),
        (normed_all, 0, normed_all.shape[0], (grad_key, grad_value), rows, width),
        (mixed_low, 0, frames, one(grad_branch), rows, width // 2),
    ]


def conv_forward(
    values, valid_rows, norm_gain, conv_pair, taps_float, batch_scale, batch_shift, conv_out
):
    normed, normal, inverse = norm_forward(values, norm_gain)
    normed_low = normed.astype(bf16)
    paired = product(normed_low, conv_pair[0])
    frames, model_width = paired.shape
    sigmoid_rows = jax.nn.sigmoid(product(normed_low, conv_pair[1]))
    gated_rows = (paired * sigmoid_rows * valid_rows).astype(bf16)
    half_width = taps_float.shape[1] // 2
    widened = with_halo(gated_rows, half_width)
    mixture = jnp.zeros((frames, model_width), f32)
    for offset in range(taps_float.shape[1]):
        mixture = mixture + widened[offset : offset + frames] * taps_float[:, offset]
    own_count = jnp.sum(valid_rows)
    own_mean = jnp.sum(mixture * valid_rows, axis=0) / jnp.maximum(own_count, 1.0)
    own_dev = (mixture - own_mean) * valid_rows
    frame_count, batch_mean, square = merge_moments(
        own_count, own_mean, jnp.sum(own_dev * own_dev, axis=0)
    )
    batch_var = square / frame_count
    inverse_std = lax.rsqrt(batch_var + epsilon)
    normal_batch = (mixture - batch_mean) * inverse_std
    shaped = normal_batch * batch_scale + batch_shift
    active = jax.nn.silu(shaped).astype(bf16)
    output = values + product(active, conv_out)
    stored = (
        normed_low,
        normal,
        inverse,
        paired,
        sigmoid_rows,
        widened,
        normal_batch,
        inverse_std,
        shaped,
        active,
        mixture,
    )
    return (output, stored, (batch_mean, batch_var, frame_count))


def conv_shaped_grad(grad_rows, valid_rows, conv_out, stored):
    normal_batch, shaped = stored[6], stored[8]
    grad_branch = grad_rows.astype(bf16)
    grad_shaped = product_tail(grad_branch, conv_out) * silu_slope(shaped) * valid_rows
    sums = jnp.stack([jnp.sum(grad_shaped, axis=0), jnp.sum(grad_shaped * normal_batch, axis=0)])
    return grad_branch, grad_shaped, sums


def conv_paired_grad(grad_shaped, totals, valid_rows, taps_float, scale_float, frame_count, stored):
    normal_batch, inverse_std = stored[6:8]
    total_shift, total_scale = totals
    grad_mixture = (
        inverse_std
        * valid_rows
        * (
            grad_shaped * scale_float
            - scale_float * (total_shift + normal_batch * total_scale) / frame_count
        )
    ).astype(bf16)
    grad_rims = with_halo(grad_mixture, taps_float.shape[1] // 2)
    return conv_taps_grad(grad_mixture, grad_rims, valid_rows, taps_float, stored)


def conv_taps_grad(grad_mixture, grad_rims, valid_rows, taps_float, stored):
    paired, sigmoid_rows, widened = stored[3:6]
    taps = taps_float.shape[1]
    half_width = taps // 2
    frames, model_width = grad_mixture.shape
    widened_float = widened.astype(f32)
    grad_float = grad_mixture.astype(f32)
    grad_gated = jnp.zeros((frames, model_width), f32)
    tap_grads = []
    for offset in range(taps):
        lower_edge = 2 * half_width - offset
        grad_gated = (
            grad_gated + grad_rims[lower_edge : lower_edge + frames] * taps_float[:, offset]
        )
        tap_grads.append(jnp.sum(widened_float[offset : offset + frames] * grad_float, axis=0))
    grad_left = grad_gated * sigmoid_rows * valid_rows
    grad_right = grad_gated * paired * sigmoid_rows * (1.0 - sigmoid_rows) * valid_rows
    return (grad_left.astype(bf16), grad_right.astype(bf16)), jnp.stack(tap_grads)


def conv_input_grad(grad_rows, grad_paired, norm_gain, conv_pair, stored):
    grad_normed = product_tail(grad_paired[0], conv_pair[0]) + product_tail(
        grad_paired[1], conv_pair[1]
    )
    grad_in, grad_gain = norm_backward(grad_normed, norm_gain, stored[1], stored[2])
    return grad_rows + grad_in, grad_gain


def conv_jobs(grad_branch, grad_paired, stored):
    normed_low, active = stored[0], stored[9]
    frames, width = normed_low.shape
    rows = owner_rows(width)
    return [
        (normed_low, 0, frames, grad_paired, rows, width),
        (active, 0, frames, one(grad_branch), rows, width // 2),
    ]


def per_device(
    inputs,
    lengths,
    token_mask,
    mask_vector,
    gain_first,
    first_up,
    first_down,
    gain_attend,
    joint_proj,
    attend_out,
    gain_conv,
    conv_pair,
    conv_taps,
    batch_scale,
    batch_shift,
    conv_out,
    gain_second,
    second_up,
    second_down,
    gain_final,
    cotangent,
):
    frames = inputs.shape[1]
    model_width = inputs.shape[2]
    taps = conv_taps.shape[1]
    length = lengths[0]
    positions = lax.axis_index("seq") * frames + jnp.arange(frames)
    valid_rows = (positions < length).astype(f32)[:, None]
    masked_float = (token_mask[0] > 0).astype(f32)[:, None]

    vectors = (
        mask_vector,
        gain_first,
        gain_attend,
        gain_conv,
        gain_second,
        gain_final,
        batch_scale,
        batch_shift,
    )
    own_small = jnp.concatenate([jnp.stack(vectors, axis=0), conv_taps.T], axis=0)
    count = own_small.shape[0]
    shards = lax.axis_size("dp") * lax.axis_size("seq")
    own_rows = model_width // shards
    small = gather_small(own_small[None])
    if in_steps(model_width):
        front = gather_packed(pack((first_up, first_down), "pack_first"))
        middle_part = pack((joint_proj, attend_out, conv_pair, conv_out), "pack_middle")
        back_part = pack((second_up, second_down), "pack_second")
        small, _, middle_part, back_part = tie(small, front, middle_part, back_part)
        middle = gather_packed(middle_part)
        up_one = down_one = Packed(front)
        squares = [packed_block(middle, i * own_rows, own_rows) for i in range(7)]
        joint_all, outward_all = squares[:3], squares[3]
        pair_all, conv_out_all = squares[4:6], squares[6]
    else:
        up_one, down_one, joint_all, outward_all, pair_all, conv_out_all = (
            fetch_weight(part)
            for part in (
                first_up,
                first_down,
                joint_proj,
                attend_out,
                conv_pair,
                conv_out,
            )
        )
        joint_all = jnp.split(joint_all, 3, axis=1)
        pair_all = jnp.split(pair_all, 2, axis=1)
    small = jnp.transpose(small, (1, 0, 2)).reshape(count, model_width).astype(f32)
    vector_mask, g_first, g_attend, g_conv, g_second, g_final, scale_float, shift_float = (
        small[i] for i in range(8)
    )
    taps_float = small[8:].T

    start_rows = jnp.where(masked_float > 0.0, vector_mask[None, :], inputs[0].astype(f32))
    rows_first, first_stored = ffn_forward(start_rows, g_first, up_one, down_one, "first")
    second_weights = []

    def gathered(rows):
        if not in_steps(model_width):
            second_weights.extend([fetch_weight(second_up), fetch_weight(second_down)])
            return rows
        rows, _, part = tie(rows, middle, back_part)
        back = Packed(gather_packed(part))
        second_weights.extend([back, back])
        return rows

    rows_second, attend_stored = attention_forward(
        rows_first, length, g_attend, joint_all, outward_all, gathered
    )
    up_two, down_two = second_weights
    rows_third, conv_stored, batch_stats = conv_forward(
        rows_second, valid_rows, g_conv, pair_all, taps_float, scale_float, shift_float, conv_out_all
    )
    rows_fourth, second_stored = ffn_forward(rows_third, g_second, up_two, down_two, "second")
    normed, normal, inverse = norm_forward(rows_fourth, g_final)
    output = (normed * valid_rows).astype(bf16)

    steps = in_steps(model_width)
    frame_count = batch_stats[2]
    if not steps:
        grad_rows, grad_final = norm_backward(
            cotangent[0].astype(f32) * valid_rows, g_final, normal, inverse
        )
        branch_two = (0.5 * grad_rows).astype(bf16)
        hidden_two = ffn_hidden_grad(branch_two, down_two, second_stored, "second")
        jobs_two = ffn_jobs(branch_two, hidden_two, second_stored)
        grad_rows, grad_gain_two = ffn_input_grad(
            grad_rows, hidden_two, g_second, up_two, second_stored, "second"
        )
        branch_conv, grad_shaped, sums = conv_shaped_grad(
            grad_rows, valid_rows, conv_out_all, conv_stored
        )
        totals = sum_small(sums)
        grad_paired, grad_taps = conv_paired_grad(
            grad_shaped, totals, valid_rows, taps_float, scale_float, frame_count, conv_stored
        )
        jobs_conv = conv_jobs(branch_conv, grad_paired, conv_stored)
        grad_rows, grad_gain_conv = conv_input_grad(
            grad_rows, grad_paired, g_conv, pair_all, conv_stored
        )
        branch_attend, grad_query, grad_key, grad_value = attention_parts_grad(
            grad_rows, outward_all, attend_stored
        )
        jobs_attend = attention_jobs(
            branch_attend, grad_query, grad_key, grad_value, attend_stored
        )
        blocks = attention_blocks_grad(grad_key, grad_value, joint_all, frames)
        grad_normed = sum_parts(scatter_line(blocks))
        grad_rows, grad_gain_attend = attention_input_grad(
            grad_rows, grad_normed, grad_query, g_attend, joint_all, attend_stored
        )
        branch_one = (0.5 * grad_rows).astype(bf16)
        hidden_one = ffn_hidden_grad(branch_one, down_one, first_stored, "first")
        jobs_one = ffn_jobs(branch_one, hidden_one, first_stored)
        grad_rows, grad_gain_one = ffn_input_grad(
            grad_rows, hidden_one, g_first, up_one, first_stored, "first"
        )
    else:
        gain = lambda vector: vector[None]
        own_valid = jnp.clip(length - lax.axis_index("seq") * frames, 0, frames)
        own_valid = own_valid[None].astype(jnp.int32)
        grad_rows, grad_final, branch_two = step_call(
            final_back_kernel,
            "final_back",
            [own_valid],
            [cotangent[0], rows_fourth, gain(g_final)],
            input_outs(rows_fourth),
        )
        hidden_two = ffn_hidden_grad(branch_two, down_two, second_stored, "second")
        two = ModuleScatter(ffn_jobs(branch_two, hidden_two, second_stored), "second_terms")
        two.share()
        two.first_send()
        grad_rows, grad_gain_two, branch_conv = ffn_up_back_input(
            hidden_two, rows_third, gain(g_second), grad_rows, up_two, 1.0, "second_up_back"
        )
        depth, inverse_std = conv_stored[10], conv_stored[7]
        spread = jnp.broadcast_to(frame_count, (model_width,))
        vectors = jnp.stack([batch_stats[0], inverse_std, scale_float, shift_float, spread])
        grad_shaped, sums = step_call(
            shaped_back_kernel,
            "shaped_back",
            [own_valid],
            [branch_conv, depth, vectors, Block(middle, 6)],
            [rows_like(depth), vector_like(depth, 2)],
        )
        beside = swap(sums, "dp", 1)
        (beside,) = fence([two], beside)
        totals = sum_at_once(sums + beside, "dp", (2, 4, 6))
        (totals,) = fence([two], totals)
        two.first_swap()
        totals = sum_at_once(totals, "seq", (1, 2, 3))
        rim = jax.ShapeDtypeStruct((taps // 2, model_width), bf16)
        grad_depth, top, bottom = step_call(
            depth_back_kernel,
            "depth_back",
            [own_valid],
            [grad_shaped, depth, vectors, totals],
            [rows_like(depth, bf16), rim, rim],
        )
        seq_size = lax.axis_size("seq")
        before = lax.ppermute(bottom, "seq", [(i, i + 1) for i in range(seq_size - 1)])
        after = lax.ppermute(top, "seq", [(i + 1, i) for i in range(seq_size - 1)])
        paired, sigmoid_rows, widened = conv_stored[3:6]
        tall = pltpu.VMEM((frames + 32, model_width), f32)
        paired_left, paired_right = step_call(
            taps_back_kernel,
            "taps_back",
            [own_valid],
            [before, grad_depth, after, taps_float.T, paired, sigmoid_rows],
            [rows_like(depth, bf16), rows_like(depth, bf16)],
            [tall],
        )
        (grad_taps,) = step_call(
            taps_sums_kernel,
            "taps_sums",
            [],
            [grad_depth, widened],
            [vector_like(depth, taps)],
            [tall, pltpu.VMEM(depth.shape, f32)],
        )
        conv = ModuleScatter(
            conv_jobs(branch_conv, (paired_left, paired_right), conv_stored), "conv_terms"
        )
        conv.share()
        conv.first_send()
        grad_rows, grad_gain_conv, branch_attend = step_call(
            conv_input_kernel,
            "conv_input_back",
            [],
            [
                paired_left,
                paired_right,
                rows_second,
                gain(g_conv),
                grad_rows,
                Block(middle, 4),
                Block(middle, 5),
            ],
            input_outs(rows_second),
        )
        grad_rows, branch_attend = fence([two, conv], grad_rows, branch_attend)
        two.second_send()
        grad_rows, branch_attend = fence([two, conv], grad_rows, branch_attend)
        two.second_swap()
        conv.first_swap()

        grad_query, grad_key, grad_value = attend_back(
            attend_stored[6], attend_stored[4], attend_stored[5], attend_stored[7], branch_attend, middle
        )
        attend_sum = ModuleScatter(
            attention_jobs(branch_attend, grad_query, grad_key, grad_value, attend_stored),
            "attend_terms",
        )
        blocks = blocks_back(grad_key, grad_value, middle, frames)
        attend_sum.share()

        def send_attend(up, down):
            attend_sum.first_send()
            return fence([attend_sum, conv], up, down)

        def fold_conv(up, down):
            attend_sum.first_swap()
            conv.second_send()
            return fence([conv], up, down)

        def send_two(up, down):
            conv.second_swap()
            two.z_send(1)
            return fence([two], up, down)

        parts = scatter_line(blocks, (send_attend, fold_conv, send_two))
        two.z_swap(1)
        grad_rows, grad_gain_attend, branch_one = step_call(
            attend_input_kernel,
            "attend_input_back",
            [],
            [*parts, grad_query, rows_first, gain(g_attend), grad_rows, Block(middle, 0)],
            input_outs(rows_first),
        )
        down_sum = ModuleScatter(ffn_jobs(branch_one, None, first_stored)[1:], "down_terms")
        down_sum.share()
        down_sum.first_send()
        branch_one, grad_rows = fence([attend_sum, down_sum], branch_one, grad_rows)
        down_sum.first_swap()
        hidden_one = ffn_hidden_grad(branch_one, down_one, first_stored, "first")
        hidden_one, grad_rows = fence([two, conv], hidden_one, grad_rows)
        two.z_send(2)
        two.z_swap(2)
        conv.z_send(1)
        conv.z_swap(1)
        up_sum = ModuleScatter(ffn_jobs(branch_one, hidden_one, first_stored)[:1], "up_terms")
        up_sum.share()
        attend_sum.second_send()
        up_sum.first_send()
        hidden_one, grad_rows = fence(
            [two, conv, down_sum, attend_sum, up_sum], hidden_one, grad_rows
        )
        attend_sum.second_swap()
        up_sum.first_swap()
        conv.z_send(2)
        conv.z_swap(2)
        down_sum.second_send()
        two_grads = two.finish()
        grad_rows, grad_gain_one, _ = ffn_up_back_input(
            hidden_one, start_rows, gain(g_first), grad_rows, up_one, 1.0, "first_up_back"
        )
        grad_final, grad_gain_two, grad_gain_conv, grad_gain_attend, grad_gain_one = (
            g[0]
            for g in (grad_final, grad_gain_two, grad_gain_conv, grad_gain_attend, grad_gain_one)
        )
    total_shift, total_scale = totals
    input_grad = grad_rows * (1.0 - masked_float)
    mask_grad = jnp.sum(grad_rows * masked_float, axis=0)

    sums = jnp.concatenate(
        [
            jnp.stack(
                [
                    mask_grad,
                    grad_gain_one,
                    grad_gain_attend,
                    grad_gain_conv,
                    grad_gain_two,
                    grad_final,
                ]
            ),
            grad_taps,
        ],
        axis=0,
    )
    sums = jnp.transpose(sums.reshape(-1, shards, own_rows), (1, 0, 2))
    if steps:
        few = SmallScatter(sums)
        (two_grads,) = fence([conv, attend_sum, up_sum, down_sum, few], two_grads)
        down_sum.second_swap()
        attend_sum.z_send(1)
        attend_sum.z_swap(1)
        few.step()
        up_sum.second_send()
        up_sum.second_swap()
        attend_sum.z_send(2)
        attend_sum.z_swap(2)
        conv_grads = conv.finish()
        (conv_grads,) = fence([down_sum, attend_sum, up_sum, few], conv_grads)
        down_sum.z_send(1)
        down_sum.z_swap(1)
        up_sum.z_send(1)
        up_sum.z_swap(1)
        few.step()
        fence([down_sum, up_sum, attend_sum, few])
        down_sum.z_send(2)
        down_sum.z_swap(2)
        up_sum.z_send(2)
        up_sum.z_swap(2)
        few.step()
        few.step()
        few.step()
        few.step()
        sums = few.keep[0]
        grad_up_two, grad_down_two = two_grads
        grad_pair, grad_conv_out = conv_grads
        attend_grads = attend_sum.finish()
        (grad_up_one,) = up_sum.finish()
        (grad_down_one,) = down_sum.finish()
    else:
        sums = scatter_small(sums)[0]
        grad_up_two, grad_down_two = scatter_module(jobs_two)
        grad_pair, grad_conv_out = scatter_module(jobs_conv)
        attend_grads = scatter_module(jobs_attend)
        grad_up_one, grad_down_one = scatter_module(jobs_one)
    grad_joint = jnp.concatenate(list(attend_grads[:2]), axis=1)
    grad_attend_out = attend_grads[2]
    own_start = (lax.axis_index("dp") * lax.axis_size("seq") + lax.axis_index("seq")) * own_rows
    scale_grad = lax.dynamic_slice_in_dim(total_scale, own_start, own_rows)
    shift_grad = lax.dynamic_slice_in_dim(total_shift, own_start, own_rows)
    batch_mean, batch_var, _ = batch_stats
    moment_var = batch_var * frame_count / (frame_count - 1.0)
    return (
        output[None],
        input_grad[None],
        sums[0],
        sums[1],
        grad_up_one,
        grad_down_one,
        sums[2],
        grad_joint,
        grad_attend_out,
        sums[3],
        grad_pair,
        sums[6 : 6 + taps].T,
        scale_grad,
        shift_grad,
        grad_conv_out,
        sums[4],
        grad_up_two,
        grad_down_two,
        sums[5],
        batch_mean,
        moment_var,
    )


def solution(mesh):
    both = P(("dp", "seq"))
    rows = P(("dp", "seq"), None)
    frames = P("dp", "seq", None)
    in_specs = (
        frames,
        P("dp"),
        P("dp", "seq"),
        both,
        both,
        rows,
        rows,
        both,
        rows,
        rows,
        both,
        rows,
        rows,
        both,
        both,
        rows,
        both,
        rows,
        rows,
        both,
        frames,
    )
    out_specs = (
        frames,
        frames,
        both,
        both,
        rows,
        rows,
        both,
        rows,
        rows,
        both,
        rows,
        rows,
        both,
        both,
        rows,
        both,
        rows,
        rows,
        both,
        P(),
        P(),
    )
    return jax.shard_map(
        per_device, mesh=mesh, in_specs=in_specs, out_specs=out_specs, check_vma=False
    )
```
